32 devices in a mesh: rows: 8 (over z, x), heads: 4 (over y, core).
Axes of the slice: x: 2, y: 2, z: 4, core: 2. Of those that a mesh axis runs over, the one named last changes fastest.
Arguments:
- patches: float32 [16384, 48], P(('rows', 'heads')), may hold values from -6 to 6
- segments: int32 [16384], P('rows'), may hold values from 0 to 3, as said below
- labels: int32 [64, 4], P(('rows', 'heads')), may hold values from 0 to 999
- w_in: bfloat16 [48, 768], replicated, may hold values from -0.875 to 0.875
- b_in: float32 [768], replicated, may hold values from -3 to 3
- pos_table: bfloat16 [256, 768], replicated, may hold values from -3 to 3
- cls_table: bfloat16 [1000, 768], replicated, may hold values from -3 to 3
- ln1_gain: float32 [1, 768], replicated, may hold values from 0.1 to 1.9
- ln1_bias: float32 [1, 768], replicated, may hold values from -2 to 2
- w_query: bfloat16 [1, 768, 768], P(None, None, 'heads'), may hold values from -0.21875 to 0.21875
- w_key: bfloat16 [1, 768, 768], P(None, None, 'heads'), may hold values from -0.21875 to 0.21875
- w_value: bfloat16 [1, 768, 768], P(None, None, 'heads'), may hold values from -0.21875 to 0.21875
- w_attn_out: bfloat16 [1, 768, 768], P(None, 'heads'), may hold values from -1.25 to 1.25
- ln2_gain: float32 [1, 768], replicated, may hold values from 0.1 to 1.9
- ln2_bias: float32 [1, 768], replicated, may hold values from -2 to 2
- w_up: bfloat16 [1, 768, 3072], P(None, None, 'heads'), may hold values from -0.21875 to 0.21875
- b_up: bfloat16 [1, 3072], P(None, 'heads'), may hold values from -3 to 3
- w_down: bfloat16 [1, 3072, 768], P(None, 'heads'), may hold values from -0.109375 to 0.109375
- b_down: float32 [1, 768], replicated, may hold values from -3 to 3
- w_out: bfloat16 [768, 96], replicated, may hold values from -0.02734375 to 0.02734375
- b_out: float32 [96], replicated, may hold values from -2 to 2
- latent_grad: float32 [16384, 48], P(('rows', 'heads')), may hold values from -6 to 6
- logdet_grad: float32 [16384], P(('rows', 'heads')), may hold values from -6 to 6
Outputs:
- latents: float32 [16384, 48], P(('rows', 'heads'))
- logdet: float32 [16384], P(('rows', 'heads'))
- patches_grad: float32 [16384, 48], P(('rows', 'heads'))
- scale_mean: float32 [64], P(('rows', 'heads'))
- scale_max: float32 [64], P(('rows', 'heads'))
- w_in_grad: float32 [48, 768], replicated
- b_in_grad: float32 [768], replicated
- pos_table_grad: float32 [256, 768], replicated
- cls_table_grad: float32 [1000, 768], replicated
- ln1_gain_grad: float32 [1, 768], replicated
- ln1_bias_grad: float32 [1, 768], replicated
- w_query_grad: float32 [1, 768, 768], P(None, None, 'heads')
- w_key_grad: float32 [1, 768, 768], P(None, None, 'heads')
- w_value_grad: float32 [1, 768, 768], P(None, None, 'heads')
- w_attn_out_grad: float32 [1, 768, 768], P(None, 'heads')
- ln2_gain_grad: float32 [1, 768], replicated
- ln2_bias_grad: float32 [1, 768], replicated
- w_up_grad: float32 [1, 768, 3072], P(None, None, 'heads')
- b_up_grad: float32 [1, 3072], P(None, 'heads')
- w_down_grad: float32 [1, 3072, 768], P(None, 'heads')
- b_down_grad: float32 [1, 768], replicated
- w_out_grad: float32 [768, 96], replicated
- b_out_grad: float32 [96], replicated
The draws below stay inside these ranges and needn't reach their ends.
Inputs may be any that keep to these rules, and one draw needn't show every extreme that they name: Each row of 256 patches is either one segment numbered 0, or 4 segments of 64 patches numbered 0 to 3 in order; the first row is of the second kind.
All inputs are finite; a program needn't handle non-finite values.
Results may differ from the reference program's by a relative error of at most 0.034.
Values may be sent and summed in bfloat16 or wider, within the bound.
No kernel may reach another device: no remote copies, remote signals or barrier semaphores. Data moves between devices by JAX's collectives and lax.ppermute only.
A program may use at most 128 MiB of HBM per device.

```python
import jax
import jax.numpy as jnp
from jax import lax

D = 768
HEADS = 12
HEAD_DIM = 64
FF = 3072
CH = 48
CLASSES = 1000
SEQ = 256
SLOTS = 4
LAYERS = 1
ROWS_DEV = 8
ROWS = 64
TOKENS = 16384


def draw_segments(key, part):
    packed = jax.random.randint(key, (ROWS,), 0, 4) == 0
    packed = packed.at[0].set(True)
    places = jnp.arange(SEQ, dtype=jnp.int32)
    numbers = jnp.where(packed[:, None], places[None, :] // (SEQ // SLOTS), 0)
    return numbers.reshape(-1).astype(jnp.int32)


def place_ends(result, own_key, smallest, top_value):
    dims = result.shape
    index_at = [jax.random.randint(jax.random.fold_in(own_key, axis), (), 0, dims[axis]) for axis in range(len(dims))]
    result = result.at[tuple(index_at)].set(smallest)
    longest = dims.index(max(dims))
    index_at[longest] = (index_at[longest] + 1) % dims[longest]
    return result.at[tuple(index_at)].set(top_value)


def shard_levels(own_key, dims, cuts, low, top_value):
    factor_of = 1.0
    for dim, parts in cuts:
        draws = jax.random.uniform(jax.random.fold_in(jax.random.fold_in(own_key, 6), dim), (parts,), jnp.float32, low / len(cuts), top_value / len(cuts))
        factor_of = factor_of * jnp.repeat(jnp.exp(draws), dims[dim] // parts).reshape((-1,) + (1,) * (len(dims) - 1 - dim))
    return factor_of


def gaussian(key, dims, scale, bound, cuts=(), kind=jnp.bfloat16):
    result = scale * jax.random.normal(key, dims, jnp.float32)
    if cuts:
        result = result * shard_levels(key, dims, cuts, -0.22, 0.18)
    return jnp.clip(result, -bound, bound).astype(kind)


def setup_inputs(seed: int = 0) -> dict:
    seeds = jax.random.split(jax.random.key(seed), 24)
    return {
        "patches": gaussian(seeds[0], (TOKENS, CH), 1.0, 6.0, ((0, 32),), jnp.float32),
        "segments": draw_segments(jax.random.fold_in(seeds[23], 71), 0),
        "labels": place_ends(jax.random.randint(seeds[2], (ROWS, SLOTS), 0, CLASSES), jax.random.fold_in(seeds[2], 1), 0, CLASSES - 1).astype(jnp.int32),
        "w_in": gaussian(seeds[3], (CH, D), CH ** -0.5, 0.875),
        "b_in": gaussian(seeds[4], (D,), 0.5, 3.0, (), jnp.float32),
        "pos_table": gaussian(seeds[5], (SEQ, D), 0.5, 3.0),
        "cls_table": gaussian(seeds[6], (CLASSES, D), 0.5, 3.0),
        "ln1_gain": jnp.clip(1.0 + 0.18 * jax.random.normal(seeds[7], (LAYERS, D), jnp.float32), 0.1, 1.9),
        "ln1_bias": gaussian(seeds[8], (LAYERS, D), 0.3, 2.0, (), jnp.float32),
        "w_query": gaussian(seeds[9], (LAYERS, D, D), D ** -0.5, 0.21875, ((2, 4),)),
        "w_key": gaussian(seeds[10], (LAYERS, D, D), D ** -0.5, 0.21875, ((2, 4),)),
        "w_value": gaussian(seeds[11], (LAYERS, D, D), D ** -0.5, 0.21875, ((2, 4),)),
        "w_attn_out": gaussian(seeds[12], (LAYERS, D, D), (D // 32) ** -0.5, 1.25, ((1, 4),)),
        "ln2_gain": jnp.clip(1.0 + 0.18 * jax.random.normal(seeds[13], (LAYERS, D), jnp.float32), 0.1, 1.9),
        "ln2_bias": gaussian(seeds[14], (LAYERS, D), 0.3, 2.0, (), jnp.float32),
        "w_up": gaussian(seeds[15], (LAYERS, D, FF), D ** -0.5, 0.21875, ((2, 4),)),
        "b_up": gaussian(seeds[16], (LAYERS, FF), 0.5, 3.0, ((1, 4),)),
        "w_down": gaussian(seeds[17], (LAYERS, FF, D), FF ** -0.5, 0.109375, ((1, 4),)),
        "b_down": gaussian(seeds[18], (LAYERS, D), 0.5, 3.0, (), jnp.float32),
        "w_out": gaussian(seeds[19], (D, 2 * CH), (D * 64) ** -0.5, 0.02734375),
        "b_out": gaussian(seeds[20], (2 * CH,), 0.3, 2.0, (), jnp.float32),
        "latent_grad": gaussian(seeds[21], (TOKENS, CH), 1.0, 6.0, ((0, 32),), jnp.float32),
        "logdet_grad": gaussian(seeds[22], (TOKENS,), 1.0, 6.0, ((0, 32),), jnp.float32),
    }


@jax.custom_vjp
def low(v):
    return lax.optimization_barrier(v.astype(jnp.bfloat16)).astype(jnp.float32)

@jax.custom_vjp
def low_back(v):
    return v

def low_keep(v):
    return (low(v), None)

def low_pass(kept, grad):
    return (grad,)

def back_keep(v):
    return (v, None)

def back_low(kept, grad):
    return (low(grad),)
low.defvjp(low_keep, low_pass)
low_back.defvjp(back_keep, back_low)
PRECISE = lax.Precision.HIGHEST

def product(matrix, other):
    return jnp.matmul(matrix, other, precision=PRECISE)

def layer_norm(values, gains, offset):
    average = lax.optimization_barrier(jnp.mean(values, -1, keepdims=True))
    centered = values - average
    spread = lax.optimization_barrier(jnp.mean(centered * centered, -1, keepdims=True))
    return centered * lax.rsqrt(spread + 1e-05) * gains + offset

def forward(params, patch_rows, seg_rows, label_rows):
    w_in, b_in, pos_table, cls_table, ln1_gain, ln1_bias, w_query, w_key, w_value, w_attn_out, ln2_gain, ln2_bias, w_up, b_up, w_down, b_down, w_out, b_out = params
    group_rows = patch_rows.shape[0]
    causal = lax.broadcasted_iota(jnp.int32, (SEQ, SEQ), 0) >= lax.broadcasted_iota(jnp.int32, (SEQ, SEQ), 1)
    allowed = (seg_rows[:, :, None] == seg_rows[:, None, :]) & causal[None]
    position = lax.optimization_barrier(jnp.sum(allowed.astype(jnp.int32), -1)) - 1
    token_label = jnp.take_along_axis(label_rows, seg_rows, axis=1)
    hidden = low_back(product(low(patch_rows), w_in) + b_in) + pos_table[position] + cls_table[token_label]
    factor = HEAD_DIM ** (-0.5)
    for depth in range(LAYERS):
        normed = low(layer_norm(hidden, ln1_gain[depth], ln1_bias[depth]))

        def project(weight):
            return low(low_back(product(normed, weight))).reshape(group_rows, SEQ, HEADS, HEAD_DIM)
        queries = project(w_query[depth])
        key_rows = project(w_key[depth])
        values = project(w_value[depth])
        scores = low_back(jnp.einsum('gqhe,gkhe->ghqk', queries, key_rows, precision=PRECISE)) * factor
        scores = jnp.where(allowed[:, None], scores, -1e+30)
        probs = low(jax.nn.softmax(scores, -1))
        attended = jnp.einsum('ghqk,gkhe->gqhe', probs, values, precision=PRECISE)
        attended = low(low_back(attended)).reshape(group_rows, SEQ, D)
        hidden = hidden + low_back(product(attended, w_attn_out[depth]))
        normed = low(layer_norm(hidden, ln2_gain[depth], ln2_bias[depth]))
        pre_act = low_back(product(normed, w_up[depth]) + b_up[depth])
        activated = low(jax.nn.gelu(pre_act, approximate=False))
        hidden = hidden + low_back(product(activated, w_down[depth])) + b_down[depth]
    head_out = low_back(product(low(hidden), w_out) + b_out)
    previous = jnp.concatenate([jnp.zeros_like(head_out[:, :1]), head_out[:, :-1]], 1)
    carried = jnp.concatenate([jnp.zeros_like(seg_rows[:, :1]), (seg_rows[:, 1:] == seg_rows[:, :-1]).astype(jnp.int32)], 1)
    previous = jnp.where(carried[..., None] > 0, previous, 0.0)
    shifts = previous[..., :CH]
    logscale = previous[..., CH:]
    latent_rows = (patch_rows - shifts) * jnp.exp(-logscale)
    logdet_rows = -lax.optimization_barrier(jnp.sum(logscale, -1))
    return ((latent_rows, logdet_rows), (lax.optimization_barrier(jnp.mean(logscale, axis=(1, 2))), lax.optimization_barrier(jnp.max(logscale, axis=(1, 2)))))

def reference(patches, segments, labels, w_in, b_in, pos_table, cls_table, ln1_gain, ln1_bias, w_query, w_key, w_value, w_attn_out, ln2_gain, ln2_bias, w_up, b_up, w_down, b_down, w_out, b_out, latent_grad, logdet_grad):
    params = tuple((weight.astype(jnp.float32) for weight in (w_in, b_in, pos_table, cls_table, ln1_gain, ln1_bias, w_query, w_key, w_value, w_attn_out, ln2_gain, ln2_bias, w_up, b_up, w_down, b_down, w_out, b_out)))
    groups = ROWS // ROWS_DEV

    def regroup(array):
        return array.reshape((groups, ROWS_DEV, SEQ) + array.shape[1:])
    pieces = (regroup(patches.astype(jnp.float32)), regroup(segments), labels.reshape(groups, ROWS_DEV, SLOTS), regroup(latent_grad.astype(jnp.float32)), regroup(logdet_grad.astype(jnp.float32)))

    def advance(totals, piece):
        patch_rows, seg_rows, label_rows, grad_latent, grad_logdet = piece

        def apply_flow(weights_in, patch_vals):
            return forward(weights_in, patch_vals, seg_rows, label_rows)
        results, pullback, row_stats = jax.vjp(apply_flow, params, patch_rows, has_aux=True)
        grad_params, grad_patch = pullback((grad_latent, grad_logdet))
        totals = jax.tree.map(jnp.add, totals, grad_params)
        return (totals, (results[0], results[1], grad_patch, row_stats[0], row_stats[1]))
    zero_grads = jax.tree.map(jnp.zeros_like, params)
    totals, (latent_rows, logdet_rows, grad_rows, scale_means, scale_maxes) = lax.scan(advance, zero_grads, pieces)
    g_w_in, g_b_in, g_pos, g_cls, g_ln1_gain, g_ln1_bias, g_query, g_key, g_value, g_attn_out, g_ln2_gain, g_ln2_bias, g_up, g_b_up, g_down, g_b_down, g_w_out, g_b_out = totals
    return (latent_rows.reshape(TOKENS, CH), logdet_rows.reshape(TOKENS), grad_rows.reshape(TOKENS, CH), scale_means.reshape(ROWS), scale_maxes.reshape(ROWS), g_w_in, g_b_in, g_pos, g_cls, g_ln1_gain, g_ln1_bias, g_query, g_key, g_value, g_attn_out, g_ln2_gain, g_ln2_bias, g_up, g_b_up, g_down, g_b_down, g_w_out, g_b_out)
```

```python
import jax
import jax.numpy as jnp
from jax import lax
from jax.sharding import PartitionSpec as P

HEAD_DIM = 64
EPSILON = 1e-05
BF = jnp.bfloat16
F32 = jnp.float32


def norm_parts(values):
    average = jnp.mean(values, -1, keepdims=True)
    centered = values - average
    spread = jnp.mean(centered * centered, -1, keepdims=True)
    rstd = lax.rsqrt(spread + EPSILON)
    return centered * rstd, rstd


def gelu_exact(values):
    return jax.nn.gelu(values, approximate=False)


def nn(matrix, other):
    return jnp.dot(matrix, other, preferred_element_type=F32)


def tn(matrix, other):
    return lax.dot_general(matrix, other, (((0,), (0,)), ((), ())), preferred_element_type=F32)


def nt(matrix, other):
    return lax.dot_general(matrix, other, (((1,), (1,)), ((), ())), preferred_element_type=F32)


def make_program(rows_size, heads_size):
    levels = rows_size.bit_length() - 1

    def swap_heads(array, bit):
        pairs = [(i, i ^ bit) for i in range(heads_size)]
        return lax.ppermute(array, "heads", pairs)

    def swap_rows(array, bit):
        pairs = [(i, i ^ bit) for i in range(rows_size)]
        return lax.ppermute(array, "rows", pairs)

    def gather_slots(own, row_bit):
        half = own.shape[0] // 2
        near = swap_heads(own, 1)
        mine = lax.dynamic_slice_in_dim(own, row_bit * half, half, 0)
        mine = swap_heads(mine, 2)
        other = swap_rows(mine, 1)
        low = jnp.where(row_bit == 0, mine, other)
        high = jnp.where(row_bit == 0, other, mine)
        far = jnp.concatenate([low, high], 0)
        return [own, near, far, swap_heads(far, 1)]

    def gather_all(array):
        for bit in (1, 2):
            array = jnp.concatenate([array, swap_heads(array, bit)], 0)
        for level in range(levels):
            array = jnp.concatenate([array, swap_rows(array, 1 << level)], 0)
        return array

    def relative(array, row_index):
        pieces = array.reshape((2,) * levels + (array.shape[0] // rows_size,) + array.shape[1:])
        for level in range(levels):
            bit = (row_index >> level) & 1
            pieces = jnp.where(bit == 1, jnp.flip(pieces, level), pieces)
        return pieces

    def add_low(first, second):
        return (first.astype(F32) + second.astype(F32)).astype(BF)

    def reduce_slots(slots, row_index):
        shape = slots[0].shape
        zero = add_low(slots[0], swap_heads(slots[1], 1))
        two = add_low(slots[2], swap_heads(slots[3], 1))
        total = add_low(zero, swap_heads(two, 2))
        total = relative(total, row_index)
        for level in range(levels):
            total = add_low(total[0], swap_rows(total[1], 1 << level))
        for level in reversed(range(levels)):
            total = jnp.stack([total, swap_rows(total, 1 << level)], 0)
        return relative(total.reshape(shape), row_index).reshape(shape).astype(F32)

    def program(
        patches,
        segments,
        labels,
        w_in,
        b_in,
        pos_table,
        cls_table,
        ln1_gain,
        ln1_bias,
        w_query,
        w_key,
        w_value,
        w_attn_out,
        ln2_gain,
        ln2_bias,
        w_up,
        b_up,
        w_down,
        b_down,
        w_out,
        b_out,
        latent_grad,
        logdet_grad,
    ):
        tokens = patches.shape[0]
        length, width = pos_table.shape
        slot_count = labels.shape[1]
        channels = patches.shape[1]
        classes = cls_table.shape[0]
        part = w_query.shape[2]
        heads_here = part // HEAD_DIM
        head_index = lax.axis_index("heads")
        row_index = lax.axis_index("rows")
        row_bit = row_index & 1

        pack_t = jnp.concatenate(
            [w_query[0], w_key[0], w_value[0], w_attn_out[0].T], 1
        )
        slots_t = gather_slots(pack_t, row_bit)
        slots_u = gather_slots(w_up[0], row_bit)
        slots_d = gather_slots(w_down[0], row_bit)
        bias_up = [b_up, swap_heads(b_up, 1), swap_heads(b_up, 2), swap_heads(b_up, 3)]
        bias_up = [bias.astype(F32) for bias in bias_up]
        all_labels = gather_all(labels)

        own_segs = lax.dynamic_slice_in_dim(segments, head_index * tokens, tokens)
        seg_rows = own_segs.reshape(-1, length)
        row_count = seg_rows.shape[0]
        causal = lax.broadcasted_iota(jnp.int32, (length, length), 0) >= lax.broadcasted_iota(
            jnp.int32, (length, length), 1
        )
        allowed = (seg_rows[:, :, None] == seg_rows[:, None, :]) & causal[None]
        position = (jnp.sum(allowed.astype(jnp.int32), -1) - 1).reshape(-1)
        slot_ids = lax.broadcasted_iota(jnp.int32, (1, 1, slot_count), 2)
        token_label = jnp.sum(
            jnp.where(seg_rows[:, :, None] == slot_ids, labels[:, None, :], 0), -1
        ).reshape(-1)
        pos_onehot = (position[:, None] == lax.broadcasted_iota(jnp.int32, (1, length), 1)).astype(BF)
        cls_onehot = (
            token_label[:, None] == lax.broadcasted_iota(jnp.int32, (1, classes), 1)
        ).astype(BF)
        patch_low = patches.astype(BF)
        hidden0 = (
            nn(patch_low, w_in) + b_in + nn(pos_onehot, pos_table) + nn(cls_onehot, cls_table)
        )

        xhat1, rstd1 = norm_parts(hidden0)
        normed1 = (xhat1 * ln1_gain[0] + ln1_bias[0]).astype(BF)

        def per_row(matrix):
            return matrix.reshape(row_count, length, -1, HEAD_DIM)

        weight_t = jnp.concatenate(slots_t, 1).reshape(width, heads_size, 4, part)
        weight_qkv = [weight_t[:, :, i].reshape(width, heads_size * part) for i in range(4)]
        queries = per_row(nn(normed1, weight_qkv[0]).astype(BF))
        keys = per_row(nn(normed1, weight_qkv[1]).astype(BF))
        values = per_row(nn(normed1, weight_qkv[2]).astype(BF))
        scores = jnp.einsum("bqhe,bkhe->bhqk", queries, keys, preferred_element_type=F32)
        scores = jnp.where(allowed[:, None], scores * HEAD_DIM ** (-0.5), -1e30)
        probs = jax.nn.softmax(scores, -1)
        probs_low = probs.astype(BF)
        attended = jnp.einsum("bhqk,bkhe->bqhe", probs_low, values, preferred_element_type=F32)
        attended = attended.astype(BF).reshape(tokens, width)
        hidden1 = hidden0 + nt(attended, weight_qkv[3])
        xhat2, rstd2 = norm_parts(hidden1)
        normed2 = (xhat2 * ln2_gain[0] + ln2_bias[0]).astype(BF)

        slot_order = [head_index ^ j for j in range(heads_size)]
        pre_act = [nn(normed2, slots_u[j]) + bias_up[j] for j in range(heads_size)]
        activated = [gelu_exact(p).astype(BF) for p in pre_act]
        branch = sum(nn(activated[j], slots_d[j]) for j in range(heads_size))
        hidden2 = hidden1 + branch + b_down[0]
        top_low = hidden2.astype(BF)
        head_out = nn(top_low, w_out) + b_out
        carried = jnp.concatenate(
            [jnp.zeros((row_count, 1), dtype=bool), seg_rows[:, 1:] == seg_rows[:, :-1]], 1
        ).reshape(-1, 1)
        previous = jnp.concatenate([jnp.zeros_like(head_out[:1]), head_out[:-1]], 0)
        previous = jnp.where(carried, previous, 0.0)
        shifts = previous[:, :channels]
        logscale = previous[:, channels:]
        shrink = jnp.exp(-logscale)
        latents = (patches - shifts) * shrink
        logdet = -jnp.sum(logscale, -1)
        scale_rows = logscale.reshape(row_count, -1)
        scale_mean = jnp.mean(scale_rows, -1)
        scale_max = jnp.max(scale_rows, -1)

        grad_direct = latent_grad * shrink
        grad_prev = jnp.concatenate(
            [-grad_direct, -latent_grad * latents - logdet_grad[:, None]], 1
        )
        grad_prev = jnp.where(carried, grad_prev, 0.0)
        grad_head = jnp.concatenate([grad_prev[1:], jnp.zeros_like(grad_prev[:1])], 0).astype(BF)
        grad_w_out = tn(grad_head, top_low)
        grad_b_out = jnp.sum(grad_head.astype(F32), 0)
        grad_hidden2 = nt(grad_head, w_out)
        grad_b_down = jnp.sum(grad_hidden2, 0)
        grad_branch = grad_hidden2.astype(BF)

        grads_d = [tn(activated[j], grad_branch).astype(BF) for j in range(heads_size)]
        sum_down = reduce_slots(grads_d, row_index)
        grad_pre = []
        for j in range(heads_size):
            grad_act = nt(grad_branch, slots_d[j])
            _, pull = jax.vjp(gelu_exact, pre_act[j])
            grad_pre.append(pull(grad_act)[0].astype(BF))
        grads_u = [tn(normed2, grad_pre[j]).astype(BF) for j in range(heads_size)]
        sum_up = reduce_slots(grads_u, row_index)
        grad_b_up = [jnp.sum(g.astype(F32), 0) for g in grad_pre]
        grad_normed2 = sum(nt(grad_pre[j], slots_u[j]) for j in range(heads_size))

        def norm_back(grad, gain, xhat, rstd):
            d = grad * gain
            back = rstd * (
                d - jnp.mean(d, -1, keepdims=True) - xhat * jnp.mean(d * xhat, -1, keepdims=True)
            )
            return back, jnp.sum(grad * xhat, 0), jnp.sum(grad, 0)

        back1, grad_gain2, grad_bias2 = norm_back(grad_normed2, ln2_gain[0], xhat2, rstd2)
        grad_hidden1 = grad_hidden2 + back1
        grad_mix = grad_hidden1.astype(BF)
        grad_attended = per_row(nn(grad_mix, weight_qkv[3]).astype(BF))
        grad_probs = jnp.einsum("bqhe,bkhe->bhqk", grad_attended, values, preferred_element_type=F32)
        inner = jnp.sum(probs * grad_probs, -1, keepdims=True)
        grad_scores = (probs * (grad_probs - inner) * HEAD_DIM ** (-0.5)).astype(BF)
        grad_query = jnp.einsum("bhqk,bkhe->bqhe", grad_scores, keys, preferred_element_type=F32)
        grad_key = jnp.einsum("bhqk,bqhe->bkhe", grad_scores, queries, preferred_element_type=F32)
        grad_value = jnp.einsum(
            "bhqk,bqhe->bkhe", probs_low, grad_attended, preferred_element_type=F32
        )
        grad_query, grad_key, grad_value = (
            g.astype(BF).reshape(tokens, width) for g in (grad_query, grad_key, grad_value)
        )
        grad_normed1 = (
            nt(grad_query, weight_qkv[0])
            + nt(grad_key, weight_qkv[1])
            + nt(grad_value, weight_qkv[2])
        )
        back0, grad_gain1, grad_bias1 = norm_back(grad_normed1, ln1_gain[0], xhat1, rstd1)
        grad_hidden0 = grad_hidden1 + back0
        grad_embed = grad_hidden0.astype(BF)
        grad_w_in = tn(patch_low, grad_embed)
        grad_b_in = jnp.sum(grad_embed.astype(F32), 0)
        patches_grad = grad_direct + nt(grad_embed, w_in)

        quarter = length // slot_count
        packed_row = seg_rows[:, -1] > 0
        grad_slots = grad_hidden0.reshape(row_count, slot_count, quarter, width)
        single_part = jnp.sum(
            jnp.where(
                packed_row[:, None, None], 0.0, grad_hidden0.reshape(row_count, length, width)
            ),
            0,
        )
        packed_part = jnp.sum(jnp.where(packed_row[:, None, None, None], grad_slots, 0.0), (0, 1))
        grad_pos = single_part + jnp.concatenate(
            [packed_part, jnp.zeros((length - quarter, width), F32)], 0
        )
        slot_sums = jnp.sum(grad_slots, 2)
        row_total = jnp.sum(slot_sums, 1)
        first_slot = lax.broadcasted_iota(jnp.int32, (1, slot_count, 1), 1) == 0
        slot_vectors = jnp.where(
            packed_row[:, None, None], slot_sums, jnp.where(first_slot, row_total[:, None, :], 0.0)
        )
        all_slots = gather_all(slot_vectors.reshape(-1, width).astype(BF))
        label_onehot = (
            lax.broadcasted_iota(jnp.int32, (classes, 1), 0) == all_labels.reshape(1, -1)
        ).astype(BF)
        sum_cls = nn(label_onehot, all_slots)

        small = jnp.concatenate(
            [
                grad_w_in,
                grad_w_out,
                grad_pos,
                jnp.stack(
                    [
                        grad_b_in,
                        grad_gain1,
                        grad_bias1,
                        grad_gain2,
                        grad_bias2,
                        grad_b_down,
                        jnp.pad(grad_b_out, (0, width - 2 * channels)),
                    ]
                ),
            ],
            0,
        ).astype(BF)
        block = -(-small.shape[0] // (16 * heads_size)) * 16
        small = jnp.pad(small, ((0, block * heads_size - small.shape[0]), (0, 0)))
        small = small.reshape(heads_size, block, width)
        grads_t = []
        for j in range(heads_size):
            columns = slice(j * part, (j + 1) * part)
            grads_t.append(
                jnp.concatenate(
                    [
                        jnp.concatenate(
                            [
                                tn(normed1, grad_query[:, columns]),
                                tn(normed1, grad_key[:, columns]),
                                tn(normed1, grad_value[:, columns]),
                                tn(grad_mix, attended[:, columns]),
                            ],
                            1,
                        ).astype(BF),
                        lax.dynamic_index_in_dim(small, slot_order[j], 0, keepdims=False),
                        jnp.pad(grad_b_up[j][None].astype(BF), ((0, 15), (0, 0))),
                    ],
                    0,
                )
            )
        sum_t = reduce_slots(grads_t, row_index)
        own_small = sum_t[width : width + block].astype(BF)
        pair = jnp.stack([own_small, swap_heads(own_small, 1)], 0)
        quad = jnp.concatenate([pair, swap_heads(pair, 2)], 0)
        ordered = jnp.stack(
            [lax.dynamic_index_in_dim(quad, slot_order[j], 0, keepdims=False) for j in range(heads_size)]
        )
        flat = ordered.reshape(-1, width).astype(F32)
        sizes = [channels, 2 * channels, length]
        sum_w_in = flat[: sizes[0]]
        sum_w_out = flat[sizes[0] : sizes[0] + sizes[1]].T
        start = sizes[0] + sizes[1]
        sum_pos = flat[start : start + length]
        start += length
        sum_b_in, sum_gain1, sum_bias1, sum_gain2, sum_bias2, sum_b_down = (
            flat[start + i] for i in range(6)
        )
        sum_b_out = flat[start + 6, : 2 * channels]
        sum_b_up = sum_t[width + block]
        return (
            latents,
            logdet,
            patches_grad,
            scale_mean,
            scale_max,
            sum_w_in,
            sum_b_in,
            sum_pos,
            sum_cls,
            sum_gain1[None],
            sum_bias1[None],
            sum_t[None, :width, :part],
            sum_t[None, :width, part : 2 * part],
            sum_t[None, :width, 2 * part : 3 * part],
            sum_t[:width, 3 * part :].T[None],
            sum_gain2[None],
            sum_bias2[None],
            sum_up[None],
            sum_b_up[None],
            sum_down[None],
            sum_b_down[None],
            sum_w_out,
            sum_b_out,
        )

    return program


def solution(mesh):
    tokens = P(("rows", "heads"))
    tokens2 = P(("rows", "heads"), None)
    last = P(None, None, "heads")
    middle = P(None, "heads", None)
    in_specs = (
        (tokens2, P("rows"), tokens2)
        + (P(),) * 6
        + (last, last, last, middle)
        + (P(), P(), last, P(None, "heads"), middle, P(), P(), P())
        + (tokens2, tokens)
    )
    out_specs = (
        (tokens2, tokens, tokens2, tokens, tokens)
        + (P(),) * 6
        + (last, last, last, middle)
        + (P(), P(), last, P(None, "heads"), middle, P(), P(), P())
    )
    program = make_program(mesh.shape["rows"], mesh.shape["heads"])
    return jax.shard_map(
        program, mesh=mesh, in_specs=in_specs, out_specs=out_specs, check_vma=False
    )
```

```python
import functools

import jax
import jax.numpy as jnp
from jax import lax
from jax.experimental import pallas as pl
from jax.experimental.pallas import tpu as pltpu
from jax.sharding import PartitionSpec as P

HEAD_DIM = 64
EPSILON = 1e-05
SCALE = HEAD_DIM**-0.5
BF = jnp.bfloat16
F32 = jnp.float32
PIECES = 4
EXTRA = 16
GROUP = 32
CHAIN_ORDERS = ("yxz", "zxy", "yzx", "xyz")
BEFORE_FAR = (0, 1)
BEFORE_NEAR = ()
BEFORE_EMBED = (0, 1, 2)
TAIL = (0, 3, 0, 2, 1, 3, 1, 0, 2, 3, 2, 1, 0, 3, 1, 2, 3, 2, 3)
CHUNK = 64

VMEM = pl.BlockSpec(memory_space=pltpu.VMEM)
SMEM = pl.BlockSpec(memory_space=pltpu.SMEM)
HBM = pl.BlockSpec(memory_space=pl.ANY)


def nn(matrix, other):
    return lax.dot_general(matrix, other, (((1,), (0,)), ((), ())), preferred_element_type=F32)


def tn(matrix, other):
    return lax.dot_general(matrix, other, (((0,), (0,)), ((), ())), preferred_element_type=F32)


def nt(matrix, other):
    return lax.dot_general(matrix, other, (((1,), (1,)), ((), ())), preferred_element_type=F32)


def norm_parts(values):
    average = jnp.mean(values, -1, keepdims=True)
    centered = values - average
    spread = jnp.mean(centered * centered, -1, keepdims=True)
    rstd = lax.rsqrt(spread + EPSILON)
    return centered * rstd, rstd


def norm_back(grad, gain, xhat, rstd):
    scaled = grad * gain
    back = scaled - jnp.mean(scaled, -1, keepdims=True)
    back = back - xhat * jnp.mean(scaled * xhat, -1, keepdims=True)
    return rstd * back


def column_sum(values):
    return jnp.sum(values, 0, keepdims=True)


def over_rows(tokens, body):
    def step(index, carry):
        body(pl.ds(pl.multiple_of(index * CHUNK, CHUNK), CHUNK))
        return carry

    lax.fori_loop(0, tokens // CHUNK, step, 0)


def gelu_pair(values):
    scaled = jnp.abs(values) * 0.7071067811865476
    t = 1.0 / (1.0 + 0.3275911 * scaled)
    bell = jnp.exp(-0.5 * values * values)
    poly = 1.061405429 * t - 1.453152027
    poly = poly * t + 1.421413741
    poly = poly * t - 0.284496736
    poly = poly * t + 0.254829592
    tail = 0.5 * poly * t * bell
    below = jnp.where(values >= 0.0, 1.0 - tail, tail)
    return values * below, below + values * bell * 0.3989422804014327


def packed_flag(where_ref, seg_ref, row, length):
    start = where_ref[0] + row * length
    return seg_ref[start + length - 1] > 0


def embed_kernel(
    where_ref, seg_ref, patch_ref, w_ref, b_ref, pos_ref, cls_ref, gain_ref, bias_ref, hid_ref, norm_ref
):
    tokens, width = hid_ref.shape
    length = pos_ref.shape[0]
    slots = cls_ref.shape[0] // (tokens // length)
    quarter = length // slots
    hid_ref[...] = tn(patch_ref[...].astype(BF), w_ref[...]) + b_ref[...]
    for row in range(tokens // length):
        packed = packed_flag(where_ref, seg_ref, row, length)
        for slot in range(slots):
            at = slice(row * length + slot * quarter, row * length + (slot + 1) * quarter)
            here = pos_ref[slot * quarter : (slot + 1) * quarter].astype(F32)
            first = pos_ref[:quarter].astype(F32)
            one = cls_ref[row * slots + slot : row * slots + slot + 1]
            start = cls_ref[row * slots : row * slots + 1]
            value = hid_ref[at] + jnp.where(packed, first, here) + jnp.where(packed, one, start)
            hid_ref[at] = value
            xhat, _ = norm_parts(value)
            norm_ref[at] = (xhat * gain_ref[...] + bias_ref[...]).astype(BF)


def fetch_near(parts, weight_ref, sems):
    unit = weight_ref.shape[1] // 2
    copies = []
    for slot, ref in enumerate(parts):
        for half in range(2):
            for u in range(2):
                source = ref.at[half, pl.ds(unit * u, unit)]
                copies.append((source, weight_ref.at[2 * half + u, pl.ds(unit * slot, unit)]))
    return start_copies(copies, sems)


def fetch_far(where_ref, parts, weight_ref, sems):
    far, far_other, cross, cross_other = parts
    unit = weight_ref.shape[1] // 2
    x = where_ref[1]
    copies = []
    for slot, ref, half in ((0, far, x), (0, far_other, 1 - x), (1, cross, x), (1, cross_other, 1 - x)):
        for u in range(2):
            source = ref.at[pl.ds(unit * u, unit)]
            copies.append((source, weight_ref.at[2 * half + u, pl.ds(unit * slot, unit)]))
    return start_copies(copies, sems)


def fetch_half(where_ref, parts, weight_ref, sems):
    if len(parts) == 2:
        return fetch_near(parts, weight_ref, sems)
    return fetch_far(where_ref, parts, weight_ref, sems)


def start_copies(copies, sems):
    made = [pltpu.make_async_copy(src, dst, sems.at[i]) for i, (src, dst) in enumerate(copies)]
    for copy in made:
        copy.start()
    return made


def fetch_full(where_ref, parts, weight_ref, sems):
    own, near, far, far_other, cross, cross_other = parts
    half = weight_ref.shape[1] // 2
    mine = pl.ds(pl.multiple_of(where_ref[1] * half, half), half)
    other = pl.ds(pl.multiple_of((1 - where_ref[1]) * half, half), half)
    copies = [
        (own, weight_ref.at[0]),
        (near, weight_ref.at[1]),
        (far, weight_ref.at[2, mine]),
        (far_other, weight_ref.at[2, other]),
        (cross, weight_ref.at[3, mine]),
        (cross_other, weight_ref.at[3, other]),
    ]
    return start_copies(copies, sems)


def allowed_mask(packed, quarter, first, rows, keys):
    q = lax.broadcasted_iota(jnp.int32, (rows, keys), 0) + first
    k = lax.broadcasted_iota(jnp.int32, (rows, keys), 1)
    shift = quarter.bit_length() - 1
    same = (q >> shift) == (k >> shift)
    return (k <= q) & (same | jnp.logical_not(packed))


def attend_kernel(where_ref, seg_ref, hid_ref, norm_ref, *rest, length, quarter, count):
    parts = rest[:count]
    q_ref, k_ref, v_ref, prob_ref, att_ref, out_ref, weight_ref, sems = rest[count:]
    tokens = hid_ref.shape[0]
    for copy in fetch_half(where_ref, parts, weight_ref, sems):
        copy.wait()
    q_ref[...] = nt(norm_ref[...], weight_ref[0]).astype(BF)
    k_ref[...] = nt(norm_ref[...], weight_ref[1]).astype(BF)
    v_ref[...] = nt(norm_ref[...], weight_ref[2]).astype(BF)
    pairs = q_ref.shape[1] // 128
    lane = lax.broadcasted_iota(jnp.int32, (1, 128), 1)
    lefts = [(lane < HEAD_DIM).astype(BF), (lane >= HEAD_DIM).astype(BF)]
    block = length // 2

    def step(index, carry):
        row = index // pairs
        pair = index % pairs
        packed = packed_flag(where_ref, seg_ref, row, length)
        lanes = pl.ds(pl.multiple_of(pair * 128, 128), 128)
        for part in range(2):
            keys = (part + 1) * block
            here = pl.ds(pl.multiple_of(row * length + part * block, block), block)
            upto = pl.ds(pl.multiple_of(row * length, length), keys)
            mask = allowed_mask(packed, quarter, part * block, block, keys)
            queries = q_ref[here, lanes]
            key_rows = k_ref[upto, lanes]
            values = v_ref[upto, lanes]
            result = None
            for head in range(2):
                scores = nt(queries * lefts[head], key_rows) * SCALE
                scores = jnp.where(mask, scores, -1e30)
                top = jnp.max(scores, -1, keepdims=True)
                grown = jnp.exp(scores - top)
                probs = (grown / jnp.sum(grown, -1, keepdims=True)).astype(BF)
                prob_ref[2 * index + head, part * block : (part + 1) * block, :keys] = probs
                term = nn(probs, values * lefts[head])
                result = term if result is None else result + term
            att_ref[here, lanes] = result.astype(BF)
        return carry

    lax.fori_loop(0, tokens // length * pairs, step, 0)
    out_ref[...] = hid_ref[...] + nn(att_ref[...], weight_ref[3])


def up_kernel(
    where_ref, hid_ref, gain_ref, bias_ref, own, near, far, far_other, cross, cross_other,
    own_t, near_t, far_t, cross_t,
    norm_ref, act_ref, slope_ref, weight_ref, bup_ref, sems, bias_sems,
):
    tokens, width = hid_ref.shape
    copies = fetch_full(where_ref, (own, near, far, far_other, cross, cross_other), weight_ref, sems)
    last = pl.ds(far_t.shape[0] - EXTRA, EXTRA)
    packs = (own_t.at[0, last], near_t.at[0, last], far_t.at[last], cross_t.at[last])
    copies += start_copies([(pack, bup_ref.at[slot]) for slot, pack in enumerate(packs)], bias_sems)

    def normalize(at):
        xhat, _ = norm_parts(hid_ref[at])
        norm_ref[at] = (xhat * gain_ref[...] + bias_ref[...]).astype(BF)

    over_rows(tokens, normalize)
    for copy in copies:
        copy.wait()
    block = 128

    def step(slot, carry):
        bias = bup_ref[slot, :1].astype(F32)
        for first in range(0, tokens, block):
            at = slice(first, first + block)
            pre = nn(norm_ref[at], weight_ref[slot]) + bias
            value, slope = gelu_pair(pre)
            act_ref[slot, at] = value.astype(BF)
            slope_ref[slot, at] = slope.astype(BF)
        return carry

    lax.fori_loop(0, act_ref.shape[0], step, 0)


def send_pieces(where_ref, stage_ref, slot, keep, send, sems, rows):
    even = slot % 2 == 0
    place = slot // 2

    for piece in range(PIECES):
        target = piece ^ where_ref[2]
        source = stage_ref.at[piece * rows : (piece + 1) * rows]

        @pl.when(even)
        def _():
            pltpu.make_async_copy(source, keep.at[place, target, :rows], sems.at[piece]).start()

        @pl.when(jnp.logical_not(even))
        def _():
            pltpu.make_async_copy(source, send.at[place, target, :rows], sems.at[piece]).start()


def wait_pieces(stage_ref, keep, sems, rows):
    for piece in range(PIECES):
        source = stage_ref.at[piece * rows : (piece + 1) * rows]
        pltpu.make_async_copy(source, keep.at[0, 0, :rows], sems.at[piece]).wait()


def down_kernel(
    where_ref, seg_ref, hid_ref, act_ref, bdown_ref, wout_ref, bout_ref, patch_ref, lgrad_ref, dgrad_ref,
    own, near, far, far_other, cross, cross_other,
    latent_ref, logdet_ref, stat_ref, direct_ref, grad_ref, gwout_ref, gvec_ref, keep_ref, send_ref,
    weight_ref, branch_ref, stage_ref, sems, out_sems,
    *, length, quarter,
):
    tokens, width = hid_ref.shape
    channels = patch_ref.shape[0]
    for copy in fetch_full(where_ref, (own, near, far, far_other, cross, cross_other), weight_ref, sems):
        copy.wait()
    total = nn(act_ref[0], weight_ref[0])
    for slot in range(1, 4):
        total = total + nn(act_ref[slot], weight_ref[slot])
    top_low = (hid_ref[...] + total + bdown_ref[...]).astype(BF)
    head_out = nt(wout_ref[...], top_low) + bout_ref[...]
    token = lax.broadcasted_iota(jnp.int32, (1, tokens), 1)
    row_count = tokens // length
    starts = jnp.zeros((1, tokens), jnp.bool_)
    for row in range(row_count):
        packed = packed_flag(where_ref, seg_ref, row, length)
        inside = (token >= row * length) & (token < (row + 1) * length)
        fresh = (token & jnp.where(packed, quarter - 1, length - 1)) == 0
        starts = starts | (inside & fresh)
    previous = jnp.where(starts, 0.0, pltpu.roll(head_out, 1, 1))
    shifts = previous[:channels]
    logscale = previous[channels:]
    shrink = jnp.exp(-logscale)
    latents = (patch_ref[...] - shifts) * shrink
    latent_ref[...] = latents
    logdet_ref[...] = -column_sum(logscale)
    stats = jnp.zeros(stat_ref.shape, F32)
    lane = lax.broadcasted_iota(jnp.int32, stat_ref.shape, 1)
    kind = lax.broadcasted_iota(jnp.int32, stat_ref.shape, 0)
    for row in range(row_count):
        part = logscale[:, row * length : (row + 1) * length]
        mean = jnp.sum(part) * (1.0 / (length * channels))
        stats = jnp.where((lane == row) & (kind == 0), mean, stats)
        stats = jnp.where((lane == row) & (kind == 1), jnp.max(part), stats)
    stat_ref[...] = stats
    lgrad = lgrad_ref[...]
    direct = lgrad * shrink
    direct_ref[...] = direct
    grad_prev = jnp.concatenate([-direct, -lgrad * latents - dgrad_ref[...]], 0)
    grad_prev = jnp.where(starts, 0.0, grad_prev)
    grad_head = pltpu.roll(grad_prev, tokens - 1, 1).astype(BF)
    gwout_ref[...] = nn(grad_head, top_low)
    grad_hidden = tn(grad_head, wout_ref[...])
    grad_ref[...] = grad_hidden
    branch_ref[...] = grad_hidden.astype(BF)
    gvec_ref[...] = jnp.zeros(gvec_ref.shape, F32)
    gvec_ref[0:1, :] = column_sum(grad_hidden)
    row_of = nt(jnp.ones((8, tokens), BF), grad_head)
    gvec_ref[1:2, : 2 * channels] = row_of[:1]
    rows = width // PIECES

    def step(slot, carry):
        @pl.when(slot >= 2)
        def _():
            wait_pieces(stage_ref.at[slot % 2], keep_ref, out_sems.at[slot % 2], rows)

        stage_ref[slot % 2] = tn(act_ref[slot], branch_ref[...]).astype(BF)
        send_pieces(where_ref, stage_ref.at[slot % 2], slot, keep_ref, send_ref, out_sems.at[slot % 2], rows)
        return carry

    lax.fori_loop(0, 4, step, 0)
    for slot in range(2):
        wait_pieces(stage_ref.at[slot], keep_ref, out_sems.at[slot], rows)


def up_back_kernel(
    where_ref, grad_ref, slope_ref, norm_ref, hid_ref, gain_ref,
    own_d, near_d, far_d, far_other_d, cross_d, cross_other_d,
    own_u, near_u, far_u, far_other_u, cross_u, cross_other_u,
    gout_ref, mix_ref, gvec_ref, keep_ref, send_ref,
    down_ref, up_ref, branch_ref, total_ref, pre_ref, stage_ref, sems, out_sems,
):
    tokens, width = grad_ref.shape
    copies = fetch_full(
        where_ref, (own_d, near_d, far_d, far_other_d, cross_d, cross_other_d), down_ref, sems.at[0]
    )
    copies += fetch_full(
        where_ref, (own_u, near_u, far_u, far_other_u, cross_u, cross_other_u), up_ref, sems.at[1]
    )
    branch_ref[...] = grad_ref[...].astype(BF)
    total_ref[...] = jnp.zeros(total_ref.shape, F32)
    gvec_ref[...] = jnp.zeros(gvec_ref.shape, F32)
    for copy in copies:
        copy.wait()
    rows = width // PIECES

    def step(slot, carry):
        @pl.when(slot >= 2)
        def _():
            wait_pieces(stage_ref.at[slot % 2], keep_ref, out_sems.at[slot % 2], rows)

        grad_pre = (nt(branch_ref[...], down_ref[slot]) * slope_ref[slot].astype(F32)).astype(BF)
        pre_ref[...] = grad_pre
        gvec_ref[pl.ds(slot, 1), :] = column_sum(grad_pre.astype(F32))
        stage_ref[slot % 2] = tn(norm_ref[...], pre_ref[...]).astype(BF)
        send_pieces(where_ref, stage_ref.at[slot % 2], slot, keep_ref, send_ref, out_sems.at[slot % 2], rows)
        total_ref[...] += nt(pre_ref[...], up_ref[slot])
        return carry

    lax.fori_loop(0, 4, step, 0)

    def finish(at):
        xhat, rstd = norm_parts(hid_ref[at])
        grad = total_ref[at]
        value = grad_ref[at] + norm_back(grad, gain_ref[...], xhat, rstd)
        gout_ref[at] = value
        mix_ref[at] = value.astype(BF)
        gvec_ref[4:5, :] += column_sum(grad * xhat)
        gvec_ref[5:6, :] += column_sum(grad)

    over_rows(tokens, finish)
    for slot in range(2):
        wait_pieces(stage_ref.at[slot], keep_ref, out_sems.at[slot], rows)


def attend_back_kernel(
    where_ref, mix_ref, q_ref, k_ref, v_ref, prob_ref, att_ref, norm_ref, *rest, length, quarter, count, chained
):
    before_ref = rest[0] if chained else None
    rest = rest[1:] if chained else rest
    parts = rest[:count]
    (
        total_ref, gq_ref, keep_ref, send_ref,
        weight_ref, gatt_ref, dq_ref, dk_ref, dv_ref, stage_ref, sems, out_sems,
    ) = rest[count:]
    tokens = mix_ref.shape[0]
    for copy in fetch_half(where_ref, parts, weight_ref, sems):
        copy.wait()
    gatt_ref[...] = nt(mix_ref[...], weight_ref[3]).astype(BF)
    pairs = q_ref.shape[1] // 128
    lane = lax.broadcasted_iota(jnp.int32, (1, 128), 1)
    lefts = [(lane < HEAD_DIM).astype(BF), (lane >= HEAD_DIM).astype(BF)]
    block = length // 2
    unit = weight_ref.shape[1] // 2
    rows = unit // PIECES

    def publish(kind, left, right):
        stage_ref[kind] = tn(left, right).astype(BF)
        for slot, into in enumerate((keep_ref, send_ref)):
            for piece in range(PIECES):
                at = slot * unit + piece * rows
                pltpu.make_async_copy(
                    stage_ref.at[kind, at : at + rows],
                    into.at[piece ^ where_ref[2], kind * rows : (kind + 1) * rows],
                    out_sems.at[kind, slot * PIECES + piece],
                ).start()

    publish(2, att_ref[...], mix_ref[...])

    def step(index, carry):
        row = index // pairs
        pair = index % pairs
        lanes = pl.ds(pl.multiple_of(pair * 128, 128), 128)
        grads_k = [None, None]
        grads_v = [None, None]
        for part in range(2):
            keys = (part + 1) * block
            here = pl.ds(pl.multiple_of(row * length + part * block, block), block)
            upto = pl.ds(pl.multiple_of(row * length, length), keys)
            queries = q_ref[here, lanes]
            key_rows = k_ref[upto, lanes]
            values = v_ref[upto, lanes]
            grad_out = gatt_ref[here, lanes]
            result = None
            for head in range(2):
                probs = prob_ref[2 * index + head, part * block : (part + 1) * block, :keys]
                wide = probs.astype(F32)
                grad_mine = grad_out * lefts[head]
                grad_probs = nt(grad_mine, values)
                inner = jnp.sum(wide * grad_probs, -1, keepdims=True)
                grad_scores = (wide * (grad_probs - inner) * SCALE).astype(BF)
                term = nn(grad_scores, key_rows * lefts[head])
                result = term if result is None else result + term
                term_k = tn(grad_scores, queries * lefts[head])
                term_v = tn(probs, grad_mine)
                grads_k[part] = term_k if grads_k[part] is None else grads_k[part] + term_k
                grads_v[part] = term_v if grads_v[part] is None else grads_v[part] + term_v
            dq_ref[here, lanes] = result.astype(BF)
        low = pl.ds(pl.multiple_of(row * length, length), block)
        high = pl.ds(pl.multiple_of(row * length + block, block), block)
        dk_ref[low, lanes] = (grads_k[0] + grads_k[1][:block]).astype(BF)
        dk_ref[high, lanes] = grads_k[1][block:].astype(BF)
        dv_ref[low, lanes] = (grads_v[0] + grads_v[1][:block]).astype(BF)
        dv_ref[high, lanes] = grads_v[1][block:].astype(BF)
        return carry

    lax.fori_loop(0, tokens // length * pairs, step, 0)
    publish(0, dk_ref[...], norm_ref[...])
    publish(1, dv_ref[...], norm_ref[...])
    gq_ref[...] = tn(dq_ref[...], norm_ref[...]).astype(BF)
    total = nn(dq_ref[...], weight_ref[0]) + nn(dk_ref[...], weight_ref[1]) + nn(dv_ref[...], weight_ref[2])
    if chained:
        total = total + before_ref[...]
    total_ref[...] = total
    for kind in range(3):
        for piece in range(2 * PIECES):
            pltpu.make_async_copy(
                stage_ref.at[kind, :rows], keep_ref.at[0, :rows], out_sems.at[kind, piece]
            ).wait()


def embed_back_kernel(
    where_ref, seg_ref, label_ref, grad_ref, total_ref, hid_ref, gain_ref, patch_ref, direct_ref, win_ref,
    gwout_ref, gdown_ref, gup_ref, gq_near, gq_far,
    pgrad_ref, slot_ref, keep_ref, send_ref,
    value_ref, embed_ref, acc_ref, small_ref, sems,
    *, length, quarter,
):
    tokens, width = hid_ref.shape
    channels = patch_ref.shape[0]
    unit = width // 4
    rows = unit // PIECES
    sources = []
    for slot in range(4):
        source = (gq_near, gq_far)[slot // 2]
        into = (keep_ref, send_ref)[slot % 2]
        for piece in range(PIECES):
            at = (slot % 2) * unit + piece * rows
            sources.append((source.at[at : at + rows], into.at[slot // 2, piece ^ where_ref[2], :rows]))
    copies = start_copies(sources, sems.at[0])
    acc_ref[...] = jnp.zeros(acc_ref.shape, F32)

    def finish(at):
        xhat, rstd = norm_parts(hid_ref[at])
        grad = total_ref[at]
        acc_ref[1:2, :] += column_sum(grad * xhat)
        acc_ref[2:3, :] += column_sum(grad)
        value = grad_ref[at] + norm_back(grad, gain_ref[...], xhat, rstd)
        value_ref[at] = value
        embed = value.astype(BF)
        embed_ref[at] = embed
        acc_ref[0:1, :] += column_sum(embed.astype(F32))

    over_rows(tokens, finish)
    acc_ref[3:5, :] = gup_ref[4:6, :]
    acc_ref[5:7, :] = gdown_ref[0:2, :]
    for slot in range(4):
        acc_ref[pl.ds(7 + (slot ^ where_ref[3]), 1), :] = gup_ref[slot : slot + 1, :]
    small_ref[:channels] = nn(patch_ref[...].astype(BF), embed_ref[...]).astype(BF)
    small_ref[channels : 3 * channels] = gwout_ref[...].astype(BF)
    first = 3 * channels
    rows_here = tokens // length
    slots = length // quarter
    packed = [packed_flag(where_ref, seg_ref, row, length) for row in range(rows_here)]
    zero = jnp.zeros((quarter, width), F32)
    for slot in range(slots):
        value = zero
        for row in range(rows_here):
            at = row * length + slot * quarter
            here = value_ref[at : at + quarter]
            value = value + jnp.where(packed[row], 0.0, here)
            if slot == 0:
                every = here
                for later in range(1, slots):
                    every = every + value_ref[at + later * quarter : at + (later + 1) * quarter]
                value = value + jnp.where(packed[row], every, 0.0)
        small_ref[first + slot * quarter : first + (slot + 1) * quarter] = value.astype(BF)
    start = first + length
    small_ref[start : start + EXTRA] = acc_ref[...].astype(BF)
    start += EXTRA
    small_ref[start:] = jnp.zeros((small_ref.shape[0] - start, width), BF)
    moved = []
    for block in range(4):
        slot = block ^ where_ref[3]
        for piece in range(PIECES):
            at = (block * PIECES + piece) * GROUP
            moved.append((slot, piece ^ where_ref[2], small_ref.at[at : at + GROUP]))
    for index, (slot, piece, source) in enumerate(moved):

        @pl.when(slot % 2 == 0)
        def _():
            into = keep_ref.at[slot // 2, piece, rows:]
            pltpu.make_async_copy(source, into, sems.at[1, index]).start()

        @pl.when(slot % 2 == 1)
        def _():
            into = send_ref.at[slot // 2, piece, rows:]
            pltpu.make_async_copy(source, into, sems.at[1, index]).start()

    lane = lax.broadcasted_iota(jnp.int32, (1, slot_ref.shape[1] - width), 1)
    for row in range(rows_here):
        sums = []
        for slot in range(slots):
            at = row * length + slot * quarter
            sums.append(column_sum(value_ref[at : at + quarter]))
        every = sums[0]
        for slot in range(1, slots):
            every = every + sums[slot]
        for slot in range(slots):
            other = every if slot == 0 else jnp.zeros_like(every)
            index = row * slots + slot
            slot_ref[index : index + 1, :width] = jnp.where(packed[row], sums[slot], other)
            label = label_ref[row, slot]
            digits = jnp.where(lane == 0, label >> 5, jnp.where(lane == 1, label & 31, 0))
            slot_ref[index : index + 1, width:] = digits.astype(F32)
    pgrad_ref[...] = direct_ref[...] + nt(win_ref[...], embed_ref[...])
    for copy in copies:
        copy.wait()
    for index in range(4 * PIECES):
        pltpu.make_async_copy(
            small_ref.at[:GROUP], keep_ref.at[0, 0, rows:], sems.at[1, index]
        ).wait()


def piece_list(low, high):
    found = []
    for bit, ref in ((0, low), (1, high)):
        for i in range(ref.shape[0]):
            for j in range(ref.shape[1]):
                found.append((ref, i, j, i + (bit if low.shape[0] == 1 else 0), j + (bit if low.shape[1] == 1 else 0)))
    return [(ref, i, j, 2 * x + z) for ref, i, j, x, z in found]


def place_kernel(where_ref, low_ref, high_ref, out_ref):
    rows = low_ref.shape[2]
    for ref, i, j, piece in piece_list(low_ref, high_ref):
        at = pl.multiple_of((piece ^ where_ref[2]) * rows, rows)
        out_ref[pl.ds(at, rows)] = ref[i, j].astype(F32)


def place_last_kernel(
    where_ref, mix_low, mix_high, low_ref, high_ref, all_ref,
    gk_ref, gv_ref, go_ref, gq_ref, gin_ref, gout_ref, gpos_ref, *rest,
):
    *vectors, bup_ref, bout_ref, flat_ref = rest
    rows = gq_ref.shape[0] // PIECES
    for ref, i, j, piece in piece_list(mix_low, mix_high):
        at = pl.ds(pl.multiple_of((piece ^ where_ref[2]) * rows, rows), rows)
        gk_ref[at] = ref[i, j, :rows].astype(F32)
        gv_ref[at] = ref[i, j, rows : 2 * rows].astype(F32)
        go_ref[at] = ref[i, j, 2 * rows :].astype(F32)
    for ref, i, j, piece in piece_list(low_ref, high_ref):
        at = pl.ds(pl.multiple_of((piece ^ where_ref[2]) * rows, rows), rows)
        gq_ref[at] = ref[i, j, :rows].astype(F32)
    channels = gin_ref.shape[0]
    for slot in range(4):
        rel = (0, 2, 1, 3)[slot]
        for piece in range(PIECES):
            group = (rel ^ where_ref[3]) * PIECES + (piece ^ where_ref[2])
            flat_ref[pl.ds(pl.multiple_of(group * GROUP, GROUP), GROUP)] = all_ref[slot, piece].astype(F32)
    start = 3 * channels
    gin_ref[...] = flat_ref[:channels]
    gout_ref[...] = flat_ref[channels:start]
    length = gpos_ref.shape[0]
    gpos_ref[...] = flat_ref[start : start + length]
    start += length
    for index, ref in enumerate(vectors):
        ref[...] = flat_ref[start + index : start + index + 1]
    bout_ref[...] = flat_ref[start + 6 : start + 7, : bout_ref.shape[1]]
    bup_ref[...] = flat_ref[pl.ds(start + 7 + where_ref[3], 1)]


def make_program(rows_size, heads_size):
    levels = rows_size.bit_length() - 1

    def swap_heads(array, bit):
        return lax.ppermute(array, "heads", [(i, i ^ bit) for i in range(heads_size)])

    def swap_rows(array, bit):
        return lax.ppermute(array, "rows", [(i, i ^ bit) for i in range(rows_size)])

    def add_low(arrays):
        total = arrays[0].astype(F32)
        for other in arrays[1:]:
            total = total + other.astype(F32)
        return total.astype(BF)

    def ordered(value, token):
        value, token = lax.optimization_barrier((value, token))
        return value

    class Chain:
        axes = {"x": (1, 1), "z": (2, 2)}

        def __init__(self, order):
            self.order = order
            self.near, self.far, self.both = [], [], []
            self.left = list(order) + ["w"] + [a for a in reversed(order) if a != "y"]

        def add(self, group, *arrays):
            for array in arrays:
                group.append(array.reshape((-1, 2, 2) + array.shape[-2:]))

        def core(self, group, send, token):
            send = ordered(send, token)
            self.add(group, swap_heads(send, 1))
            return send

        def side(self, arrays, axis, index):
            return [lax.slice_in_dim(t, index, index + 1, axis=axis) for t in arrays]

        def step(self, token):
            kind = self.left.pop(0)
            reducing = "w" in self.left
            if kind == "y":
                send = ordered(add_low(self.side(self.both, 0, 1) + self.far), token)
                self.both = self.side(self.both, 0, 0) + self.near + [swap_heads(send, 2)]
            elif kind == "w":
                total = add_low(self.both)
                for level in range(2, levels):
                    send = ordered(total, token)
                    total = add_low([send, swap_rows(send, 1 << level)])
                self.total = total
            elif reducing:
                axis, bit = self.axes[kind]
                send = ordered(add_low(self.side(self.both, axis, 1)), token)
                self.both = self.side(self.both, axis, 0) + [swap_rows(send, bit)]
            else:
                axis, bit = self.axes[kind]
                send = ordered(self.total, token)
                got = swap_rows(send, bit)
                if self.left:
                    self.total = jnp.concatenate([send, got], axis)
                else:
                    self.low, self.high = send[0], got[0]
            return send

    def program(
        patches, segments, labels, w_in, b_in, pos_table, cls_table, ln1_gain, ln1_bias,
        w_query, w_key, w_value, w_attn_out, ln2_gain, ln2_bias, w_up, b_up, w_down, b_down,
        w_out, b_out, latent_grad, logdet_grad,
    ):
        tokens, channels = patches.shape
        length, width = pos_table.shape
        slot_count = labels.shape[1]
        quarter = length // slot_count
        classes = cls_table.shape[0]
        part = w_query.shape[2]
        row_count = tokens // length
        head_index = lax.axis_index("heads")
        row_index = lax.axis_index("rows")
        row_bit = row_index & 1
        mask = ((row_index & 1) << 1) | ((row_index >> 1) & 1)
        where = jnp.stack([head_index * tokens, row_bit, mask, head_index]).astype(jnp.int32)
        rows = width // PIECES
        unit = part // PIECES
        heads = width // HEAD_DIM
        square = 2 * tokens * width * width

        def shape(*dims, dtype=F32):
            return jax.ShapeDtypeStruct(dims, dtype)

        def call(kernel, operands, specs, outs, out_specs, scratch=(), work=1.0, **options):
            return pl.pallas_call(
                functools.partial(kernel, **options) if options else kernel,
                in_specs=specs,
                out_specs=out_specs,
                out_shape=outs,
                scratch_shapes=list(scratch),
                compiler_params=pltpu.CompilerParams(vmem_limit_bytes=60 << 20),
                cost_estimate=pl.CostEstimate(
                    flops=int(work * square), transcendentals=0, bytes_accessed=8 << 20
                ),
            )(*operands)

        dma = pltpu.SemaphoreType.DMA
        low = shape(tokens, width, dtype=BF)
        full = shape(tokens, width)
        half_low = shape(tokens, width // 2, dtype=BF)

        bias_rows = jnp.pad(b_up, ((0, EXTRA - 1), (0, 0)))
        pack_t = jnp.stack(
            [
                jnp.concatenate([w_query[0].T, w_key[0].T, bias_rows], 0),
                jnp.concatenate([w_value[0].T, w_attn_out[0], bias_rows], 0),
            ]
        )
        own_u, own_d = w_up[0], w_down[0]
        half_rows = width // 2
        half_t = lax.dynamic_index_in_dim(pack_t, row_bit, 0, keepdims=False)
        far_t = swap_heads(half_t, 2)
        near_t = swap_heads(ordered(pack_t, half_t), 1)
        half_u = lax.dynamic_slice_in_dim(own_u, row_bit * half_rows, half_rows, 0)
        half_d = lax.dynamic_slice_in_dim(own_d, row_bit * half_rows, half_rows, 0)
        near_u = swap_heads(ordered(own_u, half_t), 1)
        near_d = swap_heads(ordered(own_d, half_t), 1)
        cls_rows = cls_table[labels.reshape(-1)].astype(F32)
        patches_t = patches.T
        hidden0, normed1 = call(
            embed_kernel,
            (
                where, segments, ordered(patches_t, half_t), w_in, b_in[None], pos_table, cls_rows,
                ln1_gain, ln1_bias,
            ),
            [SMEM, SMEM] + [VMEM] * 7,
            (full, low),
            (VMEM, VMEM),
            work=0.3,
        )
        far_t = ordered(far_t, normed1)
        far_other_t = swap_rows(far_t, 1)
        half_u = ordered(half_u, far_t)
        far_u = swap_heads(half_u, 2)
        cross_t = swap_heads(far_t, 1)

        def attend(hidden, normed, parts):
            return call(
                attend_kernel,
                (where, segments, hidden, normed) + parts,
                [SMEM, SMEM, VMEM, VMEM] + [HBM] * len(parts),
                (
                    half_low, half_low, half_low,
                    shape(row_count * heads // 2, length, length, dtype=BF), half_low, full,
                ),
                (VMEM,) * 6,
                [pltpu.VMEM((4, width // 2, width), BF), dma((8,))],
                work=5.0,
                length=length,
                quarter=quarter,
                count=len(parts),
            )

        parts_near = (pack_t, near_t)
        *saved_near, mixed = attend(hidden0, ordered(normed1, half_u), parts_near)
        far_other_t = ordered(far_other_t, mixed)
        cross_other_t = swap_heads(far_other_t, 1)
        far_u = ordered(far_u, far_other_t)
        far_other_u = swap_rows(far_u, 1)
        half_d = ordered(half_d, far_u)
        far_d = swap_heads(half_d, 2)
        cross_u = swap_heads(far_u, 1)
        parts_far = (far_t, far_other_t, cross_t, cross_other_t)
        *saved_far, hidden1 = attend(mixed, ordered(normed1, half_d), parts_far)
        far_other_u = ordered(far_other_u, hidden1)
        cross_other_u = swap_heads(far_other_u, 1)
        far_d = ordered(far_d, hidden1)
        far_other_d = swap_rows(far_d, 1)
        cross_d = swap_heads(far_d, 1)
        parts_u = (own_u, near_u, far_u, far_other_u, cross_u, cross_other_u)
        four = shape(heads_size, tokens, width, dtype=BF)
        normed2, activated, slope = call(
            up_kernel,
            (where, ordered(hidden1, far_d), ln2_gain, ln2_bias)
            + parts_u
            + (pack_t, near_t, far_t, cross_t),
            [SMEM] + [VMEM] * 3 + [HBM] * 10,
            (low, four, four),
            (VMEM,) * 3,
            [
                pltpu.VMEM((heads_size, width, width), BF),
                pltpu.VMEM((heads_size, EXTRA, width), BF),
                dma((6,)),
                dma((4,)),
            ],
            work=6.0,
        )
        far_other_d = ordered(far_other_d, normed2)
        cross_other_d = swap_heads(far_other_d, 1)
        parts_d = (own_d, near_d, far_d, far_other_d, cross_d, cross_other_d)
        pieces = shape(2, PIECES, rows, width, dtype=BF)
        stage = pltpu.VMEM((2, width, width), BF)
        out_sems = dma((2, PIECES))
        latents, logdet, stats, direct, grad_hidden2, grad_w_out, gdown, keep_d, send_d = call(
            down_kernel,
            (
                where, segments, hidden1, activated, b_down, w_out.T, b_out[:, None], patches_t, latent_grad.T,
                logdet_grad[None],
            )
            + parts_d,
            [SMEM, SMEM] + [VMEM] * 8 + [HBM] * 6,
            (
                shape(channels, tokens), shape(1, tokens), shape(8, 128), shape(channels, tokens),
                full, shape(2 * channels, width), shape(8, width), pieces, pieces,
            ),
            (VMEM,) * 7 + (HBM, HBM),
            [pltpu.VMEM((heads_size, width, width), BF), pltpu.VMEM((tokens, width), BF), stage, dma((6,)), out_sems],
            work=8.0,
            length=length,
            quarter=quarter,
        )
        chains = [Chain(order) for order in CHAIN_ORDERS]
        down, up, mix, last = chains
        down.add(down.both, keep_d)
        token = down.core(down.both, send_d, grad_hidden2)
        grad_hidden1, grad_mix, gup, keep_u, send_u = call(
            up_back_kernel,
            (where, ordered(grad_hidden2, token), slope, normed2, hidden1, ln2_gain) + parts_d + parts_u,
            [SMEM] + [VMEM] * 5 + [HBM] * 12,
            (full, low, shape(8, width), pieces, pieces),
            (VMEM, VMEM, VMEM, HBM, HBM),
            [
                pltpu.VMEM((heads_size, width, width), BF),
                pltpu.VMEM((heads_size, width, width), BF),
                pltpu.VMEM((tokens, width), BF),
                pltpu.VMEM((tokens, width), F32),
                pltpu.VMEM((tokens, width), BF),
                stage,
                dma((2, 6)),
                out_sems,
            ],
            work=12.0,
        )
        up.add(up.both, keep_u)
        token = up.core(up.both, send_u, grad_mix)

        def advance(order, token):
            for index in order:
                token = chains[index].step(token)
            return token

        def attend_back(saved, parts, before, token):
            chained = () if before is None else (before,)
            mixed_pieces = shape(PIECES, 3 * unit, width, dtype=BF)
            return call(
                attend_back_kernel,
                (where, ordered(grad_mix, token)) + tuple(saved) + (normed1,) + chained + parts,
                [SMEM] + [VMEM] * (7 + len(chained)) + [HBM] * len(parts),
                (full, shape(width // 2, width, dtype=BF), mixed_pieces, mixed_pieces),
                (VMEM, VMEM, HBM, HBM),
                [pltpu.VMEM((4, width // 2, width), BF)]
                + [pltpu.VMEM((tokens, width // 2), BF)] * 4
                + [pltpu.VMEM((3, width // 2, width), BF), dma((8,)), dma((3, 2 * PIECES))],
                work=8.0,
                length=length,
                quarter=quarter,
                count=len(parts),
                chained=before is not None,
            )

        token = advance(BEFORE_FAR, token)
        total_far, gq_far, keep_far, send_far = attend_back(saved_far, parts_far, None, token)
        mix.add(mix.far, keep_far)
        token = mix.core(mix.far, send_far, total_far)
        token = advance(BEFORE_NEAR, token)
        total_near, gq_near, keep_near, send_near = attend_back(saved_near, parts_near, total_far, token)
        mix.add(mix.near, keep_near)
        token = mix.core(mix.near, send_near, total_near)
        token = advance(BEFORE_EMBED, token)
        groups = 4 * PIECES
        last_pieces = shape(2, PIECES, unit + GROUP, width, dtype=BF)
        patches_grad, slot_rows, keep_q, send_q = call(
            embed_back_kernel,
            (
                where, segments, labels, ordered(grad_hidden1, token), total_near, hidden0, ln1_gain, patches_t,
                direct, w_in, grad_w_out, gdown, gup, gq_near, gq_far,
            ),
            [SMEM, SMEM, SMEM] + [VMEM] * 12,
            (shape(channels, tokens), shape(row_count * slot_count, width + 128), last_pieces, last_pieces),
            (VMEM, VMEM, HBM, HBM),
            [
                pltpu.VMEM((tokens, width), F32),
                pltpu.VMEM((tokens, width), BF),
                pltpu.VMEM((EXTRA, width), F32),
                pltpu.VMEM((groups * GROUP, width), BF),
                dma((2, groups)),
            ],
            work=3.0,
            length=length,
            quarter=quarter,
        )
        last.add(last.both, keep_q)
        token = last.core(last.both, send_q, patches_grad)
        gathered = slot_rows.astype(BF)
        steps = list(TAIL)
        gathers = [("r", 1 << level) for level in reversed(range(levels))] + [("h", 2), ("h", 1)]
        while steps or gathers:
            if steps:
                token = advance(steps[:1], token)
                steps = steps[1:]
            if gathers:
                kind, bit = gathers.pop(0)
                gathered = ordered(gathered, token)
                token = gathered
                swap = swap_rows if kind == "r" else swap_heads
                gathered = jnp.concatenate([gathered, swap(gathered, bit)], 0)
        digits = gathered[:, width : width + 2].astype(jnp.int32)
        slot_label = digits[:, 0] * 32 + digits[:, 1]
        label_onehot = (
            lax.broadcasted_iota(jnp.int32, (classes, 1), 0) == slot_label[None, :]
        ).astype(BF)
        sum_cls = nn(label_onehot, gathered[:, :width])

        def place(chain):
            return call(
                place_kernel, (where, chain.low, chain.high), [SMEM, VMEM, VMEM], shape(width, width), VMEM
            )

        sum_down, sum_up = place(down), place(up)
        axis = Chain.axes[[a for a in last.order if a != "y"][0]][0] - 1
        small = jnp.concatenate([last.low[:, :, unit:], last.high[:, :, unit:]], axis)
        small = small.reshape(1, PIECES, GROUP, width)
        small = jnp.concatenate([small, swap_heads(small, 2)], 0)
        small = jnp.concatenate([small, swap_heads(small, 1)], 0)
        units = shape(part, width)
        line = shape(1, width)
        sum_k, sum_v, sum_o, sum_q, sum_w_in, sum_w_out, sum_pos, *lines = call(
            place_last_kernel,
            (where, mix.low, mix.high, last.low, last.high, small),
            [SMEM] + [VMEM] * 5,
            (units,) * 4
            + (shape(channels, width), shape(2 * channels, width), shape(length, width))
            + (line,) * 7
            + (shape(1, 2 * channels),),
            (VMEM,) * 15,
            [pltpu.VMEM((groups * GROUP, width), F32)],
        )
        sum_b_in, sum_gain1, sum_bias1, sum_gain2, sum_bias2, sum_b_down, sum_b_up, sum_b_out = lines
        return (
            latents.T,
            logdet.reshape(tokens),
            patches_grad.T,
            stats[0, :row_count],
            stats[1, :row_count],
            sum_w_in,
            sum_b_in.reshape(width),
            sum_pos,
            sum_cls,
            sum_gain1,
            sum_bias1,
            sum_q.T[None],
            sum_k.T[None],
            sum_v.T[None],
            sum_o[None],
            sum_gain2,
            sum_bias2,
            sum_up[None],
            sum_b_up,
            sum_down[None],
            sum_b_down,
            sum_w_out.T,
            sum_b_out.reshape(2 * channels),
        )

    return program


def solution(mesh):
    tokens = P(("rows", "heads"))
    tokens2 = P(("rows", "heads"), None)
    last = P(None, None, "heads")
    middle = P(None, "heads", None)
    in_specs = (
        (tokens2, P("rows"), tokens2)
        + (P(),) * 6
        + (last, last, last, middle)
        + (P(), P(), last, P(None, "heads"), middle, P(), P(), P())
        + (tokens2, tokens)
    )
    out_specs = (
        (tokens2, tokens, tokens2, tokens, tokens)
        + (P(),) * 6
        + (last, last, last, middle)
        + (P(), P(), last, P(None, "heads"), middle, P(), P(), P())
    )
    program = make_program(mesh.shape["rows"], mesh.shape["heads"])
    return jax.shard_map(
        program, mesh=mesh, in_specs=in_specs, out_specs=out_specs, check_vma=False
    )
```

```python
import functools

import jax
import jax.numpy as jnp
from jax import lax
from jax.experimental import pallas as pl
from jax.experimental.pallas import tpu as pltpu
from jax.sharding import PartitionSpec as P

HEAD_DIM = 64
EPSILON = 1e-05
SCALE = HEAD_DIM**-0.5
BF = jnp.bfloat16
F32 = jnp.float32
PIECES = 4
EXTRA = 16
GROUP = 32
CHUNK = 64
GATHER_ROWS = 32
CHAIN_ORDERS = ("yxz", "zxy", "yxz", "zyx")
TAIL = (1, 3, 4, 0, 1, 3, 2, 4, 1, 3, 2, 3, 0, 2, 4, 3, 1, 4, 3, 0, 4, 2, 5, 1, 2, 5)

VMEM = pl.BlockSpec(memory_space=pltpu.VMEM)
SMEM = pl.BlockSpec(memory_space=pltpu.SMEM)
HBM = pl.BlockSpec(memory_space=pl.ANY)


def nn(matrix, other):
    return lax.dot_general(matrix, other, (((1,), (0,)), ((), ())), preferred_element_type=F32)


def tn(matrix, other):
    return lax.dot_general(matrix, other, (((0,), (0,)), ((), ())), preferred_element_type=F32)


def nt(matrix, other):
    return lax.dot_general(matrix, other, (((1,), (1,)), ((), ())), preferred_element_type=F32)


def norm_parts(values):
    average = jnp.mean(values, -1, keepdims=True)
    centered = values - average
    spread = jnp.mean(centered * centered, -1, keepdims=True)
    rstd = lax.rsqrt(spread + EPSILON)
    return centered * rstd, rstd


def norm_back(grad, gain, xhat, rstd):
    scaled = grad * gain
    back = scaled - jnp.mean(scaled, -1, keepdims=True)
    back = back - xhat * jnp.mean(scaled * xhat, -1, keepdims=True)
    return rstd * back


def column_sum(values):
    return jnp.sum(values, 0, keepdims=True)


def over_rows(tokens, body):
    def step(index, carry):
        body(pl.ds(pl.multiple_of(index * CHUNK, CHUNK), CHUNK))
        return carry

    lax.fori_loop(0, tokens // CHUNK, step, 0)


def gelu_pair(values):
    scaled = jnp.abs(values) * 0.7071067811865476
    base = 1.0 + 0.3275911 * scaled
    t = pl.reciprocal(base, approx=True)
    t = t * (2.0 - base * t)
    bell = jnp.exp(-0.5 * values * values)
    poly = 1.061405429 * t - 1.453152027
    poly = poly * t + 1.421413741
    poly = poly * t - 0.284496736
    poly = poly * t + 0.254829592
    tail = 0.5 * poly * t * bell
    below = jnp.where(values >= 0.0, 1.0 - tail, tail)
    return values * below, below + values * bell * 0.3989422804014327


def packed_flag(where_ref, seg_ref, row, length):
    start = where_ref[0] + row * length
    return seg_ref[start + length - 1] > 0


def embed_kernel(
    where_ref, seg_ref, patch_ref, w_ref, b_ref, pos_ref, cls_ref, gain_ref, bias_ref, hid_ref, norm_ref
):
    tokens, width = hid_ref.shape
    length = pos_ref.shape[0]
    slots = cls_ref.shape[0] // (tokens // length)
    quarter = length // slots
    hid_ref[...] = tn(patch_ref[...].astype(BF), w_ref[...]) + b_ref[...]
    for row in range(tokens // length):
        packed = packed_flag(where_ref, seg_ref, row, length)
        for slot in range(slots):
            at = slice(row * length + slot * quarter, row * length + (slot + 1) * quarter)
            here = pos_ref[slot * quarter : (slot + 1) * quarter].astype(F32)
            first = pos_ref[:quarter].astype(F32)
            one = cls_ref[row * slots + slot : row * slots + slot + 1]
            start = cls_ref[row * slots : row * slots + 1]
            value = hid_ref[at] + jnp.where(packed, first, here) + jnp.where(packed, one, start)
            hid_ref[at] = value
            xhat, _ = norm_parts(value)
            norm_ref[at] = (xhat * gain_ref[...] + bias_ref[...]).astype(BF)


def fetch_near(parts, weight_ref, sems):
    unit = weight_ref.shape[1] // 2
    copies = []
    for slot, ref in enumerate(parts):
        for half in range(2):
            for u in range(2):
                source = ref.at[half, pl.ds(unit * u, unit)]
                copies.append((source, weight_ref.at[2 * half + u, pl.ds(unit * slot, unit)]))
    return start_copies(copies, sems)


def fetch_far(where_ref, parts, weight_ref, sems):
    far, far_other, cross, cross_other = parts
    unit = weight_ref.shape[1] // 2
    x = where_ref[1]
    copies = []
    for slot, ref, half in ((0, far, x), (0, far_other, 1 - x), (1, cross, x), (1, cross_other, 1 - x)):
        for u in range(2):
            source = ref.at[pl.ds(unit * u, unit)]
            copies.append((source, weight_ref.at[2 * half + u, pl.ds(unit * slot, unit)]))
    return start_copies(copies, sems)


def fetch_half(where_ref, parts, weight_ref, sems):
    if len(parts) == 2:
        return fetch_near(parts, weight_ref, sems)
    return fetch_far(where_ref, parts, weight_ref, sems)


def start_copies(copies, sems):
    made = [pltpu.make_async_copy(src, dst, sems.at[i]) for i, (src, dst) in enumerate(copies)]
    for copy in made:
        copy.start()
    return made


def fetch_full(where_ref, parts, weight_ref, sems):
    own, near, far, far_other, cross, cross_other = parts
    half = weight_ref.shape[1] // 2
    mine = pl.ds(pl.multiple_of(where_ref[1] * half, half), half)
    other = pl.ds(pl.multiple_of((1 - where_ref[1]) * half, half), half)
    copies = [
        (own, weight_ref.at[0], 0),
        (near, weight_ref.at[1], 1),
        (far, weight_ref.at[2, mine], 2),
        (far_other, weight_ref.at[2, other], 2),
        (cross, weight_ref.at[3, mine], 3),
        (cross_other, weight_ref.at[3, other], 3),
    ]
    for source, target, slot in copies:
        pltpu.make_async_copy(source, target, sems.at[slot]).start()


def wait_slot(source, into_ref, sems, slot):
    pltpu.make_async_copy(source, into_ref.at[slot], sems.at[slot]).wait()


def mask_bias(packed, quarter, length):
    q = lax.broadcasted_iota(jnp.int32, (length, length), 1)
    k = lax.broadcasted_iota(jnp.int32, (length, length), 0)
    shift = quarter.bit_length() - 1
    same = (q >> shift) == (k >> shift)
    return jnp.where((k <= q) & (same | jnp.logical_not(packed)), 0.0, -1e30)


def head_lanes(value):
    lane = lax.broadcasted_iota(jnp.int32, (1, 128), 1)
    return [jnp.where(side, value, 0.0).astype(BF) for side in (lane < HEAD_DIM, lane >= HEAD_DIM)]


def attend_kernel(where_ref, seg_ref, hid_ref, norm_ref, *rest, length, quarter, count):
    parts = rest[:count]
    q_ref, k_ref, v_ref, prob_ref, att_ref, out_ref, weight_ref, bias_ref, sems = rest[count:]
    tokens = hid_ref.shape[0]
    copies = fetch_half(where_ref, parts, weight_ref, sems)
    for row in range(tokens // length):
        bias_ref[row] = mask_bias(packed_flag(where_ref, seg_ref, row, length), quarter, length)
    for copy in copies:
        copy.wait()
    q_ref[...] = nt(norm_ref[...], weight_ref[0]).astype(BF)
    k_ref[...] = nt(norm_ref[...], weight_ref[1]).astype(BF)
    v_ref[...] = nt(norm_ref[...], weight_ref[2]).astype(BF)
    pairs = q_ref.shape[1] // 128
    lefts = head_lanes(1.0)
    scaled = head_lanes(SCALE)
    block = length // 2

    def step(index, carry):
        row = index // pairs
        pair = index % pairs
        lanes = pl.ds(pl.multiple_of(pair * 128, 128), 128)
        for part in range(2):
            keys = (part + 1) * block
            here = pl.ds(pl.multiple_of(row * length + part * block, block), block)
            upto = pl.ds(pl.multiple_of(row * length, length), keys)
            bias = bias_ref[row, :keys, part * block : (part + 1) * block]
            queries = q_ref[here, lanes]
            key_rows = k_ref[upto, lanes]
            values = v_ref[upto, lanes]
            result = None
            for head in range(2):
                scores = nt(key_rows, queries * scaled[head]) + bias
                top = jnp.max(scores, 0, keepdims=True)
                grown = jnp.exp(scores - top)
                probs = (grown * (1.0 / jnp.sum(grown, 0, keepdims=True))).astype(BF)
                prob_ref[2 * index + head, :keys, part * block : (part + 1) * block] = probs
                term = tn(probs, values * lefts[head])
                result = term if result is None else result + term
            att_ref[here, lanes] = result.astype(BF)
        return carry

    lax.fori_loop(0, tokens // length * pairs, step, 0)
    out_ref[...] = hid_ref[...] + nn(att_ref[...], weight_ref[3])


def up_kernel(
    where_ref, hid_ref, gain_ref, bias_ref, own, near, far, far_other, cross, cross_other,
    own_t, near_t, far_t, cross_t,
    norm_ref, act_out, slope_out, weight_ref, bup_ref, act_ref, slope_ref, sems, bias_sems, out_sems,
):
    tokens, width = hid_ref.shape
    fetch_full(where_ref, (own, near, far, far_other, cross, cross_other), weight_ref, sems)
    last = pl.ds(far_t.shape[0] - EXTRA, EXTRA)
    packs = (own_t.at[0, last], near_t.at[0, last], far_t.at[last], cross_t.at[last])
    biases = start_copies([(pack, bup_ref.at[slot]) for slot, pack in enumerate(packs)], bias_sems)

    def normalize(at):
        xhat, _ = norm_parts(hid_ref[at])
        norm_ref[at] = (xhat * gain_ref[...] + bias_ref[...]).astype(BF)

    over_rows(tokens, normalize)
    for bias in biases:
        bias.wait()
    block = 128

    def step(slot, carry):
        wait_slot(own, weight_ref, sems, slot)
        bias = bup_ref[slot, :1].astype(F32)
        for first in range(0, tokens, block):
            at = slice(first, first + block)
            pre = nn(norm_ref[at], weight_ref[slot]) + bias
            value, slope = gelu_pair(pre)
            act_ref[slot, at] = value.astype(BF)
            slope_ref[slot, at] = slope.astype(BF)
        pltpu.make_async_copy(act_ref.at[slot], act_out.at[slot], out_sems.at[0, slot]).start()
        pltpu.make_async_copy(slope_ref.at[slot], slope_out.at[slot], out_sems.at[1, slot]).start()
        return carry

    lax.fori_loop(0, 4, step, 0)
    for slot in range(4):
        pltpu.make_async_copy(act_ref.at[slot], act_out.at[slot], out_sems.at[0, slot]).wait()
        pltpu.make_async_copy(slope_ref.at[slot], slope_out.at[slot], out_sems.at[1, slot]).wait()


def send_pieces(where_ref, stage_ref, slot, keep, sends, sems, rows):
    for piece in range(PIECES):
        source = stage_ref.at[piece * rows : (piece + 1) * rows]
        target = piece ^ where_ref[2]

        @pl.when(slot % 2 == 0)
        def _():
            pltpu.make_async_copy(source, keep.at[slot // 2, target], sems.at[piece]).start()

        for index, send in enumerate(sends):

            @pl.when(slot == 2 * index + 1)
            def _():
                pltpu.make_async_copy(source, send.at[target], sems.at[piece]).start()


def wait_pieces(stage_ref, keep, sems, rows):
    for piece in range(PIECES):
        source = stage_ref.at[piece * rows : (piece + 1) * rows]
        pltpu.make_async_copy(source, keep.at[0, 0, :rows], sems.at[piece]).wait()


def down_kernel(
    where_ref, seg_ref, hid_ref, act_in, bdown_ref, wout_ref, bout_ref, patch_ref, lgrad_ref, dgrad_ref,
    own, near, far, far_other, cross, cross_other,
    latent_ref, logdet_ref, stat_ref, direct_ref, grad_ref, gwout_ref, gvec_ref, keep_ref, send_near, send_far,
    weight_ref, act_ref, total_ref, branch_ref, stage_ref, sems, act_sems, out_sems,
    *, length, quarter,
):
    tokens, width = hid_ref.shape
    channels = patch_ref.shape[0]
    send_refs = (send_near, send_far)
    start_copies([(act_in.at[slot], act_ref.at[slot]) for slot in range(4)], act_sems)
    fetch_full(where_ref, (own, near, far, far_other, cross, cross_other), weight_ref, sems)
    total_ref[...] = hid_ref[...] + bdown_ref[...]

    def gather(slot, carry):
        wait_slot(act_in.at[slot], act_ref, act_sems, slot)
        wait_slot(own, weight_ref, sems, slot)
        total_ref[...] += nn(act_ref[slot], weight_ref[slot])
        return carry

    lax.fori_loop(0, 4, gather, 0)
    top_low = total_ref[...].astype(BF)
    head_out = nt(wout_ref[...], top_low) + bout_ref[...]
    token = lax.broadcasted_iota(jnp.int32, (1, tokens), 1)
    row_count = tokens // length
    starts = jnp.zeros((1, tokens), jnp.bool_)
    for row in range(row_count):
        packed = packed_flag(where_ref, seg_ref, row, length)
        inside = (token >= row * length) & (token < (row + 1) * length)
        fresh = (token & jnp.where(packed, quarter - 1, length - 1)) == 0
        starts = starts | (inside & fresh)
    previous = jnp.where(starts, 0.0, pltpu.roll(head_out, 1, 1))
    shifts = previous[:channels]
    logscale = previous[channels:]
    shrink = jnp.exp(-logscale)
    latents = (patch_ref[...] - shifts) * shrink
    latent_ref[...] = latents
    logdet_ref[...] = -column_sum(logscale)
    stats = jnp.zeros(stat_ref.shape, F32)
    lane = lax.broadcasted_iota(jnp.int32, stat_ref.shape, 1)
    kind = lax.broadcasted_iota(jnp.int32, stat_ref.shape, 0)
    for row in range(row_count):
        part = logscale[:, row * length : (row + 1) * length]
        mean = jnp.sum(part) * (1.0 / (length * channels))
        stats = jnp.where((lane == row) & (kind == 0), mean, stats)
        stats = jnp.where((lane == row) & (kind == 1), jnp.max(part), stats)
    stat_ref[...] = stats
    lgrad = lgrad_ref[...]
    direct = lgrad * shrink
    direct_ref[...] = direct
    grad_prev = jnp.concatenate([-direct, -lgrad * latents - dgrad_ref[...]], 0)
    grad_prev = jnp.where(starts, 0.0, grad_prev)
    grad_head = pltpu.roll(grad_prev, tokens - 1, 1).astype(BF)
    gwout_ref[...] = nn(grad_head, top_low)
    grad_hidden = tn(grad_head, wout_ref[...])
    grad_ref[...] = grad_hidden
    branch_ref[...] = grad_hidden.astype(BF)
    gvec_ref[...] = jnp.zeros(gvec_ref.shape, F32)
    gvec_ref[0:1, :] = column_sum(grad_hidden)
    row_of = nt(jnp.ones((8, tokens), BF), grad_head)
    gvec_ref[1:2, : 2 * channels] = row_of[:1]
    rows = width // PIECES


    def step(slot, carry):
        @pl.when(slot >= 2)
        def _():
            wait_pieces(stage_ref.at[slot % 2], keep_ref, out_sems.at[slot % 2], rows)

        stage_ref[slot % 2] = tn(act_ref[slot], branch_ref[...]).astype(BF)
        send_pieces(where_ref, stage_ref.at[slot % 2], slot, keep_ref, send_refs, out_sems.at[slot % 2], rows)
        return carry

    lax.fori_loop(0, 4, step, 0)
    for slot in range(2):
        wait_pieces(stage_ref.at[slot], keep_ref, out_sems.at[slot], rows)


def grad_pre_kernel(
    where_ref, grad_ref, slope_in, own, near, far, far_other, cross, cross_other,
    pre_out, sum_ref, weight_ref, slope_ref, branch_ref, pre_ref, sems, slope_sems, out_sems,
):
    start_copies([(slope_in.at[slot], slope_ref.at[slot]) for slot in range(4)], slope_sems)
    fetch_full(where_ref, (own, near, far, far_other, cross, cross_other), weight_ref, sems)
    branch_ref[...] = grad_ref[...].astype(BF)

    def step(slot, carry):
        wait_slot(slope_in.at[slot], slope_ref, slope_sems, slot)
        wait_slot(own, weight_ref, sems, slot)
        grad_pre = (nt(branch_ref[...], weight_ref[slot]) * slope_ref[slot].astype(F32)).astype(BF)
        pre_ref[slot] = grad_pre
        pltpu.make_async_copy(pre_ref.at[slot], pre_out.at[slot], out_sems.at[slot]).start()
        sum_ref[pl.ds(slot, 1), :] = column_sum(grad_pre.astype(F32))
        return carry

    lax.fori_loop(0, 4, step, 0)
    for slot in range(4):
        pltpu.make_async_copy(pre_ref.at[slot], pre_out.at[slot], out_sems.at[slot]).wait()


def up_back_kernel(
    where_ref, grad_ref, pre_in, norm_ref, hid_ref, gain_ref, own, near, far, far_other, cross, cross_other,
    gout_ref, mix_ref, gvec_ref, keep_ref, send_near, send_far,
    weight_ref, pre_ref, total_ref, stage_ref, sems, pre_sems, out_sems,
):
    tokens, width = grad_ref.shape
    send_refs = (send_near, send_far)
    start_copies([(pre_in.at[slot], pre_ref.at[slot]) for slot in range(4)], pre_sems)
    total_ref[...] = jnp.zeros(total_ref.shape, F32)
    fetch_full(where_ref, (own, near, far, far_other, cross, cross_other), weight_ref, sems)
    gvec_ref[...] = jnp.zeros(gvec_ref.shape, F32)
    rows = width // PIECES

    def step(slot, carry):
        @pl.when(slot >= 2)
        def _():
            wait_pieces(stage_ref.at[slot % 2], keep_ref, out_sems.at[slot % 2], rows)

        wait_slot(pre_in.at[slot], pre_ref, pre_sems, slot)
        wait_slot(own, weight_ref, sems, slot)
        stage_ref[slot % 2] = tn(norm_ref[...], pre_ref[slot]).astype(BF)
        send_pieces(where_ref, stage_ref.at[slot % 2], slot, keep_ref, send_refs, out_sems.at[slot % 2], rows)
        total_ref[...] += nt(pre_ref[slot], weight_ref[slot])
        return carry

    lax.fori_loop(0, 4, step, 0)

    def finish(at):
        xhat, rstd = norm_parts(hid_ref[at])
        grad = total_ref[at]
        value = grad_ref[at] + norm_back(grad, gain_ref[...], xhat, rstd)
        gout_ref[at] = value
        mix_ref[at] = value.astype(BF)
        gvec_ref[0:1, :] += column_sum(grad * xhat)
        gvec_ref[1:2, :] += column_sum(grad)

    over_rows(tokens, finish)
    for slot in range(2):
        wait_pieces(stage_ref.at[slot], keep_ref, out_sems.at[slot], rows)


def attend_back_kernel(
    where_ref, mix_ref, q_ref, k_ref, v_ref, prob_ref, att_ref, norm_ref, *rest, length, quarter, count, chained
):
    before_ref = rest[0] if chained else None
    rest = rest[1:] if chained else rest
    parts = rest[:count]
    (
        total_ref, gq_ref, keep_ref, send_ref,
        weight_ref, gatt_ref, dq_ref, dk_ref, dv_ref, stage_ref, sems, out_sems,
    ) = rest[count:]
    tokens = mix_ref.shape[0]
    for copy in fetch_half(where_ref, parts, weight_ref, sems):
        copy.wait()
    gatt_ref[...] = nt(mix_ref[...], weight_ref[3]).astype(BF)
    pairs = q_ref.shape[1] // 128
    lefts = head_lanes(1.0)
    scaled = head_lanes(SCALE)
    block = length // 2
    unit = weight_ref.shape[1] // 2
    rows = unit // PIECES

    def publish(kind, left, right):
        stage_ref[kind] = tn(left, right).astype(BF)
        for slot, into in enumerate((keep_ref, send_ref)):
            for piece in range(PIECES):
                at = slot * unit + piece * rows
                pltpu.make_async_copy(
                    stage_ref.at[kind, at : at + rows],
                    into.at[piece ^ where_ref[2], kind * rows : (kind + 1) * rows],
                    out_sems.at[kind, slot * PIECES + piece],
                ).start()

    publish(2, att_ref[...], mix_ref[...])

    def step(index, carry):
        row = index // pairs
        pair = index % pairs
        lanes = pl.ds(pl.multiple_of(pair * 128, 128), 128)
        grads_k = [None, None]
        grads_v = [None, None]
        for part in range(2):
            keys = (part + 1) * block
            here = pl.ds(pl.multiple_of(row * length + part * block, block), block)
            upto = pl.ds(pl.multiple_of(row * length, length), keys)
            queries = q_ref[here, lanes]
            key_rows = k_ref[upto, lanes]
            values = v_ref[upto, lanes]
            grad_out = gatt_ref[here, lanes]
            result = None
            for head in range(2):
                probs = prob_ref[2 * index + head, :keys, part * block : (part + 1) * block]
                wide = probs.astype(F32)
                grad_mine = grad_out * lefts[head]
                grad_probs = nt(values, grad_mine)
                inner = jnp.sum(wide * grad_probs, 0, keepdims=True)
                grad_scores = (wide * (grad_probs - inner)).astype(BF)
                term = tn(grad_scores, key_rows * scaled[head])
                result = term if result is None else result + term
                term_k = nn(grad_scores, queries * scaled[head])
                term_v = nn(probs, grad_mine)
                grads_k[part] = term_k if grads_k[part] is None else grads_k[part] + term_k
                grads_v[part] = term_v if grads_v[part] is None else grads_v[part] + term_v
            dq_ref[here, lanes] = result.astype(BF)
        low = pl.ds(pl.multiple_of(row * length, length), block)
        high = pl.ds(pl.multiple_of(row * length + block, block), block)
        dk_ref[low, lanes] = (grads_k[0] + grads_k[1][:block]).astype(BF)
        dk_ref[high, lanes] = grads_k[1][block:].astype(BF)
        dv_ref[low, lanes] = (grads_v[0] + grads_v[1][:block]).astype(BF)
        dv_ref[high, lanes] = grads_v[1][block:].astype(BF)
        return carry

    lax.fori_loop(0, tokens // length * pairs, step, 0)
    publish(0, dk_ref[...], norm_ref[...])
    publish(1, dv_ref[...], norm_ref[...])
    gq_ref[...] = tn(dq_ref[...], norm_ref[...]).astype(BF)
    total = nn(dq_ref[...], weight_ref[0]) + nn(dk_ref[...], weight_ref[1]) + nn(dv_ref[...], weight_ref[2])
    if chained:
        total = total + before_ref[...]
    total_ref[...] = total
    for kind in range(3):
        for piece in range(2 * PIECES):
            pltpu.make_async_copy(
                stage_ref.at[kind, :rows], keep_ref.at[0, :rows], out_sems.at[kind, piece]
            ).wait()


def embed_back_kernel(
    where_ref, seg_ref, label_ref, grad_ref, total_ref, hid_ref, gain_ref, patch_ref, direct_ref, win_ref,
    gwout_ref, gdown_ref, gup_ref, gpre_ref, gq_near, gq_far,
    pgrad_ref, slot_ref, keep_ref, send_ref,
    value_ref, embed_ref, acc_ref, small_ref, sems,
    *, length, quarter,
):
    tokens, width = hid_ref.shape
    channels = patch_ref.shape[0]
    unit = width // 4
    rows = unit // PIECES
    sources = []
    for slot in range(4):
        source = (gq_near, gq_far)[slot // 2]
        into = (keep_ref, send_ref)[slot % 2]
        for piece in range(PIECES):
            at = (slot % 2) * unit + piece * rows
            sources.append((source.at[at : at + rows], into.at[slot // 2, piece ^ where_ref[2], :rows]))
    copies = start_copies(sources, sems.at[0])
    acc_ref[...] = jnp.zeros(acc_ref.shape, F32)

    def finish(at):
        xhat, rstd = norm_parts(hid_ref[at])
        grad = total_ref[at]
        acc_ref[1:2, :] += column_sum(grad * xhat)
        acc_ref[2:3, :] += column_sum(grad)
        value = grad_ref[at] + norm_back(grad, gain_ref[...], xhat, rstd)
        value_ref[at] = value
        embed = value.astype(BF)
        embed_ref[at] = embed
        acc_ref[0:1, :] += column_sum(embed.astype(F32))

    over_rows(tokens, finish)
    acc_ref[3:5, :] = gup_ref[0:2, :]
    acc_ref[5:7, :] = gdown_ref[0:2, :]
    for slot in range(4):
        acc_ref[pl.ds(7 + (slot ^ where_ref[3]), 1), :] = gpre_ref[slot : slot + 1, :]
    small_ref[:channels] = nn(patch_ref[...].astype(BF), embed_ref[...]).astype(BF)
    small_ref[channels : 3 * channels] = gwout_ref[...].astype(BF)
    first = 3 * channels
    rows_here = tokens // length
    slots = length // quarter
    packed = [packed_flag(where_ref, seg_ref, row, length) for row in range(rows_here)]
    zero = jnp.zeros((quarter, width), F32)
    for slot in range(slots):
        value = zero
        for row in range(rows_here):
            at = row * length + slot * quarter
            here = value_ref[at : at + quarter]
            value = value + jnp.where(packed[row], 0.0, here)
            if slot == 0:
                every = here
                for later in range(1, slots):
                    every = every + value_ref[at + later * quarter : at + (later + 1) * quarter]
                value = value + jnp.where(packed[row], every, 0.0)
        small_ref[first + slot * quarter : first + (slot + 1) * quarter] = value.astype(BF)
    start = first + length
    small_ref[start : start + EXTRA] = acc_ref[...].astype(BF)
    start += EXTRA
    small_ref[start:] = jnp.zeros((small_ref.shape[0] - start, width), BF)
    moved = []
    for block in range(4):
        slot = block ^ where_ref[3]
        for piece in range(PIECES):
            at = (block * PIECES + piece) * GROUP
            moved.append((slot, piece ^ where_ref[2], small_ref.at[at : at + GROUP]))
    for index, (slot, piece, source) in enumerate(moved):

        @pl.when(slot % 2 == 0)
        def _():
            into = keep_ref.at[slot // 2, piece, rows:]
            pltpu.make_async_copy(source, into, sems.at[1, index]).start()

        @pl.when(slot % 2 == 1)
        def _():
            into = send_ref.at[slot // 2, piece, rows:]
            pltpu.make_async_copy(source, into, sems.at[1, index]).start()

    lane = lax.broadcasted_iota(jnp.int32, (1, slot_ref.shape[1] - width), 1)
    for row in range(rows_here):
        sums = []
        for slot in range(slots):
            at = row * length + slot * quarter
            sums.append(column_sum(value_ref[at : at + quarter]))
        every = sums[0]
        for slot in range(1, slots):
            every = every + sums[slot]
        for slot in range(slots):
            other = every if slot == 0 else jnp.zeros_like(every)
            index = row * slots + slot
            slot_ref[index : index + 1, :width] = jnp.where(packed[row], sums[slot], other)
            label = label_ref[row, slot]
            digits = jnp.where(lane == 0, label >> 5, jnp.where(lane == 1, label & 31, 0))
            slot_ref[index : index + 1, width:] = digits.astype(F32)
    pgrad_ref[...] = direct_ref[...] + nt(win_ref[...], embed_ref[...])
    for copy in copies:
        copy.wait()
    for index in range(4 * PIECES):
        pltpu.make_async_copy(
            small_ref.at[:GROUP], keep_ref.at[0, 0, rows:], sems.at[1, index]
        ).wait()


def add_kernel(*refs):
    *sources, out_ref = refs
    total = sources[0][...].astype(F32)
    for ref in sources[1:]:
        total = total + ref[...].astype(F32)
    out_ref[...] = total.astype(BF)


def piece_list(low, high):
    found = []
    for bit, ref in ((0, low), (1, high)):
        for i in range(ref.shape[0]):
            for j in range(ref.shape[1]):
                found.append((ref, i, j, i + (bit if low.shape[0] == 1 else 0), j + (bit if low.shape[1] == 1 else 0)))
    return [(ref, i, j, 2 * x + z) for ref, i, j, x, z in found]


def place_kernel(where_ref, low_ref, high_ref, out_ref):
    rows = low_ref.shape[2]
    for ref, i, j, piece in piece_list(low_ref, high_ref):
        at = pl.multiple_of((piece ^ where_ref[2]) * rows, rows)
        out_ref[pl.ds(at, rows)] = ref[i, j].astype(F32)


def place_last_kernel(
    where_ref, mix_low, mix_high, low_ref, high_ref, all_ref,
    gk_ref, gv_ref, go_ref, gq_ref, gin_ref, gout_ref, gpos_ref, *rest,
):
    *vectors, bup_ref, bout_ref, flat_ref = rest
    rows = gq_ref.shape[0] // PIECES
    for ref, i, j, piece in piece_list(mix_low, mix_high):
        at = pl.ds(pl.multiple_of((piece ^ where_ref[2]) * rows, rows), rows)
        gk_ref[at] = ref[i, j, :rows].astype(F32)
        gv_ref[at] = ref[i, j, rows : 2 * rows].astype(F32)
        go_ref[at] = ref[i, j, 2 * rows :].astype(F32)
    for ref, i, j, piece in piece_list(low_ref, high_ref):
        at = pl.ds(pl.multiple_of((piece ^ where_ref[2]) * rows, rows), rows)
        gq_ref[at] = ref[i, j, :rows].astype(F32)
    channels = gin_ref.shape[0]
    for slot in range(4):
        rel = (0, 2, 1, 3)[slot]
        for piece in range(PIECES):
            group = (rel ^ where_ref[3]) * PIECES + (piece ^ where_ref[2])
            flat_ref[pl.ds(pl.multiple_of(group * GROUP, GROUP), GROUP)] = all_ref[slot, piece].astype(F32)
    start = 3 * channels
    gin_ref[...] = flat_ref[:channels]
    gout_ref[...] = flat_ref[channels:start]
    length = gpos_ref.shape[0]
    gpos_ref[...] = flat_ref[start : start + length]
    start += length
    for index, ref in enumerate(vectors):
        ref[...] = flat_ref[start + index : start + index + 1]
    bout_ref[...] = flat_ref[start + 6 : start + 7, : bout_ref.shape[1]]
    bup_ref[...] = flat_ref[pl.ds(start + 7 + where_ref[3], 1)]


def make_program(rows_size, heads_size):
    levels = rows_size.bit_length() - 1

    def swap_heads(array, bit):
        return lax.ppermute(array, "heads", [(i, i ^ bit) for i in range(heads_size)])

    def swap_rows(array, bit):
        return lax.ppermute(array, "rows", [(i, i ^ bit) for i in range(rows_size)])

    def add_low(arrays):
        total = arrays[0].astype(F32)
        for other in arrays[1:]:
            total = total + other.astype(F32)
        return total.astype(BF)

    def tie(*values):
        return lax.optimization_barrier(values)

    def ordered(value, token):
        return tie(value, token)[0]

    class View:
        def __init__(self, array, start=(0, 0, 0), size=None):
            self.array, self.start = array, tuple(start)
            self.size = tuple(size or array.shape[:3])

        def narrow(self, axis, index):
            start, size = list(self.start), list(self.size)
            if size[axis] > 1:
                start[axis] += index
            size[axis] = 1
            return View(self.array, start, size)

        def value(self):
            stop = [a + b for a, b in zip(self.start, self.size)] + list(self.array.shape[3:])
            return lax.slice(self.array, self.start + (0, 0), stop)

    def add_views(views):
        return add_low([view.value() for view in views])

    class Chain:
        axes = {"y": 0, "x": 1, "z": 2}

        def __init__(self, order):
            self.order = order
            self.groups = []
            self.left = list(order) + ["w"] + [a for a in reversed(order) if a != "y"]

        def view(self, array):
            return View(array.reshape((-1, 2, 2) + array.shape[-2:]))

        def prepare(self, add=add_views):
            kind = self.left[0]
            if kind == "y":
                return [add([view.narrow(0, 1) for view in self.groups[-1]])]
            if "w" in self.left[1:]:
                axis = self.axes[kind]
                return [add([view.narrow(axis, 1) for view in group]) for group in self.groups]
            return [add(self.groups[0])] if kind == "w" else [self.total]

        def launch(self, sends):
            self.sends = sends
            kind = self.left[0]
            if kind == "y":
                self.got = [swap_heads(send, 2) for send in sends]
            else:
                self.got = [swap_rows(send, 1 << "xzw".index(kind)) for send in sends]

        def deliver(self, got):
            kind = self.left.pop(0)
            if kind == "w":
                self.total = add_low([self.sends[0], got[0]])
                for level in range(3, levels):
                    self.total = add_low([self.total, swap_rows(self.total, 1 << level)])
            elif "w" in self.left:
                axis = self.axes[kind]
                if kind == "y":
                    self.groups = self.groups[:1]
                self.groups = [
                    [view.narrow(axis, 0) for view in group] + [View(more)]
                    for group, more in zip(self.groups, got)
                ]
            elif self.left:
                self.total = jnp.concatenate([self.sends[0], got[0]], self.axes[kind])
            else:
                self.low, self.high = self.sends[0][0], got[0][0]

    def program(
        patches, segments, labels, w_in, b_in, pos_table, cls_table, ln1_gain, ln1_bias,
        w_query, w_key, w_value, w_attn_out, ln2_gain, ln2_bias, w_up, b_up, w_down, b_down,
        w_out, b_out, latent_grad, logdet_grad,
    ):
        tokens, channels = patches.shape
        length, width = pos_table.shape
        slot_count = labels.shape[1]
        quarter = length // slot_count
        classes = cls_table.shape[0]
        part = w_query.shape[2]
        row_count = tokens // length
        head_index = lax.axis_index("heads")
        row_index = lax.axis_index("rows")
        row_bit = row_index & 1
        mask = ((row_index & 1) << 1) | ((row_index >> 1) & 1)
        where = jnp.stack([head_index * tokens, row_bit, mask, head_index]).astype(jnp.int32)
        rows = width // PIECES
        unit = part // PIECES
        heads = width // HEAD_DIM
        square = 2 * tokens * width * width

        def shape(*dims, dtype=F32):
            return jax.ShapeDtypeStruct(dims, dtype)

        def call(kernel, operands, specs, outs, out_specs, scratch=(), room=60, **options):
            return pl.pallas_call(
                functools.partial(kernel, **options) if options else kernel,
                in_specs=specs,
                out_specs=out_specs,
                out_shape=outs,
                scratch_shapes=list(scratch),
                compiler_params=pltpu.CompilerParams(vmem_limit_bytes=room << 20),
                cost_estimate=pl.CostEstimate(
                    flops=1, transcendentals=0, bytes_accessed=1
                ),
            )(*operands)

        dma = pltpu.SemaphoreType.DMA
        low = shape(tokens, width, dtype=BF)
        full = shape(tokens, width)
        half_low = shape(tokens, width // 2, dtype=BF)

        bias_rows = jnp.pad(b_up, ((0, EXTRA - 1), (0, 0)))
        pack_t = jnp.stack(
            [
                jnp.concatenate([w_query[0].T, w_key[0].T, bias_rows], 0),
                jnp.concatenate([w_value[0].T, w_attn_out[0], bias_rows], 0),
            ]
        )
        own_u, own_d = w_up[0], w_down[0]
        half_rows = width // 2
        half_t = lax.dynamic_index_in_dim(pack_t, row_bit, 0, keepdims=False)
        far_t = swap_heads(half_t, 2)
        near_t = swap_heads(ordered(pack_t, half_t), 1)
        half_u = lax.dynamic_slice_in_dim(own_u, row_bit * half_rows, half_rows, 0)
        half_u, half_t = tie(half_u, half_t)
        far_u = swap_heads(half_u, 2)
        half_d = lax.dynamic_slice_in_dim(own_d, row_bit * half_rows, half_rows, 0)
        half_d, half_u = tie(half_d, half_u)
        far_d = swap_heads(half_d, 2)
        cls_rows = cls_table[labels.reshape(-1)].astype(F32)
        patches_t = patches.T
        hidden0, normed1 = call(
            embed_kernel,
            (
                where, segments, ordered(patches_t, half_d), w_in, b_in[None], pos_table, cls_rows,
                ln1_gain, ln1_bias,
            ),
            [SMEM, SMEM] + [VMEM] * 7,
            (full, low),
            (VMEM, VMEM),
        )
        normed1, far_t = tie(normed1, far_t)
        far_other_t = swap_rows(far_t, 1)
        cross_t = swap_heads(far_t, 1)
        near_u = swap_heads(ordered(own_u, far_t), 1)
        near_d = swap_heads(ordered(own_d, far_t), 1)

        def attend(hidden, normed, parts):
            return call(
                attend_kernel,
                (where, segments, hidden, normed) + parts,
                [SMEM, SMEM, VMEM, VMEM] + [HBM] * len(parts),
                (
                    half_low, half_low, half_low,
                    shape(row_count * heads // 2, length, length, dtype=BF), half_low, full,
                ),
                (VMEM,) * 6,
                [
                    pltpu.VMEM((4, width // 2, width), BF),
                    pltpu.VMEM((row_count, length, length), F32),
                    dma((8,)),
                ],
                length=length,
                quarter=quarter,
                count=len(parts),
            )

        parts_near = (pack_t, near_t)
        *saved_near, mixed = attend(hidden0, normed1, parts_near)
        mixed, far_other_t, far_u = tie(mixed, far_other_t, far_u)
        cross_other_t = swap_heads(far_other_t, 1)
        far_other_u = swap_rows(far_u, 1)
        cross_u = swap_heads(far_u, 1)
        parts_far = (far_t, far_other_t, cross_t, cross_other_t)
        *saved_far, hidden1 = attend(mixed, normed1, parts_far)
        hidden1, far_other_u, far_d = tie(hidden1, far_other_u, far_d)
        cross_other_u = swap_heads(far_other_u, 1)
        far_other_d = swap_rows(far_d, 1)
        cross_d = swap_heads(far_d, 1)
        parts_u = (own_u, near_u, far_u, far_other_u, cross_u, cross_other_u)
        four = shape(heads_size, tokens, width, dtype=BF)
        normed2, activated, slope = call(
            up_kernel,
            (where, hidden1, ln2_gain, ln2_bias)
            + parts_u
            + (pack_t, near_t, far_t, cross_t),
            [SMEM] + [VMEM] * 3 + [HBM] * 10,
            (low, four, four),
            (VMEM, HBM, HBM),
            [
                pltpu.VMEM((heads_size, width, width), BF),
                pltpu.VMEM((heads_size, EXTRA, width), BF),
                pltpu.VMEM((heads_size, tokens, width), BF),
                pltpu.VMEM((heads_size, tokens, width), BF),
                dma((4,)),
                dma((4,)),
                dma((2, 4)),
            ],
        )
        normed2, far_other_d = tie(normed2, far_other_d)
        cross_other_d = swap_heads(far_other_d, 1)
        parts_d = (own_d, near_d, far_d, far_other_d, cross_d, cross_other_d)
        pieces = shape(2, PIECES, rows, width, dtype=BF)
        one = shape(PIECES, rows, width, dtype=BF)
        stage = pltpu.VMEM((2, width, width), BF)
        out_sems = dma((2, PIECES))
        latents, logdet, stats, direct, grad_hidden2, grad_w_out, gdown, keep_d, *sends_d = call(
            down_kernel,
            (
                where, segments, hidden1, activated, b_down, w_out.T, b_out[:, None], patches_t, latent_grad.T,
                logdet_grad[None],
            )
            + parts_d,
            [SMEM, SMEM, VMEM, HBM] + [VMEM] * 6 + [HBM] * 6,
            (
                shape(channels, tokens), shape(1, tokens), shape(8, 128), shape(channels, tokens),
                full, shape(2 * channels, width), shape(8, width), pieces, one, one,
            ),
            (VMEM,) * 7 + (HBM,) * 3,
            [
                pltpu.VMEM((heads_size, width, width), BF),
                pltpu.VMEM((heads_size, tokens, width), BF),
                pltpu.VMEM((tokens, width), F32),
                pltpu.VMEM((tokens, width), BF),
                stage,
                dma((4,)),
                dma((4,)),
                out_sems,
            ],
            length=length,
            quarter=quarter,
        )
        chains = [Chain(order) for order in CHAIN_ORDERS]
        down, up, mix, last = chains

        def add_pieces(views):
            size = views[0].size
            block = (views[0].array.shape[3] // 2, views[0].array.shape[4])

            def spec(start):
                def at(i):
                    return tuple(a // b for a, b in zip(start, size)) + (i, 0)

                return pl.BlockSpec(size + block, at)

            return pl.pallas_call(
                add_kernel,
                grid=(2,),
                in_specs=[spec(view.start) for view in views],
                out_specs=spec((0, 0, 0)),
                out_shape=shape(*size, 2 * block[0], block[1], dtype=BF),
                cost_estimate=pl.CostEstimate(flops=1, transcendentals=0, bytes_accessed=1),
            )(*(view.array for view in views))

        def halves(chain, keep, gots):
            keep = chain.view(keep)
            return [[keep.narrow(0, index), chain.view(got)] for index, got in enumerate(gots)]

        grad_hidden2, *sends_d = tie(grad_hidden2, *sends_d)
        got_d = [swap_heads(send, 1) for send in sends_d]
        pre_grads, gpre = call(
            grad_pre_kernel,
            (where, grad_hidden2, slope) + parts_d,
            [SMEM, VMEM, HBM] + [HBM] * 6,
            (four, shape(8, width)),
            (HBM, VMEM),
            [
                pltpu.VMEM((heads_size, width, width), BF),
                pltpu.VMEM((heads_size, tokens, width), BF),
                pltpu.VMEM((tokens, width), BF),
                pltpu.VMEM((heads_size, tokens, width), BF),
                dma((4,)),
                dma((4,)),
                dma((4,)),
            ],
        )
        pre_grads, *got_d = tie(pre_grads, *got_d)
        down.groups = halves(down, keep_d, got_d)
        pre_grads, *sends = tie(pre_grads, *down.prepare(add_pieces))
        down.launch(sends)
        grad_hidden1, grad_mix, gup, keep_u, *sends_u = call(
            up_back_kernel,
            (where, grad_hidden2, pre_grads, normed2, hidden1, ln2_gain) + parts_u,
            [SMEM, VMEM, HBM] + [VMEM] * 3 + [HBM] * 6,
            (full, low, shape(8, width), pieces, one, one),
            (VMEM, VMEM, VMEM, HBM, HBM, HBM),
            [
                pltpu.VMEM((heads_size, width, width), BF),
                pltpu.VMEM((heads_size, tokens, width), BF),
                pltpu.VMEM((tokens, width), F32),
                stage,
                dma((4,)),
                dma((4,)),
                out_sems,
            ],
        )
        grad_mix, *sends_u = tie(grad_mix, *sends_u)
        got_u = [swap_heads(send, 1) for send in sends_u]

        def attend_back(saved, parts, before):
            chained = () if before is None else (before,)
            mixed_pieces = shape(PIECES, 3 * unit, width, dtype=BF)
            return call(
                attend_back_kernel,
                (where, grad_mix) + tuple(saved) + (normed1,) + chained + parts,
                [SMEM] + [VMEM] * (7 + len(chained)) + [HBM] * len(parts),
                (full, shape(width // 2, width, dtype=BF), mixed_pieces, mixed_pieces),
                (VMEM, VMEM, HBM, HBM),
                [pltpu.VMEM((4, width // 2, width), BF)]
                + [pltpu.VMEM((tokens, width // 2), BF)] * 4
                + [pltpu.VMEM((3, width // 2, width), BF), dma((8,)), dma((3, 2 * PIECES))],
                length=length,
                quarter=quarter,
                count=len(parts),
                chained=before is not None,
            )

        total_far, gq_far, keep_far, send_far = attend_back(saved_far, parts_far, None)
        total_far, send_far, *got_d = tie(total_far, send_far, *down.got)
        total_far, *got_u = tie(total_far, *got_u)
        got_far = swap_heads(send_far, 1)
        down.deliver(got_d)
        up.groups = halves(up, keep_u, got_u)
        total_far, *sends = tie(total_far, *down.prepare(add_pieces), *up.prepare(add_pieces))
        down.launch(sends[:1])
        up.launch(sends[1:])
        total_near, gq_near, keep_near, send_near = attend_back(saved_near, parts_near, total_far)
        total_near, send_near, got_far, *got_d = tie(total_near, send_near, got_far, *down.got)
        got_near = swap_heads(send_near, 1)
        mix.groups = [[], [mix.view(keep_far), mix.view(got_far)]]
        down.deliver(got_d)
        grad_hidden1, *sends = tie(grad_hidden1, *down.prepare(add_pieces), *mix.prepare(add_pieces))
        down.launch(sends[:1])
        mix.launch(sends[1:])
        groups = 4 * PIECES
        last_pieces = shape(2, PIECES, unit + GROUP, width, dtype=BF)
        patches_grad, slot_rows, keep_q, send_q = call(
            embed_back_kernel,
            (
                where, segments, labels, grad_hidden1, total_near, hidden0, ln1_gain, patches_t,
                direct, w_in, grad_w_out, gdown, gup, gpre, gq_near, gq_far,
            ),
            [SMEM, SMEM, SMEM] + [VMEM] * 13,
            (shape(channels, tokens), shape(row_count * slot_count, width + 128), last_pieces, last_pieces),
            (VMEM, VMEM, HBM, HBM),
            [
                pltpu.VMEM((tokens, width), F32),
                pltpu.VMEM((tokens, width), BF),
                pltpu.VMEM((EXTRA, width), F32),
                pltpu.VMEM((groups * GROUP, width), BF),
                dma((2, groups)),
            ],
            length=length,
            quarter=quarter,
        )
        patches_grad, send_q, *got_u = tie(patches_grad, send_q, *up.got)
        patches_grad, got_near, *got_d = tie(patches_grad, got_near, *down.got)
        last.groups = [[last.view(keep_q), last.view(swap_heads(send_q, 1))]]
        mix.groups[0] = [mix.view(keep_near), mix.view(got_near)]
        down.got, up.got = got_d, got_u
        gathered = slot_rows.astype(BF)
        gathers = [("rows", 1 << level) for level in reversed(range(levels))]
        gathers += [("heads", 2), ("heads", 1)]
        share = (len(gathers) - 1) // 4
        token = got_d[0]
        pending = {0, 1, 2}
        heads_left = [2, 1]
        got = None
        small = None
        for index in TAIL:
            if index == 4:
                more = gathers[:share] if len(gathers) > 2 + share else gathers[:1]
                for axis, bit in more:
                    gathers.pop(0)
                    if got is not None:
                        gathered = jnp.concatenate([gathered, ordered(got, token)], 0)
                    token = gathered = ordered(gathered, token)
                    got = (swap_rows if axis == "rows" else swap_heads)(gathered, bit)
                continue
            if index == 5:
                if small is None:
                    last.deliver([ordered(more, token) for more in last.got])
                    axis = Chain.axes[[a for a in last.order if a != "y"][0]] - 1
                    small = jnp.concatenate([last.low[:, :, unit:], last.high[:, :, unit:]], axis)
                    small = small.reshape(1, PIECES, GROUP, width)
                token = small = ordered(small, token)
                small_got = swap_heads(small, heads_left.pop(0))
                small = jnp.concatenate([small, small_got], 0)
                continue
            chain = chains[index]
            if index in pending:
                chain.deliver([ordered(one, token) for one in chain.got])
            pending.add(index)
            sends = []
            for send in chain.prepare():
                token = ordered(send, token)
                sends.append(token)
            chain.launch(sends)
        gathered = jnp.concatenate([gathered, got], 0)
        for axis, bit in gathers:
            swap = swap_rows if axis == "rows" else swap_heads
            gathered = jnp.concatenate([gathered, swap(gathered, bit)], 0)
        for chain in chains[:3]:
            chain.deliver(chain.got)
        gathered = gathered.reshape(-1, width + 128)
        digits = gathered[:, width : width + 2].astype(jnp.int32)
        slot_label = digits[:, 0] * 32 + digits[:, 1]
        label_onehot = (
            lax.broadcasted_iota(jnp.int32, (classes, 1), 0) == slot_label[None, :]
        ).astype(BF)
        sum_cls = nn(label_onehot, gathered[:, :width])

        def place(chain):
            return call(
                place_kernel, (where, chain.low, chain.high), [SMEM, VMEM, VMEM], shape(width, width), VMEM
            )

        sum_down, sum_up = place(down), place(up)
        units = shape(part, width)
        line = shape(1, width)
        sum_k, sum_v, sum_o, sum_q, sum_w_in, sum_w_out, sum_pos, *lines = call(
            place_last_kernel,
            (where, mix.low, mix.high, last.low, last.high, small),
            [SMEM] + [VMEM] * 5,
            (units,) * 4
            + (shape(channels, width), shape(2 * channels, width), shape(length, width))
            + (line,) * 7
            + (shape(1, 2 * channels),),
            (VMEM,) * 15,
            [pltpu.VMEM((groups * GROUP, width), F32)],
        )
        sum_b_in, sum_gain1, sum_bias1, sum_gain2, sum_bias2, sum_b_down, sum_b_up, sum_b_out = lines
        return (
            latents.T,
            logdet.reshape(tokens),
            patches_grad.T,
            stats[0, :row_count],
            stats[1, :row_count],
            sum_w_in,
            sum_b_in.reshape(width),
            sum_pos,
            sum_cls,
            sum_gain1,
            sum_bias1,
            sum_q.T[None],
            sum_k.T[None],
            sum_v.T[None],
            sum_o[None],
            sum_gain2,
            sum_bias2,
            sum_up[None],
            sum_b_up,
            sum_down[None],
            sum_b_down,
            sum_w_out.T,
            sum_b_out.reshape(2 * channels),
        )

    return program


def solution(mesh):
    tokens = P(("rows", "heads"))
    tokens2 = P(("rows", "heads"), None)
    last = P(None, None, "heads")
    middle = P(None, "heads", None)
    in_specs = (
        (tokens2, P("rows"), tokens2)
        + (P(),) * 6
        + (last, last, last, middle)
        + (P(), P(), last, P(None, "heads"), middle, P(), P(), P())
        + (tokens2, tokens)
    )
    out_specs = (
        (tokens2, tokens, tokens2, tokens, tokens)
        + (P(),) * 6
        + (last, last, last, middle)
        + (P(), P(), last, P(None, "heads"), middle, P(), P(), P())
    )
    program = make_program(mesh.shape["rows"], mesh.shape["heads"])
    return jax.shard_map(
        program, mesh=mesh, in_specs=in_specs, out_specs=out_specs, check_vma=False
    )
```

```python
import functools

import jax
import jax.numpy as jnp
from jax import lax
from jax.experimental import pallas as pl
from jax.experimental.pallas import tpu as pltpu
from jax.sharding import PartitionSpec as P

HEAD_DIM = 64
EPSILON = 1e-05
SCALE = HEAD_DIM**-0.5
BF = jnp.bfloat16
F32 = jnp.float32
PIECES = 4
EXTRA = 16
GROUP = 32
CHUNK = 64
GATHER_ROWS = 32
CHAIN_ORDERS = ("yxz", "zxy", "yxz", "zyx")
TAIL = (1, 3, 4, 0, 1, 3, 2, 4, 1, 3, 2, 3, 0, 2, 4, 3, 1, 4, 3, 0, 4, 2, 5, 1, 2, 5)

VMEM = pl.BlockSpec(memory_space=pltpu.VMEM)
SMEM = pl.BlockSpec(memory_space=pltpu.SMEM)
HBM = pl.BlockSpec(memory_space=pl.ANY)


def nn(matrix, other):
    return lax.dot_general(matrix, other, (((1,), (0,)), ((), ())), preferred_element_type=F32)


def tn(matrix, other):
    return lax.dot_general(matrix, other, (((0,), (0,)), ((), ())), preferred_element_type=F32)


def nt(matrix, other):
    return lax.dot_general(matrix, other, (((1,), (1,)), ((), ())), preferred_element_type=F32)


def norm_parts(values):
    average = jnp.mean(values, -1, keepdims=True)
    centered = values - average
    spread = jnp.mean(centered * centered, -1, keepdims=True)
    rstd = lax.rsqrt(spread + EPSILON)
    return centered * rstd, rstd


def norm_back(grad, gain, xhat, rstd):
    scaled = grad * gain
    back = scaled - jnp.mean(scaled, -1, keepdims=True)
    back = back - xhat * jnp.mean(scaled * xhat, -1, keepdims=True)
    return rstd * back


def column_sum(values):
    return jnp.sum(values, 0, keepdims=True)


def over_rows(tokens, body):
    def step(index, carry):
        body(pl.ds(pl.multiple_of(index * CHUNK, CHUNK), CHUNK))
        return carry

    lax.fori_loop(0, tokens // CHUNK, step, 0)


def gelu_pair(values):
    scaled = jnp.abs(values) * 0.7071067811865476
    base = 1.0 + 0.3275911 * scaled
    t = pl.reciprocal(base, approx=True)
    t = t * (2.0 - base * t)
    bell = jnp.exp(-0.5 * values * values)
    poly = 1.061405429 * t - 1.453152027
    poly = poly * t + 1.421413741
    poly = poly * t - 0.284496736
    poly = poly * t + 0.254829592
    tail = 0.5 * poly * t * bell
    below = jnp.where(values >= 0.0, 1.0 - tail, tail)
    return values * below, below + values * bell * 0.3989422804014327


def packed_flag(where_ref, seg_ref, row, length):
    start = where_ref[0] + row * length
    return seg_ref[start + length - 1] > 0


def embed_kernel(
    where_ref, seg_ref, patch_ref, w_ref, b_ref, pos_ref, cls_ref, gain_ref, bias_ref, hid_ref, norm_ref
):
    tokens, width = hid_ref.shape
    length = pos_ref.shape[0]
    slots = cls_ref.shape[0] // (tokens // length)
    quarter = length // slots
    hid_ref[...] = tn(patch_ref[...].astype(BF), w_ref[...]) + b_ref[...]
    for row in range(tokens // length):
        packed = packed_flag(where_ref, seg_ref, row, length)
        for slot in range(slots):
            at = slice(row * length + slot * quarter, row * length + (slot + 1) * quarter)
            here = pos_ref[slot * quarter : (slot + 1) * quarter].astype(F32)
            first = pos_ref[:quarter].astype(F32)
            one = cls_ref[row * slots + slot : row * slots + slot + 1]
            start = cls_ref[row * slots : row * slots + 1]
            value = hid_ref[at] + jnp.where(packed, first, here) + jnp.where(packed, one, start)
            hid_ref[at] = value
            xhat, _ = norm_parts(value)
            norm_ref[at] = (xhat * gain_ref[...] + bias_ref[...]).astype(BF)


def fetch_near(parts, weight_ref, sems):
    unit = weight_ref.shape[1] // 2
    copies = []
    for slot, ref in enumerate(parts):
        for half in range(2):
            for u in range(2):
                source = ref.at[half, pl.ds(unit * u, unit)]
                copies.append((source, weight_ref.at[2 * half + u, pl.ds(unit * slot, unit)]))
    return start_copies(copies, sems)


def fetch_far(where_ref, parts, weight_ref, sems):
    far, far_other, cross, cross_other = parts
    unit = weight_ref.shape[1] // 2
    x = where_ref[1]
    copies = []
    for slot, ref, half in ((0, far, x), (0, far_other, 1 - x), (1, cross, x), (1, cross_other, 1 - x)):
        for u in range(2):
            source = ref.at[pl.ds(unit * u, unit)]
            copies.append((source, weight_ref.at[2 * half + u, pl.ds(unit * slot, unit)]))
    return start_copies(copies, sems)


def fetch_half(where_ref, parts, weight_ref, sems):
    if len(parts) == 2:
        return fetch_near(parts, weight_ref, sems)
    return fetch_far(where_ref, parts, weight_ref, sems)


def start_copies(copies, sems):
    made = [pltpu.make_async_copy(src, dst, sems.at[i]) for i, (src, dst) in enumerate(copies)]
    for copy in made:
        copy.start()
    return made


def fetch_full(where_ref, parts, weight_ref, sems):
    own, near, far, far_other, cross, cross_other = parts
    half = weight_ref.shape[1] // 2
    mine = pl.ds(pl.multiple_of(where_ref[1] * half, half), half)
    other = pl.ds(pl.multiple_of((1 - where_ref[1]) * half, half), half)
    copies = [
        (own, weight_ref.at[0], 0),
        (near, weight_ref.at[1], 1),
        (far, weight_ref.at[2, mine], 2),
        (far_other, weight_ref.at[2, other], 2),
        (cross, weight_ref.at[3, mine], 3),
        (cross_other, weight_ref.at[3, other], 3),
    ]
    for source, target, slot in copies:
        pltpu.make_async_copy(source, target, sems.at[slot]).start()


def wait_slot(source, into_ref, sems, slot):
    pltpu.make_async_copy(source, into_ref.at[slot], sems.at[slot]).wait()


def mask_bias(packed, quarter, length):
    q = lax.broadcasted_iota(jnp.int32, (length, length), 1)
    k = lax.broadcasted_iota(jnp.int32, (length, length), 0)
    shift = quarter.bit_length() - 1
    same = (q >> shift) == (k >> shift)
    return jnp.where((k <= q) & (same | jnp.logical_not(packed)), 0.0, -1e30)


def head_lanes(value):
    lane = lax.broadcasted_iota(jnp.int32, (1, 128), 1)
    return [jnp.where(side, value, 0.0).astype(BF) for side in (lane < HEAD_DIM, lane >= HEAD_DIM)]


def attend_kernel(where_ref, seg_ref, hid_ref, norm_ref, *rest, length, quarter, count):
    parts = rest[:count]
    q_ref, k_ref, v_ref, prob_ref, att_ref, out_ref, weight_ref, bias_ref, sems = rest[count:]
    tokens = hid_ref.shape[0]
    copies = fetch_half(where_ref, parts, weight_ref, sems)
    for row in range(tokens // length):
        bias_ref[row] = mask_bias(packed_flag(where_ref, seg_ref, row, length), quarter, length)
    for copy in copies:
        copy.wait()
    q_ref[...] = nt(norm_ref[...], weight_ref[0]).astype(BF)
    k_ref[...] = nt(norm_ref[...], weight_ref[1]).astype(BF)
    v_ref[...] = nt(norm_ref[...], weight_ref[2]).astype(BF)
    pairs = q_ref.shape[1] // 128
    lefts = head_lanes(1.0)
    scaled = head_lanes(SCALE)
    block = length // 2

    def step(index, carry):
        row = index // pairs
        pair = index % pairs
        lanes = pl.ds(pl.multiple_of(pair * 128, 128), 128)
        for part in range(2):
            keys = (part + 1) * block
            here = pl.ds(pl.multiple_of(row * length + part * block, block), block)
            upto = pl.ds(pl.multiple_of(row * length, length), keys)
            bias = bias_ref[row, :keys, part * block : (part + 1) * block]
            queries = q_ref[here, lanes]
            key_rows = k_ref[upto, lanes]
            values = v_ref[upto, lanes]
            result = None
            for head in range(2):
                scores = nt(key_rows, queries * scaled[head]) + bias
                top = jnp.max(scores, 0, keepdims=True)
                grown = jnp.exp(scores - top)
                probs = (grown * (1.0 / jnp.sum(grown, 0, keepdims=True))).astype(BF)
                prob_ref[2 * index + head, :keys, part * block : (part + 1) * block] = probs
                term = tn(probs, values * lefts[head])
                result = term if result is None else result + term
            att_ref[here, lanes] = result.astype(BF)
        return carry

    lax.fori_loop(0, tokens // length * pairs, step, 0)
    out_ref[...] = hid_ref[...] + nn(att_ref[...], weight_ref[3])


def up_kernel(
    where_ref, hid_ref, gain_ref, bias_ref, own, near, far, far_other, cross, cross_other,
    own_t, near_t, far_t, cross_t,
    norm_ref, act_out, slope_out, weight_ref, bup_ref, act_ref, slope_ref, sems, bias_sems, out_sems,
):
    tokens, width = hid_ref.shape
    fetch_full(where_ref, (own, near, far, far_other, cross, cross_other), weight_ref, sems)
    last = pl.ds(far_t.shape[0] - EXTRA, EXTRA)
    packs = (own_t.at[0, last], near_t.at[0, last], far_t.at[last], cross_t.at[last])
    biases = start_copies([(pack, bup_ref.at[slot]) for slot, pack in enumerate(packs)], bias_sems)

    def normalize(at):
        xhat, _ = norm_parts(hid_ref[at])
        norm_ref[at] = (xhat * gain_ref[...] + bias_ref[...]).astype(BF)

    over_rows(tokens, normalize)
    for bias in biases:
        bias.wait()
    block = 128

    def step(slot, carry):
        wait_slot(own, weight_ref, sems, slot)
        bias = bup_ref[slot, :1].astype(F32)
        for first in range(0, tokens, block):
            at = slice(first, first + block)
            pre = nn(norm_ref[at], weight_ref[slot]) + bias
            value, slope = gelu_pair(pre)
            act_ref[slot, at] = value.astype(BF)
            slope_ref[slot, at] = slope.astype(BF)
        pltpu.make_async_copy(act_ref.at[slot], act_out.at[slot], out_sems.at[0, slot]).start()
        pltpu.make_async_copy(slope_ref.at[slot], slope_out.at[slot], out_sems.at[1, slot]).start()
        return carry

    lax.fori_loop(0, 4, step, 0)
    for slot in range(4):
        pltpu.make_async_copy(act_ref.at[slot], act_out.at[slot], out_sems.at[0, slot]).wait()
        pltpu.make_async_copy(slope_ref.at[slot], slope_out.at[slot], out_sems.at[1, slot]).wait()


def send_pieces(where_ref, stage_ref, slot, keep, sends, sems, rows):
    for piece in range(PIECES):
        source = stage_ref.at[piece * rows : (piece + 1) * rows]
        target = piece ^ where_ref[2]

        @pl.when(slot % 2 == 0)
        def _():
            pltpu.make_async_copy(source, keep.at[slot // 2, target], sems.at[piece]).start()

        for index, send in enumerate(sends):

            @pl.when(slot == 2 * index + 1)
            def _():
                pltpu.make_async_copy(source, send.at[target], sems.at[piece]).start()


def wait_pieces(stage_ref, keep, sems, rows):
    for piece in range(PIECES):
        source = stage_ref.at[piece * rows : (piece + 1) * rows]
        pltpu.make_async_copy(source, keep.at[0, 0, :rows], sems.at[piece]).wait()


def down_kernel(
    where_ref, seg_ref, hid_ref, act_in, bdown_ref, wout_ref, bout_ref, patch_ref, lgrad_ref, dgrad_ref,
    own, near, far, far_other, cross, cross_other,
    latent_ref, logdet_ref, mean_ref, max_ref, direct_ref, grad_ref, gwout_ref, gvec_ref, keep_ref, send_near, send_far,
    weight_ref, act_ref, total_ref, branch_ref, stage_ref, sems, act_sems, out_sems,
    *, length, quarter,
):
    tokens, width = hid_ref.shape
    channels = patch_ref.shape[0]
    send_refs = (send_near, send_far)
    start_copies([(act_in.at[slot], act_ref.at[slot]) for slot in range(4)], act_sems)
    fetch_full(where_ref, (own, near, far, far_other, cross, cross_other), weight_ref, sems)
    total_ref[...] = hid_ref[...] + bdown_ref[...]

    def gather(slot, carry):
        wait_slot(act_in.at[slot], act_ref, act_sems, slot)
        wait_slot(own, weight_ref, sems, slot)
        total_ref[...] += nn(act_ref[slot], weight_ref[slot])
        return carry

    lax.fori_loop(0, 4, gather, 0)
    top_low = total_ref[...].astype(BF)
    head_out = nt(wout_ref[...], top_low) + bout_ref[...]
    token = lax.broadcasted_iota(jnp.int32, (1, tokens), 1)
    row_count = tokens // length
    starts = jnp.zeros((1, tokens), jnp.bool_)
    for row in range(row_count):
        packed = packed_flag(where_ref, seg_ref, row, length)
        inside = (token >= row * length) & (token < (row + 1) * length)
        fresh = (token & jnp.where(packed, quarter - 1, length - 1)) == 0
        starts = starts | (inside & fresh)
    previous = jnp.where(starts, 0.0, pltpu.roll(head_out, 1, 1))
    shifts = previous[:channels]
    logscale = previous[channels:]
    shrink = jnp.exp(-logscale)
    latents = (patch_ref[...] - shifts) * shrink
    latent_ref[...] = latents
    logdet_ref[...] = -column_sum(logscale)
    lane = lax.broadcasted_iota(jnp.int32, mean_ref.shape, 1)
    means = jnp.zeros(mean_ref.shape, F32)
    tops = means
    for row in range(row_count):
        part = logscale[:, row * length : (row + 1) * length]
        means = jnp.where(lane == row, jnp.sum(part) * (1.0 / (length * channels)), means)
        tops = jnp.where(lane == row, jnp.max(part), tops)
    mean_ref[...] = means
    max_ref[...] = tops
    lgrad = lgrad_ref[...]
    direct = lgrad * shrink
    direct_ref[...] = direct
    grad_prev = jnp.concatenate([-direct, -lgrad * latents - dgrad_ref[...]], 0)
    grad_prev = jnp.where(starts, 0.0, grad_prev)
    grad_head = pltpu.roll(grad_prev, tokens - 1, 1).astype(BF)
    gwout_ref[...] = nn(grad_head, top_low)
    grad_hidden = tn(grad_head, wout_ref[...])
    grad_ref[...] = grad_hidden
    branch_ref[...] = grad_hidden.astype(BF)
    gvec_ref[...] = jnp.zeros(gvec_ref.shape, F32)
    gvec_ref[0:1, :] = column_sum(grad_hidden)
    row_of = nt(jnp.ones((8, tokens), BF), grad_head)
    gvec_ref[1:2, : 2 * channels] = row_of[:1]
    rows = width // PIECES


    def step(slot, carry):
        @pl.when(slot >= 2)
        def _():
            wait_pieces(stage_ref.at[slot % 2], keep_ref, out_sems.at[slot % 2], rows)

        stage_ref[slot % 2] = tn(act_ref[slot], branch_ref[...]).astype(BF)
        send_pieces(where_ref, stage_ref.at[slot % 2], slot, keep_ref, send_refs, out_sems.at[slot % 2], rows)
        return carry

    lax.fori_loop(0, 4, step, 0)
    for slot in range(2):
        wait_pieces(stage_ref.at[slot], keep_ref, out_sems.at[slot], rows)


def grad_pre_kernel(
    where_ref, grad_ref, slope_in, own, near, far, far_other, cross, cross_other,
    pre_out, sum_ref, weight_ref, slope_ref, branch_ref, pre_ref, sems, slope_sems, out_sems,
):
    start_copies([(slope_in.at[slot], slope_ref.at[slot]) for slot in range(4)], slope_sems)
    fetch_full(where_ref, (own, near, far, far_other, cross, cross_other), weight_ref, sems)
    branch_ref[...] = grad_ref[...].astype(BF)

    def step(slot, carry):
        wait_slot(slope_in.at[slot], slope_ref, slope_sems, slot)
        wait_slot(own, weight_ref, sems, slot)
        grad_pre = (nt(branch_ref[...], weight_ref[slot]) * slope_ref[slot].astype(F32)).astype(BF)
        pre_ref[slot] = grad_pre
        pltpu.make_async_copy(pre_ref.at[slot], pre_out.at[slot], out_sems.at[slot]).start()
        sum_ref[pl.ds(slot, 1), :] = column_sum(grad_pre.astype(F32))
        return carry

    lax.fori_loop(0, 4, step, 0)
    for slot in range(4):
        pltpu.make_async_copy(pre_ref.at[slot], pre_out.at[slot], out_sems.at[slot]).wait()


def up_back_kernel(
    where_ref, grad_ref, pre_in, norm_ref, hid_ref, gain_ref, own, near, far, far_other, cross, cross_other,
    gout_ref, mix_ref, gvec_ref, keep_ref, send_near, send_far,
    weight_ref, pre_ref, total_ref, stage_ref, sems, pre_sems, out_sems,
):
    tokens, width = grad_ref.shape
    send_refs = (send_near, send_far)
    start_copies([(pre_in.at[slot], pre_ref.at[slot]) for slot in range(4)], pre_sems)
    total_ref[...] = jnp.zeros(total_ref.shape, F32)
    fetch_full(where_ref, (own, near, far, far_other, cross, cross_other), weight_ref, sems)
    gvec_ref[...] = jnp.zeros(gvec_ref.shape, F32)
    rows = width // PIECES

    def step(slot, carry):
        @pl.when(slot >= 2)
        def _():
            wait_pieces(stage_ref.at[slot % 2], keep_ref, out_sems.at[slot % 2], rows)

        wait_slot(pre_in.at[slot], pre_ref, pre_sems, slot)
        wait_slot(own, weight_ref, sems, slot)
        stage_ref[slot % 2] = tn(norm_ref[...], pre_ref[slot]).astype(BF)
        send_pieces(where_ref, stage_ref.at[slot % 2], slot, keep_ref, send_refs, out_sems.at[slot % 2], rows)
        total_ref[...] += nt(pre_ref[slot], weight_ref[slot])
        return carry

    lax.fori_loop(0, 4, step, 0)

    def finish(at):
        xhat, rstd = norm_parts(hid_ref[at])
        grad = total_ref[at]
        value = grad_ref[at] + norm_back(grad, gain_ref[...], xhat, rstd)
        gout_ref[at] = value
        mix_ref[at] = value.astype(BF)
        gvec_ref[0:1, :] += column_sum(grad * xhat)
        gvec_ref[1:2, :] += column_sum(grad)

    over_rows(tokens, finish)
    for slot in range(2):
        wait_pieces(stage_ref.at[slot], keep_ref, out_sems.at[slot], rows)


def attend_back_kernel(
    where_ref, mix_ref, q_ref, k_ref, v_ref, prob_ref, att_ref, norm_ref, *rest, length, quarter, count, chained
):
    before_ref = rest[0] if chained else None
    rest = rest[1:] if chained else rest
    parts = rest[:count]
    (
        total_ref, gq_ref, keep_ref, send_ref,
        weight_ref, gatt_ref, dq_ref, dk_ref, dv_ref, stage_ref, sems, out_sems,
    ) = rest[count:]
    tokens = mix_ref.shape[0]
    for copy in fetch_half(where_ref, parts, weight_ref, sems):
        copy.wait()
    gatt_ref[...] = nt(mix_ref[...], weight_ref[3]).astype(BF)
    pairs = q_ref.shape[1] // 128
    lefts = head_lanes(1.0)
    scaled = head_lanes(SCALE)
    block = length // 2
    unit = weight_ref.shape[1] // 2
    rows = unit // PIECES

    def publish(kind, left, right):
        stage_ref[kind] = tn(left, right).astype(BF)
        for slot, into in enumerate((keep_ref, send_ref)):
            for piece in range(PIECES):
                at = slot * unit + piece * rows
                pltpu.make_async_copy(
                    stage_ref.at[kind, at : at + rows],
                    into.at[piece ^ where_ref[2], kind * rows : (kind + 1) * rows],
                    out_sems.at[kind, slot * PIECES + piece],
                ).start()

    publish(2, att_ref[...], mix_ref[...])

    def step(index, carry):
        row = index // pairs
        pair = index % pairs
        lanes = pl.ds(pl.multiple_of(pair * 128, 128), 128)
        grads_k = [None, None]
        grads_v = [None, None]
        for part in range(2):
            keys = (part + 1) * block
            here = pl.ds(pl.multiple_of(row * length + part * block, block), block)
            upto = pl.ds(pl.multiple_of(row * length, length), keys)
            queries = q_ref[here, lanes]
            key_rows = k_ref[upto, lanes]
            values = v_ref[upto, lanes]
            grad_out = gatt_ref[here, lanes]
            result = None
            for head in range(2):
                probs = prob_ref[2 * index + head, :keys, part * block : (part + 1) * block]
                wide = probs.astype(F32)
                grad_mine = grad_out * lefts[head]
                grad_probs = nt(values, grad_mine)
                inner = jnp.sum(wide * grad_probs, 0, keepdims=True)
                grad_scores = (wide * (grad_probs - inner)).astype(BF)
                term = tn(grad_scores, key_rows * scaled[head])
                result = term if result is None else result + term
                term_k = nn(grad_scores, queries * scaled[head])
                term_v = nn(probs, grad_mine)
                grads_k[part] = term_k if grads_k[part] is None else grads_k[part] + term_k
                grads_v[part] = term_v if grads_v[part] is None else grads_v[part] + term_v
            dq_ref[here, lanes] = result.astype(BF)
        low = pl.ds(pl.multiple_of(row * length, length), block)
        high = pl.ds(pl.multiple_of(row * length + block, block), block)
        dk_ref[low, lanes] = (grads_k[0] + grads_k[1][:block]).astype(BF)
        dk_ref[high, lanes] = grads_k[1][block:].astype(BF)
        dv_ref[low, lanes] = (grads_v[0] + grads_v[1][:block]).astype(BF)
        dv_ref[high, lanes] = grads_v[1][block:].astype(BF)
        return carry

    lax.fori_loop(0, tokens // length * pairs, step, 0)
    publish(0, dk_ref[...], norm_ref[...])
    publish(1, dv_ref[...], norm_ref[...])
    gq_ref[...] = tn(dq_ref[...], norm_ref[...]).astype(BF)
    total = nn(dq_ref[...], weight_ref[0]) + nn(dk_ref[...], weight_ref[1]) + nn(dv_ref[...], weight_ref[2])
    if chained:
        total = total + before_ref[...]
    total_ref[...] = total
    for kind in range(3):
        for piece in range(2 * PIECES):
            pltpu.make_async_copy(
                stage_ref.at[kind, :rows], keep_ref.at[0, :rows], out_sems.at[kind, piece]
            ).wait()


def embed_back_kernel(
    where_ref, seg_ref, label_ref, grad_ref, total_ref, hid_ref, gain_ref, patch_ref, direct_ref, win_ref,
    gwout_ref, gdown_ref, gup_ref, gpre_ref, gq_near, gq_far,
    pgrad_ref, slot_ref, keep_ref, send_ref,
    value_ref, embed_ref, acc_ref, small_ref, sems,
    *, length, quarter,
):
    tokens, width = hid_ref.shape
    channels = patch_ref.shape[0]
    unit = width // 4
    rows = unit // PIECES
    sources = []
    for slot in range(4):
        source = (gq_near, gq_far)[slot // 2]
        into = (keep_ref, send_ref)[slot % 2]
        for piece in range(PIECES):
            at = (slot % 2) * unit + piece * rows
            sources.append((source.at[at : at + rows], into.at[slot // 2, piece ^ where_ref[2], :rows]))
    copies = start_copies(sources, sems.at[0])
    acc_ref[...] = jnp.zeros(acc_ref.shape, F32)

    def finish(at):
        xhat, rstd = norm_parts(hid_ref[at])
        grad = total_ref[at]
        acc_ref[1:2, :] += column_sum(grad * xhat)
        acc_ref[2:3, :] += column_sum(grad)
        value = grad_ref[at] + norm_back(grad, gain_ref[...], xhat, rstd)
        value_ref[at] = value
        embed = value.astype(BF)
        embed_ref[at] = embed
        acc_ref[0:1, :] += column_sum(embed.astype(F32))

    over_rows(tokens, finish)
    acc_ref[3:5, :] = gup_ref[0:2, :]
    acc_ref[5:7, :] = gdown_ref[0:2, :]
    for slot in range(4):
        acc_ref[pl.ds(7 + (slot ^ where_ref[3]), 1), :] = gpre_ref[slot : slot + 1, :]
    small_ref[:channels] = nn(patch_ref[...].astype(BF), embed_ref[...]).astype(BF)
    small_ref[channels : 3 * channels] = gwout_ref[...].astype(BF)
    first = 3 * channels
    rows_here = tokens // length
    slots = length // quarter
    packed = [packed_flag(where_ref, seg_ref, row, length) for row in range(rows_here)]
    zero = jnp.zeros((quarter, width), F32)
    for slot in range(slots):
        value = zero
        for row in range(rows_here):
            at = row * length + slot * quarter
            here = value_ref[at : at + quarter]
            value = value + jnp.where(packed[row], 0.0, here)
            if slot == 0:
                every = here
                for later in range(1, slots):
                    every = every + value_ref[at + later * quarter : at + (later + 1) * quarter]
                value = value + jnp.where(packed[row], every, 0.0)
        small_ref[first + slot * quarter : first + (slot + 1) * quarter] = value.astype(BF)
    start = first + length
    small_ref[start : start + EXTRA] = acc_ref[...].astype(BF)
    start += EXTRA
    small_ref[start:] = jnp.zeros((small_ref.shape[0] - start, width), BF)
    moved = []
    for block in range(4):
        slot = block ^ where_ref[3]
        for piece in range(PIECES):
            at = (block * PIECES + piece) * GROUP
            moved.append((slot, piece ^ where_ref[2], small_ref.at[at : at + GROUP]))
    for index, (slot, piece, source) in enumerate(moved):

        @pl.when(slot % 2 == 0)
        def _():
            into = keep_ref.at[slot // 2, piece, rows:]
            pltpu.make_async_copy(source, into, sems.at[1, index]).start()

        @pl.when(slot % 2 == 1)
        def _():
            into = send_ref.at[slot // 2, piece, rows:]
            pltpu.make_async_copy(source, into, sems.at[1, index]).start()

    lane = lax.broadcasted_iota(jnp.int32, (1, slot_ref.shape[1] - width), 1)
    for row in range(rows_here):
        sums = []
        for slot in range(slots):
            at = row * length + slot * quarter
            sums.append(column_sum(value_ref[at : at + quarter]))
        every = sums[0]
        for slot in range(1, slots):
            every = every + sums[slot]
        for slot in range(slots):
            other = every if slot == 0 else jnp.zeros_like(every)
            index = row * slots + slot
            slot_ref[index : index + 1, :width] = jnp.where(packed[row], sums[slot], other)
            label = label_ref[row, slot]
            digits = jnp.where(lane == 0, label >> 5, jnp.where(lane == 1, label & 31, 0))
            slot_ref[index : index + 1, width:] = digits.astype(F32)
    pgrad_ref[...] = direct_ref[...] + nt(win_ref[...], embed_ref[...])
    for copy in copies:
        copy.wait()
    for index in range(4 * PIECES):
        pltpu.make_async_copy(
            small_ref.at[:GROUP], keep_ref.at[0, 0, rows:], sems.at[1, index]
        ).wait()


def add_kernel(*refs, counts):
    sources, outs = refs[: sum(counts)], refs[sum(counts) :]
    for count, out_ref in zip(counts, outs):
        total = sources[0][...].astype(F32)
        for ref in sources[1:count]:
            total = total + ref[...].astype(F32)
        out_ref[...] = total.astype(BF)
        sources = sources[count:]


def piece_list(low, high):
    found = []
    for bit, ref in ((0, low), (1, high)):
        for i in range(ref.shape[0]):
            for j in range(ref.shape[1]):
                found.append((ref, i, j, i + (bit if low.shape[0] == 1 else 0), j + (bit if low.shape[1] == 1 else 0)))
    return [(ref, i, j, 2 * x + z) for ref, i, j, x, z in found]


def place_kernel(where_ref, low_in, high_in, out, low_ref, high_ref, stage_ref, in_sems, out_sems):
    rows = low_ref.shape[2]
    start_copies([(low_in, low_ref), (high_in, high_ref)], in_sems)
    pltpu.make_async_copy(low_in, low_ref, in_sems.at[0]).wait()
    pieces = piece_list(low_ref, high_ref)
    copies = []
    for index, (ref, i, j, piece) in enumerate(pieces):
        if index == 2:
            pltpu.make_async_copy(high_in, high_ref, in_sems.at[1]).wait()
        stage_ref[index] = ref[i, j].astype(F32)
        at = pl.ds(pl.multiple_of((piece ^ where_ref[2]) * rows, rows), rows)
        copies.append(pltpu.make_async_copy(stage_ref.at[index], out.at[at], out_sems.at[index]))
        copies[-1].start()
    for copy in copies:
        copy.wait()


def place_last_kernel(
    where_ref, mix_low, mix_high, low_ref, high_ref, all_ref, cross_ref,
    gk_ref, gv_ref, go_ref, gq_ref, gin_ref, gout_ref, gpos_ref, gbin_ref, *rest,
):
    *vectors, bup_ref, bout_ref, flat_ref = rest
    rows = gq_ref.shape[0] // PIECES
    for ref, i, j, piece in piece_list(mix_low, mix_high):
        at = pl.ds(pl.multiple_of((piece ^ where_ref[2]) * rows, rows), rows)
        gk_ref[at] = ref[i, j, :rows].astype(F32)
        gv_ref[at] = ref[i, j, rows : 2 * rows].astype(F32)
        go_ref[at] = ref[i, j, 2 * rows :].astype(F32)
    for ref, i, j, piece in piece_list(low_ref, high_ref):
        at = pl.ds(pl.multiple_of((piece ^ where_ref[2]) * rows, rows), rows)
        gq_ref[at] = ref[i, j, :rows].astype(F32)
    channels = gin_ref.shape[0]
    for core, ref in enumerate((all_ref, cross_ref)):
        for far in range(2):
            for piece in range(PIECES):
                head = (2 * far + core) ^ where_ref[3]
                group = head * PIECES + (piece ^ where_ref[2])
                flat_ref[pl.ds(pl.multiple_of(group * GROUP, GROUP), GROUP)] = ref[far, piece].astype(F32)
    start = 3 * channels
    gin_ref[...] = flat_ref[:channels]
    gout_ref[...] = flat_ref[channels:start]
    length = gpos_ref.shape[0]
    gpos_ref[...] = flat_ref[start : start + length]
    start += length
    for index in range(gbin_ref.shape[0]):
        gbin_ref[index : index + 1] = flat_ref[start : start + 1, index * 128 : (index + 1) * 128]
    for index, ref in enumerate(vectors):
        ref[...] = flat_ref[start + 1 + index : start + 2 + index]
    bout_ref[...] = flat_ref[start + 6 : start + 7, : bout_ref.shape[1]]
    bup_ref[...] = flat_ref[pl.ds(start + 7 + where_ref[3], 1)]


def make_program(rows_size, heads_size):
    levels = rows_size.bit_length() - 1

    def swap_heads(array, bit):
        return lax.ppermute(array, "heads", [(i, i ^ bit) for i in range(heads_size)])

    def swap_rows(array, bit):
        return lax.ppermute(array, "rows", [(i, i ^ bit) for i in range(rows_size)])

    def add_low(arrays):
        total = arrays[0].astype(F32)
        for other in arrays[1:]:
            total = total + other.astype(F32)
        return total.astype(BF)

    def tie(*values):
        return lax.optimization_barrier(values)

    def ordered(value, token):
        return tie(value, token)[0]

    class View:
        def __init__(self, array, start=(0, 0, 0), size=None):
            self.array, self.start = array, tuple(start)
            self.size = tuple(size or array.shape[:3])

        def narrow(self, axis, index):
            start, size = list(self.start), list(self.size)
            if size[axis] > 1:
                start[axis] += index
            size[axis] = 1
            return View(self.array, start, size)

        def value(self):
            stop = [a + b for a, b in zip(self.start, self.size)] + list(self.array.shape[3:])
            return lax.slice(self.array, self.start + (0, 0), stop)

    def add_views(views):
        return add_low([view.value() for view in views])

    class Chain:
        axes = {"y": 0, "x": 1, "z": 2}

        def __init__(self, order):
            self.order = order
            self.groups = []
            self.left = list(order) + ["w"] + [a for a in reversed(order) if a != "y"]

        def view(self, array):
            return View(array.reshape((-1, 2, 2) + array.shape[-2:]))

        def parts(self):
            kind = self.left[0]
            if kind == "y":
                return [[view.narrow(0, 1) for view in self.groups[-1]]]
            if "w" in self.left[1:]:
                axis = self.axes[kind]
                return [[view.narrow(axis, 1) for view in group] for group in self.groups]
            return [self.groups[0]]

        def prepare(self):
            if "w" in self.left:
                return [add_views(part) for part in self.parts()]
            return [self.total]

        def launch(self, sends):
            self.sends = sends
            kind = self.left[0]
            if kind == "y":
                self.got = [swap_heads(send, 2) for send in sends]
            else:
                self.got = [swap_rows(send, 1 << "xzw".index(kind)) for send in sends]

        def deliver(self, got):
            kind = self.left.pop(0)
            if kind == "w":
                self.total = add_low([self.sends[0], got[0]])
                for level in range(3, levels):
                    self.total = add_low([self.total, swap_rows(self.total, 1 << level)])
            elif "w" in self.left:
                axis = self.axes[kind]
                if kind == "y":
                    self.groups = self.groups[:1]
                self.groups = [
                    [view.narrow(axis, 0) for view in group] + [View(more)]
                    for group, more in zip(self.groups, got)
                ]
            elif self.left:
                self.total = jnp.concatenate([self.sends[0], got[0]], self.axes[kind])
            else:
                self.low, self.high = self.sends[0][0], got[0][0]

    def program(
        patches, segments, labels, w_in, b_in, pos_table, cls_table, ln1_gain, ln1_bias,
        w_query, w_key, w_value, w_attn_out, ln2_gain, ln2_bias, w_up, b_up, w_down, b_down,
        w_out, b_out, latent_grad, logdet_grad,
    ):
        tokens, channels = patches.shape
        length, width = pos_table.shape
        slot_count = labels.shape[1]
        quarter = length // slot_count
        classes = cls_table.shape[0]
        part = w_query.shape[2]
        row_count = tokens // length
        head_index = lax.axis_index("heads")
        row_index = lax.axis_index("rows")
        row_bit = row_index & 1
        mask = ((row_index & 1) << 1) | ((row_index >> 1) & 1)
        where = jnp.stack([head_index * tokens, row_bit, mask, head_index]).astype(jnp.int32)
        rows = width // PIECES
        unit = part // PIECES
        heads = width // HEAD_DIM
        square = 2 * tokens * width * width

        def shape(*dims, dtype=F32):
            return jax.ShapeDtypeStruct(dims, dtype)

        def call(kernel, operands, specs, outs, out_specs, scratch=(), room=60, **options):
            return pl.pallas_call(
                functools.partial(kernel, **options) if options else kernel,
                in_specs=specs,
                out_specs=out_specs,
                out_shape=outs,
                scratch_shapes=list(scratch),
                compiler_params=pltpu.CompilerParams(vmem_limit_bytes=room << 20),
                cost_estimate=pl.CostEstimate(
                    flops=1, transcendentals=0, bytes_accessed=1
                ),
            )(*operands)

        dma = pltpu.SemaphoreType.DMA
        low = shape(tokens, width, dtype=BF)
        full = shape(tokens, width)
        half_low = shape(tokens, width // 2, dtype=BF)

        bias_rows = jnp.pad(b_up, ((0, EXTRA - 1), (0, 0)))
        pack_t = jnp.stack(
            [
                jnp.concatenate([w_query[0].T, w_key[0].T, bias_rows], 0),
                jnp.concatenate([w_value[0].T, w_attn_out[0], bias_rows], 0),
            ]
        )
        own_u, own_d = w_up[0], w_down[0]
        half_rows = width // 2
        half_t = jnp.concatenate(
            [
                jnp.where(row_bit == 0, w_query[0].T, w_value[0].T),
                jnp.where(row_bit == 0, w_key[0].T, w_attn_out[0]),
                bias_rows,
            ],
            0,
        )
        far_t = swap_heads(half_t, 2)
        near_t = swap_heads(ordered(pack_t, half_t), 1)
        half_u = lax.dynamic_slice_in_dim(own_u, row_bit * half_rows, half_rows, 0)
        half_u, half_t = tie(half_u, half_t)
        far_u = swap_heads(half_u, 2)
        half_d = lax.dynamic_slice_in_dim(own_d, row_bit * half_rows, half_rows, 0)
        half_d, half_u = tie(half_d, half_u)
        far_d = swap_heads(half_d, 2)
        cls_rows = cls_table[labels.reshape(-1)].astype(F32)
        patches_t = patches.T
        hidden0, normed1 = call(
            embed_kernel,
            (
                where, segments, ordered(patches_t, half_d), w_in, b_in[None], pos_table, cls_rows,
                ln1_gain, ln1_bias,
            ),
            [SMEM, SMEM] + [VMEM] * 7,
            (full, low),
            (VMEM, VMEM),
        )
        normed1, far_t = tie(normed1, far_t)
        far_other_t = swap_rows(far_t, 1)
        cross_t = swap_heads(far_t, 1)
        near_u = swap_heads(ordered(own_u, far_t), 1)
        near_d = swap_heads(ordered(own_d, far_t), 1)

        def attend(hidden, normed, parts):
            return call(
                attend_kernel,
                (where, segments, hidden, normed) + parts,
                [SMEM, SMEM, VMEM, VMEM] + [HBM] * len(parts),
                (
                    half_low, half_low, half_low,
                    shape(row_count * heads // 2, length, length, dtype=BF), half_low, full,
                ),
                (VMEM,) * 6,
                [
                    pltpu.VMEM((4, width // 2, width), BF),
                    pltpu.VMEM((row_count, length, length), F32),
                    dma((8,)),
                ],
                length=length,
                quarter=quarter,
                count=len(parts),
            )

        parts_near = (pack_t, near_t)
        *saved_near, mixed = attend(hidden0, normed1, parts_near)
        mixed, far_other_t, far_u = tie(mixed, far_other_t, far_u)
        cross_other_t = swap_heads(far_other_t, 1)
        far_other_u = swap_rows(far_u, 1)
        cross_u = swap_heads(far_u, 1)
        parts_far = (far_t, far_other_t, cross_t, cross_other_t)
        *saved_far, hidden1 = attend(mixed, normed1, parts_far)
        hidden1, far_other_u, far_d = tie(hidden1, far_other_u, far_d)
        cross_other_u = swap_heads(far_other_u, 1)
        far_other_d = swap_rows(far_d, 1)
        cross_d = swap_heads(far_d, 1)
        parts_u = (own_u, near_u, far_u, far_other_u, cross_u, cross_other_u)
        four = shape(heads_size, tokens, width, dtype=BF)
        normed2, activated, slope = call(
            up_kernel,
            (where, hidden1, ln2_gain, ln2_bias)
            + parts_u
            + (pack_t, near_t, far_t, cross_t),
            [SMEM] + [VMEM] * 3 + [HBM] * 10,
            (low, four, four),
            (VMEM, HBM, HBM),
            [
                pltpu.VMEM((heads_size, width, width), BF),
                pltpu.VMEM((heads_size, EXTRA, width), BF),
                pltpu.VMEM((heads_size, tokens, width), BF),
                pltpu.VMEM((heads_size, tokens, width), BF),
                dma((4,)),
                dma((4,)),
                dma((2, 4)),
            ],
        )
        normed2, far_other_d = tie(normed2, far_other_d)
        cross_other_d = swap_heads(far_other_d, 1)
        parts_d = (own_d, near_d, far_d, far_other_d, cross_d, cross_other_d)
        pieces = shape(2, PIECES, rows, width, dtype=BF)
        one = shape(PIECES, rows, width, dtype=BF)
        stage = pltpu.VMEM((2, width, width), BF)
        out_sems = dma((2, PIECES))
        latents, logdet, means, tops, direct, grad_hidden2, grad_w_out, gdown, keep_d, *sends_d = call(
            down_kernel,
            (
                where, segments, hidden1, activated, b_down, w_out.T, b_out[:, None], patches_t, latent_grad.T,
                logdet_grad[None],
            )
            + parts_d,
            [SMEM, SMEM, VMEM, HBM] + [VMEM] * 6 + [HBM] * 6,
            (
                shape(channels, tokens), shape(1, tokens), shape(1, row_count), shape(1, row_count),
                shape(channels, tokens),
                full, shape(2 * channels, width), shape(8, width), pieces, one, one,
            ),
            (VMEM,) * 8 + (HBM,) * 3,
            [
                pltpu.VMEM((heads_size, width, width), BF),
                pltpu.VMEM((heads_size, tokens, width), BF),
                pltpu.VMEM((tokens, width), F32),
                pltpu.VMEM((tokens, width), BF),
                stage,
                dma((4,)),
                dma((4,)),
                out_sems,
            ],
            length=length,
            quarter=quarter,
        )
        chains = [Chain(order) for order in CHAIN_ORDERS]
        down, up, mix, last = chains

        def add_groups(*groups):
            def spec(view, start):
                size = view.size
                block = (view.array.shape[3] // 2, view.array.shape[4])

                def at(i):
                    return tuple(a // b for a, b in zip(start, size)) + (i, 0)

                return pl.BlockSpec(size + block, at)

            views = [view for group in groups for view in group]
            return pl.pallas_call(
                functools.partial(add_kernel, counts=tuple(len(group) for group in groups)),
                grid=(2,),
                in_specs=[spec(view, view.start) for view in views],
                out_specs=[spec(group[0], (0, 0, 0)) for group in groups],
                out_shape=[shape(*group[0].size, *group[0].array.shape[3:], dtype=BF) for group in groups],
                compiler_params=pltpu.CompilerParams(vmem_limit_bytes=60 << 20),
                cost_estimate=pl.CostEstimate(flops=1, transcendentals=0, bytes_accessed=1),
            )(*(view.array for view in views))

        def halves(chain, keep, gots):
            keep = chain.view(keep)
            return [[keep.narrow(0, index), chain.view(got)] for index, got in enumerate(gots)]

        grad_hidden2, *sends_d = tie(grad_hidden2, *sends_d)
        got_d = [swap_heads(send, 1) for send in sends_d]
        pre_grads, gpre = call(
            grad_pre_kernel,
            (where, grad_hidden2, slope) + parts_d,
            [SMEM, VMEM, HBM] + [HBM] * 6,
            (four, shape(8, width)),
            (HBM, VMEM),
            [
                pltpu.VMEM((heads_size, width, width), BF),
                pltpu.VMEM((heads_size, tokens, width), BF),
                pltpu.VMEM((tokens, width), BF),
                pltpu.VMEM((heads_size, tokens, width), BF),
                dma((4,)),
                dma((4,)),
                dma((4,)),
            ],
        )
        pre_grads, *got_d = tie(pre_grads, *got_d)
        down.groups = halves(down, keep_d, got_d)
        pre_grads, *sends = tie(pre_grads, *add_groups(*down.parts()))
        down.launch(sends)
        grad_hidden1, grad_mix, gup, keep_u, *sends_u = call(
            up_back_kernel,
            (where, grad_hidden2, pre_grads, normed2, hidden1, ln2_gain) + parts_u,
            [SMEM, VMEM, HBM] + [VMEM] * 3 + [HBM] * 6,
            (full, low, shape(8, width), pieces, one, one),
            (VMEM, VMEM, VMEM, HBM, HBM, HBM),
            [
                pltpu.VMEM((heads_size, width, width), BF),
                pltpu.VMEM((heads_size, tokens, width), BF),
                pltpu.VMEM((tokens, width), F32),
                stage,
                dma((4,)),
                dma((4,)),
                out_sems,
            ],
        )
        grad_mix, *sends_u = tie(grad_mix, *sends_u)
        got_u = [swap_heads(send, 1) for send in sends_u]

        def attend_back(saved, parts, before):
            chained = () if before is None else (before,)
            mixed_pieces = shape(PIECES, 3 * unit, width, dtype=BF)
            return call(
                attend_back_kernel,
                (where, grad_mix) + tuple(saved) + (normed1,) + chained + parts,
                [SMEM] + [VMEM] * (7 + len(chained)) + [HBM] * len(parts),
                (full, shape(width // 2, width, dtype=BF), mixed_pieces, mixed_pieces),
                (VMEM, VMEM, HBM, HBM),
                [pltpu.VMEM((4, width // 2, width), BF)]
                + [pltpu.VMEM((tokens, width // 2), BF)] * 4
                + [pltpu.VMEM((3, width // 2, width), BF), dma((8,)), dma((3, 2 * PIECES))],
                length=length,
                quarter=quarter,
                count=len(parts),
                chained=before is not None,
            )

        total_far, gq_far, keep_far, send_far = attend_back(saved_far, parts_far, None)
        total_far, send_far, *got_d = tie(total_far, send_far, *down.got)
        total_far, *got_u = tie(total_far, *got_u)
        got_far = swap_heads(send_far, 1)
        down.deliver(got_d)
        up.groups = halves(up, keep_u, got_u)
        total_far, *sends = tie(total_far, *add_groups(*down.parts(), *up.parts()))
        down.launch(sends[:1])
        up.launch(sends[1:])
        total_near, gq_near, keep_near, send_near = attend_back(saved_near, parts_near, total_far)
        total_near, send_near, got_far, *got_d = tie(total_near, send_near, got_far, *down.got)
        got_near = swap_heads(send_near, 1)
        mix.groups = [[], [mix.view(keep_far), mix.view(got_far)]]
        down.deliver(got_d)
        grad_hidden1, *sends = tie(grad_hidden1, *add_groups(*down.parts(), *mix.parts()))
        down.launch(sends[:1])
        mix.launch(sends[1:])
        groups = 4 * PIECES
        last_pieces = shape(2, PIECES, unit + GROUP, width, dtype=BF)
        patches_grad, slot_rows, keep_q, send_q = call(
            embed_back_kernel,
            (
                where, segments, labels, grad_hidden1, total_near, hidden0, ln1_gain, patches_t,
                direct, w_in, grad_w_out, gdown, gup, gpre, gq_near, gq_far,
            ),
            [SMEM, SMEM, SMEM] + [VMEM] * 13,
            (shape(channels, tokens), shape(row_count * slot_count, width + 128), last_pieces, last_pieces),
            (VMEM, VMEM, HBM, HBM),
            [
                pltpu.VMEM((tokens, width), F32),
                pltpu.VMEM((tokens, width), BF),
                pltpu.VMEM((EXTRA, width), F32),
                pltpu.VMEM((groups * GROUP, width), BF),
                dma((2, groups)),
            ],
            length=length,
            quarter=quarter,
        )
        patches_grad, *got_u = tie(patches_grad, *up.got)
        patches_grad, *got_d = tie(patches_grad, *down.got)
        patches_grad, send_q = tie(patches_grad, send_q)
        last.groups = [[last.view(keep_q), last.view(swap_heads(send_q, 1))]]
        mix.groups[0] = [mix.view(keep_near), mix.view(got_near)]
        down.got, up.got = got_d, got_u
        gathered = slot_rows.astype(BF)
        gathers = [("rows", 1 << level) for level in reversed(range(levels))]
        gathers += [("heads", 2), ("heads", 1)]
        share = (len(gathers) - 1) // 4
        token = got_d[0]
        pending = {0, 1, 2}
        heads_left = [2, 1]
        got = None
        small = None
        for index in TAIL:
            if index == 4:
                more = gathers[:share] if len(gathers) > 2 + share else gathers[:1]
                for axis, bit in more:
                    gathers.pop(0)
                    if got is not None:
                        gathered = jnp.concatenate([gathered, ordered(got, token)], 0)
                    token = gathered = ordered(gathered, token)
                    got = (swap_rows if axis == "rows" else swap_heads)(gathered, bit)
                continue
            if index == 5:
                if small is None:
                    last.deliver([ordered(more, token) for more in last.got])
                    axis = Chain.axes[[a for a in last.order if a != "y"][0]] - 1
                    small = jnp.concatenate([last.low[:, :, unit:], last.high[:, :, unit:]], axis)
                    small = small.reshape(1, PIECES, GROUP, width)
                token = small = ordered(small, token)
                small_got = swap_heads(small, heads_left.pop(0))
                if heads_left:
                    small = jnp.concatenate([small, small_got], 0)
                continue
            chain = chains[index]
            if index in pending:
                chain.deliver([ordered(one, token) for one in chain.got])
            pending.add(index)
            sends = []
            for send in chain.prepare():
                token = ordered(send, token)
                sends.append(token)
            chain.launch(sends)
        gathered = jnp.concatenate([gathered, got], 0)
        for axis, bit in gathers:
            swap = swap_rows if axis == "rows" else swap_heads
            gathered = jnp.concatenate([gathered, swap(gathered, bit)], 0)
        for chain in chains[:3]:
            chain.deliver(chain.got)
        gathered = gathered.reshape(-1, width + 128)
        digits = gathered[:, width : width + 2].astype(jnp.int32)
        slot_label = digits[:, 0] * 32 + digits[:, 1]
        label_onehot = (
            lax.broadcasted_iota(jnp.int32, (classes, 1), 0) == slot_label[None, :]
        ).astype(BF)
        sum_cls = nn(label_onehot, gathered[:, :width])

        def place(chain):
            return call(
                place_kernel,
                (where, chain.low, chain.high),
                [SMEM, HBM, HBM],
                shape(width, width),
                HBM,
                [
                    pltpu.VMEM(chain.low.shape, BF),
                    pltpu.VMEM(chain.high.shape, BF),
                    pltpu.VMEM((PIECES, rows, width), F32),
                    dma((2,)),
                    dma((PIECES,)),
                ],
            )

        sum_down, sum_up = place(down), place(up)
        units = shape(part, width)
        line = shape(1, width)
        sum_k, sum_v, sum_o, sum_q, sum_w_in, sum_w_out, sum_pos, *lines = call(
            place_last_kernel,
            (where, mix.low, mix.high, last.low, last.high, small, small_got),
            [SMEM] + [VMEM] * 6,
            (units,) * 4
            + (shape(channels, width), shape(2 * channels, width), shape(length, width))
            + (shape(width // 128, 128),)
            + (line,) * 6
            + (shape(1, 2 * channels),),
            (VMEM,) * 15,
            [pltpu.VMEM((groups * GROUP, width), F32)],
        )
        sum_b_in, sum_gain1, sum_bias1, sum_gain2, sum_bias2, sum_b_down, sum_b_up, sum_b_out = lines
        return (
            latents.T,
            logdet.reshape(tokens),
            patches_grad.T,
            means.reshape(row_count),
            tops.reshape(row_count),
            sum_w_in,
            sum_b_in.reshape(width),
            sum_pos,
            sum_cls,
            sum_gain1,
            sum_bias1,
            sum_q.T[None],
            sum_k.T[None],
            sum_v.T[None],
            sum_o[None],
            sum_gain2,
            sum_bias2,
            sum_up[None],
            sum_b_up,
            sum_down[None],
            sum_b_down,
            sum_w_out.T,
            sum_b_out.reshape(2 * channels),
        )

    return program


def solution(mesh):
    tokens = P(("rows", "heads"))
    tokens2 = P(("rows", "heads"), None)
    last = P(None, None, "heads")
    middle = P(None, "heads", None)
    in_specs = (
        (tokens2, P("rows"), tokens2)
        + (P(),) * 6
        + (last, last, last, middle)
        + (P(), P(), last, P(None, "heads"), middle, P(), P(), P())
        + (tokens2, tokens)
    )
    out_specs = (
        (tokens2, tokens, tokens2, tokens, tokens)
        + (P(),) * 6
        + (last, last, last, middle)
        + (P(), P(), last, P(None, "heads"), middle, P(), P(), P())
    )
    program = make_program(mesh.shape["rows"], mesh.shape["heads"])
    return jax.shard_map(
        program, mesh=mesh, in_specs=in_specs, out_specs=out_specs, check_vma=False
    )
```

```python
import functools

import jax
import jax.numpy as jnp
from jax import lax
from jax.experimental import pallas as pl
from jax.experimental.pallas import tpu as pltpu
from jax.sharding import PartitionSpec as P

HEAD_DIM = 64
EPSILON = 1e-05
SCALE = HEAD_DIM**-0.5
BF = jnp.bfloat16
F32 = jnp.float32
PIECES = 4
EXTRA = 16
GROUP = 32
CHUNK = 64
GATHER_ROWS = 32
CHAIN_ORDERS = ("yxz", "zxy", "yxz", "zyx")
TAIL = (0, 1, 3, 1, 3, 4, 2, 1, 3, 2, 4, 3, 0, 2, 3, 4, 1, 3, 4, 0, 2, 4, 5, 1, 2, 5)

VMEM = pl.BlockSpec(memory_space=pltpu.VMEM)
SMEM = pl.BlockSpec(memory_space=pltpu.SMEM)
HBM = pl.BlockSpec(memory_space=pl.ANY)


def nn(matrix, other):
    return lax.dot_general(matrix, other, (((1,), (0,)), ((), ())), preferred_element_type=F32)


def tn(matrix, other):
    return lax.dot_general(matrix, other, (((0,), (0,)), ((), ())), preferred_element_type=F32)


def nt(matrix, other):
    return lax.dot_general(matrix, other, (((1,), (1,)), ((), ())), preferred_element_type=F32)


def norm_parts(values):
    average = jnp.mean(values, -1, keepdims=True)
    centered = values - average
    spread = jnp.mean(centered * centered, -1, keepdims=True)
    rstd = lax.rsqrt(spread + EPSILON)
    return centered * rstd, rstd


def norm_back(grad, gain, xhat, rstd):
    scaled = grad * gain
    back = scaled - jnp.mean(scaled, -1, keepdims=True)
    back = back - xhat * jnp.mean(scaled * xhat, -1, keepdims=True)
    return rstd * back


def column_sum(values):
    return jnp.sum(values, 0, keepdims=True)


def over_rows(tokens, body, first=0):
    def step(index, carry):
        body(pl.ds(pl.multiple_of(index * CHUNK, CHUNK), CHUNK))
        return carry

    lax.fori_loop(first // CHUNK, tokens // CHUNK, step, 0)


def gelu_pair(values):
    scaled = jnp.abs(values) * 0.7071067811865476
    base = 1.0 + 0.3275911 * scaled
    t = pl.reciprocal(base, approx=True)
    t = t * (2.0 - base * t)
    bell = jnp.exp(-0.5 * values * values)
    poly = 1.061405429 * t - 1.453152027
    poly = poly * t + 1.421413741
    poly = poly * t - 0.284496736
    poly = poly * t + 0.254829592
    tail = 0.5 * poly * t * bell
    below = jnp.where(values >= 0.0, 1.0 - tail, tail)
    return values * below, below + values * bell * 0.3989422804014327


def packed_flag(where_ref, seg_ref, row, length):
    start = where_ref[0] + row * length
    return seg_ref[start + length - 1] > 0


def embed_kernel(
    where_ref, seg_ref, patch_ref, w_ref, b_ref, pos_ref, cls_ref, gain_ref, bias_ref, hid_ref, norm_ref
):
    tokens, width = hid_ref.shape
    length = pos_ref.shape[0]
    slots = cls_ref.shape[0] // (tokens // length)
    quarter = length // slots
    hid_ref[...] = tn(patch_ref[...].astype(BF), w_ref[...]) + b_ref[...]
    for row in range(tokens // length):
        packed = packed_flag(where_ref, seg_ref, row, length)
        for slot in range(slots):
            at = slice(row * length + slot * quarter, row * length + (slot + 1) * quarter)
            here = pos_ref[slot * quarter : (slot + 1) * quarter].astype(F32)
            first = pos_ref[:quarter].astype(F32)
            one = cls_ref[row * slots + slot : row * slots + slot + 1]
            start = cls_ref[row * slots : row * slots + 1]
            value = hid_ref[at] + jnp.where(packed, first, here) + jnp.where(packed, one, start)
            hid_ref[at] = value
            xhat, _ = norm_parts(value)
            norm_ref[at] = (xhat * gain_ref[...] + bias_ref[...]).astype(BF)


def fetch_kind(where_ref, parts, weight_ref, sems, kind):
    unit = weight_ref.shape[1] // 2
    half, rows = kind // 2, pl.ds(unit * (kind % 2), unit)
    for slot in range(2):
        target, sem = weight_ref.at[kind, pl.ds(unit * slot, unit)], sems.at[2 * kind + slot]
        if len(parts) == 2:
            pltpu.make_async_copy(parts[slot].at[half, rows], target, sem).start()
            continue
        for other in range(2):

            @pl.when((where_ref[1] == half) == (other == 0))
            def _():
                pltpu.make_async_copy(parts[2 * slot + other].at[rows], target, sem).start()


def wait_kind(weight_ref, sems, kind):
    unit = weight_ref.shape[1] // 2
    for slot in range(2):
        target = weight_ref.at[kind, pl.ds(unit * slot, unit)]
        pltpu.make_async_copy(target, target, sems.at[2 * kind + slot]).wait()


def start_copies(copies, sems):
    made = [pltpu.make_async_copy(src, dst, sems.at[i]) for i, (src, dst) in enumerate(copies)]
    for copy in made:
        copy.start()
    return made


def fetch_full(where_ref, parts, weight_ref, sems):
    own, near, far, far_other, cross, cross_other = parts
    half = weight_ref.shape[1] // 2
    mine = pl.ds(pl.multiple_of(where_ref[1] * half, half), half)
    other = pl.ds(pl.multiple_of((1 - where_ref[1]) * half, half), half)
    copies = [
        (own, weight_ref.at[0], 0),
        (near, weight_ref.at[1], 1),
        (far, weight_ref.at[2, mine], 2),
        (far_other, weight_ref.at[2, other], 2),
        (cross, weight_ref.at[3, mine], 3),
        (cross_other, weight_ref.at[3, other], 3),
    ]
    for source, target, slot in copies:
        pltpu.make_async_copy(source, target, sems.at[slot]).start()


def wait_slot(source, into_ref, sems, slot):
    pltpu.make_async_copy(source, into_ref.at[slot], sems.at[slot]).wait()


def mask_bias(packed, quarter, length, part):
    block = length // 2
    q = (lax.broadcasted_iota(jnp.int32, (length, length), 1) & (block - 1)) + part * block
    k = lax.broadcasted_iota(jnp.int32, (length, length), 0)
    shift = quarter.bit_length() - 1
    same = (q >> shift) == (k >> shift)
    return jnp.where((k <= q) & (same | jnp.logical_not(packed)), 0.0, -1e30)


def by_head(values, lanes):
    return jnp.concatenate([values * lanes[0], values * lanes[1]], 0)


def own_lanes(values):
    block = values.shape[0] // 2
    lane = lax.broadcasted_iota(jnp.int32, (1, 128), 1)
    return jnp.where(lane < HEAD_DIM, values[:block], values[block:])


def head_lanes(value):
    lane = lax.broadcasted_iota(jnp.int32, (1, 128), 1)
    return [jnp.where(side, value, 0.0).astype(BF) for side in (lane < HEAD_DIM, lane >= HEAD_DIM)]


def attend_kernel(where_ref, seg_ref, hid_in, norm_ref, *rest, length, quarter, count):
    parts = rest[:count]
    (
        q_out, k_out, v_out, prob_out, att_out, out_ref,
        weight_ref, bias_ref, hid_ref, q_ref, k_ref, v_ref, prob_ref, att_ref, sems, io_sems, prob_sems,
    ) = rest[count:]
    tokens = hid_ref.shape[0]
    for kind in range(4):
        fetch_kind(where_ref, parts, weight_ref, sems, kind)
    moves = [
        pltpu.make_async_copy(source, target, io_sems.at[index])
        for index, (source, target) in enumerate(
            ((hid_in, hid_ref), (q_ref, q_out), (k_ref, k_out), (v_ref, v_out), (att_ref, att_out))
        )
    ]
    moves[0].start()
    for row in range(tokens // length):
        for part in range(2):
            packed = packed_flag(where_ref, seg_ref, row, length)
            bias_ref[row, part] = mask_bias(packed, quarter, length, part)
    for kind, ref in enumerate((q_ref, k_ref, v_ref)):
        wait_kind(weight_ref, sems, kind)
        ref[...] = nt(norm_ref[...], weight_ref[kind]).astype(BF)
        moves[1 + kind].start()
    pairs = q_ref.shape[1] // 128
    scaled = head_lanes(SCALE)
    block = length // 2

    def step(index, carry):
        row = index // pairs
        pair = index % pairs
        lanes = pl.ds(pl.multiple_of(pair * 128, 128), 128)
        for part in range(2):
            keys = (part + 1) * block
            here = pl.ds(pl.multiple_of(row * length + part * block, block), block)
            upto = pl.ds(pl.multiple_of(row * length, length), keys)
            queries = q_ref[here, lanes]
            key_rows = k_ref[upto, lanes]
            values = v_ref[upto, lanes]
            scores = nt(key_rows, by_head(queries, scaled)) + bias_ref[row, part, :keys]
            top = jnp.max(scores, 0, keepdims=True)
            grown = jnp.exp(scores - top)
            probs = (grown * (1.0 / jnp.sum(grown, 0, keepdims=True))).astype(BF)
            prob_ref[2 * index + part, :keys] = probs
            result = own_lanes(tn(probs, values))
            att_ref[here, lanes] = result.astype(BF)
        both = pl.ds(2 * index, 2)
        pltpu.make_async_copy(prob_ref.at[both], prob_out.at[both], prob_sems.at[index]).start()
        return carry

    lax.fori_loop(0, tokens // length * pairs, step, 0)
    moves[4].start()
    moves[0].wait()
    wait_kind(weight_ref, sems, 3)
    out_ref[...] = hid_ref[...] + nn(att_ref[...], weight_ref[3])
    for move in moves[1:]:
        move.wait()
    for index in range(tokens // length * pairs):
        both = slice(2 * index, 2 * index + 2)
        pltpu.make_async_copy(prob_ref.at[both], prob_out.at[both], prob_sems.at[index]).wait()


def up_kernel(
    where_ref, hid_ref, gain_ref, bias_ref, own, near, far, far_other, cross, cross_other,
    own_t, near_t, far_t, cross_t,
    norm_ref, act_out, slope_out, weight_ref, bup_ref, act_ref, slope_ref, sems, bias_sems, out_sems,
):
    tokens, width = hid_ref.shape
    fetch_full(where_ref, (own, near, far, far_other, cross, cross_other), weight_ref, sems)
    last = pl.ds(far_t.shape[0] - EXTRA, EXTRA)
    packs = (own_t.at[0, last], near_t.at[0, last], far_t.at[last], cross_t.at[last])
    biases = start_copies([(pack, bup_ref.at[slot]) for slot, pack in enumerate(packs)], bias_sems)

    def normalize(at):
        xhat, _ = norm_parts(hid_ref[at])
        norm_ref[at] = (xhat * gain_ref[...] + bias_ref[...]).astype(BF)

    over_rows(tokens, normalize)
    for bias in biases:
        bias.wait()
    block = 128

    def step(slot, carry):
        wait_slot(own, weight_ref, sems, slot)
        bias = bup_ref[slot, :1].astype(F32)
        for first in range(0, tokens, block):
            at = slice(first, first + block)
            pre = nn(norm_ref[at], weight_ref[slot]) + bias
            value, slope = gelu_pair(pre)
            act_ref[slot, at] = value.astype(BF)
            slope_ref[slot, at] = slope.astype(BF)
        pltpu.make_async_copy(act_ref.at[slot], act_out.at[slot], out_sems.at[0, slot]).start()
        pltpu.make_async_copy(slope_ref.at[slot], slope_out.at[slot], out_sems.at[1, slot]).start()
        return carry

    lax.fori_loop(0, 4, step, 0)
    for slot in range(4):
        pltpu.make_async_copy(act_ref.at[slot], act_out.at[slot], out_sems.at[0, slot]).wait()
        pltpu.make_async_copy(slope_ref.at[slot], slope_out.at[slot], out_sems.at[1, slot]).wait()


def send_pieces(where_ref, stage_ref, slot, keep, sends, sems, rows):
    for piece in range(PIECES):
        source = stage_ref.at[piece * rows : (piece + 1) * rows]
        target = piece ^ where_ref[2]

        @pl.when(slot % 2 == 0)
        def _():
            pltpu.make_async_copy(source, keep.at[slot // 2, target], sems.at[piece]).start()

        for index, send in enumerate(sends):

            @pl.when(slot == 2 * index + 1)
            def _():
                pltpu.make_async_copy(source, send.at[target], sems.at[piece]).start()


def wait_pieces(stage_ref, keep, sems, rows):
    for piece in range(PIECES):
        source = stage_ref.at[piece * rows : (piece + 1) * rows]
        pltpu.make_async_copy(source, keep.at[0, 0, :rows], sems.at[piece]).wait()


def down_kernel(
    where_ref, seg_ref, hid_in, act_in, bdown_ref, wout_ref, bout_ref, patch_ref, lgrad_ref, dgrad_ref,
    own, near, far, far_other, cross, cross_other,
    latent_ref, logdet_ref, mean_ref, max_ref, direct_ref, grad_ref, gwout_ref, gvec_ref, keep_ref, send_near, send_far,
    weight_ref, act_ref, total_ref, branch_ref, stage_ref, hid_ref, sems, act_sems, out_sems, hid_sem,
    *, length, quarter,
):
    tokens, width = total_ref.shape
    channels = patch_ref.shape[0]
    send_refs = (send_near, send_far)
    start_copies([(act_in.at[slot], act_ref.at[slot]) for slot in range(4)], act_sems)
    fetch_full(where_ref, (own, near, far, far_other, cross, cross_other), weight_ref, sems)
    hidden = pltpu.make_async_copy(hid_in, hid_ref, hid_sem)
    hidden.start()
    total_ref[...] = jnp.zeros(total_ref.shape, F32)

    def gather(slot, carry):
        wait_slot(act_in.at[slot], act_ref, act_sems, slot)
        wait_slot(own, weight_ref, sems, slot)
        total_ref[...] += nn(act_ref[slot], weight_ref[slot])
        return carry

    lax.fori_loop(0, 4, gather, 0)
    hidden.wait()
    top_low = (total_ref[...] + hid_ref[...] + bdown_ref[...]).astype(BF)
    head_out = nt(wout_ref[...], top_low) + bout_ref[...]
    token = lax.broadcasted_iota(jnp.int32, (1, tokens), 1)
    row_count = tokens // length
    starts = jnp.zeros((1, tokens), jnp.bool_)
    for row in range(row_count):
        packed = packed_flag(where_ref, seg_ref, row, length)
        inside = (token >= row * length) & (token < (row + 1) * length)
        fresh = (token & jnp.where(packed, quarter - 1, length - 1)) == 0
        starts = starts | (inside & fresh)
    previous = jnp.where(starts, 0.0, pltpu.roll(head_out, 1, 1))
    shifts = previous[:channels]
    logscale = previous[channels:]
    shrink = jnp.exp(-logscale)
    latents = (patch_ref[...] - shifts) * shrink
    latent_ref[...] = latents
    logdet_ref[...] = -column_sum(logscale)
    lane = lax.broadcasted_iota(jnp.int32, mean_ref.shape, 1)
    means = jnp.zeros(mean_ref.shape, F32)
    tops = means
    for row in range(row_count):
        part = logscale[:, row * length : (row + 1) * length]
        means = jnp.where(lane == row, jnp.sum(part) * (1.0 / (length * channels)), means)
        tops = jnp.where(lane == row, jnp.max(part), tops)
    mean_ref[...] = means
    max_ref[...] = tops
    lgrad = lgrad_ref[...]
    direct = lgrad * shrink
    direct_ref[...] = direct
    grad_prev = jnp.concatenate([-direct, -lgrad * latents - dgrad_ref[...]], 0)
    grad_prev = jnp.where(starts, 0.0, grad_prev)
    grad_head = pltpu.roll(grad_prev, tokens - 1, 1).astype(BF)
    gwout_ref[...] = nn(grad_head, top_low)
    grad_hidden = tn(grad_head, wout_ref[...])
    grad_ref[...] = grad_hidden
    branch_ref[...] = grad_hidden.astype(BF)
    gvec_ref[...] = jnp.zeros(gvec_ref.shape, F32)
    gvec_ref[0:1, :] = column_sum(grad_hidden)
    row_of = nt(jnp.ones((8, tokens), BF), grad_head)
    gvec_ref[1:2, : 2 * channels] = row_of[:1]
    rows = width // PIECES


    def step(slot, carry):
        @pl.when(slot >= 2)
        def _():
            wait_pieces(stage_ref.at[slot % 2], keep_ref, out_sems.at[slot % 2], rows)

        stage_ref[slot % 2] = tn(act_ref[slot], branch_ref[...]).astype(BF)
        send_pieces(where_ref, stage_ref.at[slot % 2], slot, keep_ref, send_refs, out_sems.at[slot % 2], rows)
        return carry

    lax.fori_loop(0, 4, step, 0)
    for slot in range(2):
        wait_pieces(stage_ref.at[slot], keep_ref, out_sems.at[slot], rows)


def grad_pre_kernel(
    where_ref, grad_ref, slope_in, own, near, far, far_other, cross, cross_other,
    pre_out, sum_ref, weight_ref, slope_ref, branch_ref, pre_ref, sems, slope_sems, out_sems,
):
    start_copies([(slope_in.at[slot], slope_ref.at[slot]) for slot in range(4)], slope_sems)
    fetch_full(where_ref, (own, near, far, far_other, cross, cross_other), weight_ref, sems)
    branch_ref[...] = grad_ref[...].astype(BF)

    def step(slot, carry):
        wait_slot(slope_in.at[slot], slope_ref, slope_sems, slot)
        wait_slot(own, weight_ref, sems, slot)
        grad_pre = (nt(branch_ref[...], weight_ref[slot]) * slope_ref[slot].astype(F32)).astype(BF)
        pre_ref[slot] = grad_pre
        pltpu.make_async_copy(pre_ref.at[slot], pre_out.at[slot], out_sems.at[slot]).start()
        sum_ref[pl.ds(slot, 1), :] = column_sum(grad_pre.astype(F32))
        return carry

    lax.fori_loop(0, 4, step, 0)
    for slot in range(4):
        pltpu.make_async_copy(pre_ref.at[slot], pre_out.at[slot], out_sems.at[slot]).wait()


def up_back_kernel(
    where_ref, grad_in, pre_in, norm_ref, hid_in, gain_ref, own, near, far, far_other, cross, cross_other,
    gout_ref, mix_ref, gvec_ref, keep_ref, send_near, send_far,
    weight_ref, pre_ref, total_ref, stage_ref, grad_ref, hid_ref, sems, pre_sems, out_sems, late_sems,
):
    tokens, width = grad_ref.shape
    send_refs = (send_near, send_far)
    start_copies([(pre_in.at[slot], pre_ref.at[slot]) for slot in range(4)], pre_sems)
    late = start_copies([(grad_in, grad_ref), (hid_in, hid_ref)], late_sems)
    total_ref[...] = jnp.zeros(total_ref.shape, F32)
    fetch_full(where_ref, (own, near, far, far_other, cross, cross_other), weight_ref, sems)
    gvec_ref[...] = jnp.zeros(gvec_ref.shape, F32)
    rows = width // PIECES

    def step(slot, carry):
        @pl.when(slot >= 2)
        def _():
            wait_pieces(stage_ref.at[slot % 2], keep_ref, out_sems.at[slot % 2], rows)

        wait_slot(pre_in.at[slot], pre_ref, pre_sems, slot)
        wait_slot(own, weight_ref, sems, slot)
        stage_ref[slot % 2] = tn(norm_ref[...], pre_ref[slot]).astype(BF)
        send_pieces(where_ref, stage_ref.at[slot % 2], slot, keep_ref, send_refs, out_sems.at[slot % 2], rows)
        total_ref[...] += nt(pre_ref[slot], weight_ref[slot])
        return carry

    lax.fori_loop(0, 4, step, 0)

    def finish(at):
        xhat, rstd = norm_parts(hid_ref[at])
        grad = total_ref[at]
        value = grad_ref[at] + norm_back(grad, gain_ref[...], xhat, rstd)
        gout_ref[at] = value
        mix_ref[at] = value.astype(BF)
        gvec_ref[0:1, :] += column_sum(grad * xhat)
        gvec_ref[1:2, :] += column_sum(grad)

    for copy in late:
        copy.wait()
    over_rows(tokens, finish)
    for slot in range(2):
        wait_pieces(stage_ref.at[slot], keep_ref, out_sems.at[slot], rows)


def attend_back_kernel(
    where_ref, mix_in, q_in, k_in, v_in, prob_in, att_in, norm_in, *rest, length, quarter, count, chained
):
    before_in = rest[0] if chained else None
    rest = rest[1:] if chained else rest
    parts = rest[:count]
    (
        total_ref, gq_ref, keep_ref, send_ref,
        weight_ref, gatt_ref, dq_ref, dk_ref, dv_ref, stage_ref, sems, out_sems,
        mix_ref, q_ref, k_ref, v_ref, prob_ref, att_ref, norm_ref, before_ref, in_sems,
    ) = rest[count:]
    tokens = mix_ref.shape[0]
    fetch_kind(where_ref, parts, weight_ref, sems, 3)
    moves = [
        (mix_in, mix_ref), (att_in, att_ref), (q_in, q_ref), (k_in, k_ref), (v_in, v_ref), (prob_in, prob_ref),
        (norm_in, norm_ref),
    ]
    moves = start_copies(moves + ([(before_in, before_ref)] if chained else []), in_sems)
    for kind in range(3):
        fetch_kind(where_ref, parts, weight_ref, sems, kind)
    moves[0].wait()
    wait_kind(weight_ref, sems, 3)
    gatt_ref[...] = nt(mix_ref[...], weight_ref[3]).astype(BF)
    pairs = q_ref.shape[1] // 128
    lefts = head_lanes(1.0)
    scaled = head_lanes(SCALE)
    block = length // 2
    unit = weight_ref.shape[1] // 2
    rows = unit // PIECES

    def publish(kind, left, right):
        stage_ref[kind] = tn(left, right).astype(BF)
        for slot, into in enumerate((keep_ref, send_ref)):
            for piece in range(PIECES):
                at = slot * unit + piece * rows
                pltpu.make_async_copy(
                    stage_ref.at[kind, at : at + rows],
                    into.at[piece ^ where_ref[2], kind * rows : (kind + 1) * rows],
                    out_sems.at[kind, slot * PIECES + piece],
                ).start()

    moves[1].wait()
    publish(2, att_ref[...], mix_ref[...])
    for move in moves[2:6]:
        move.wait()

    def step(index, carry):
        row = index // pairs
        pair = index % pairs
        lanes = pl.ds(pl.multiple_of(pair * 128, 128), 128)
        grads_k = [None, None]
        grads_v = [None, None]
        for part in range(2):
            keys = (part + 1) * block
            here = pl.ds(pl.multiple_of(row * length + part * block, block), block)
            upto = pl.ds(pl.multiple_of(row * length, length), keys)
            queries = q_ref[here, lanes]
            key_rows = k_ref[upto, lanes]
            values = v_ref[upto, lanes]
            grad_out = gatt_ref[here, lanes]
            probs = prob_ref[2 * index + part, :keys]
            wide = probs.astype(F32)
            grad_both = by_head(grad_out, lefts)
            grad_probs = nt(values, grad_both)
            inner = jnp.sum(wide * grad_probs, 0, keepdims=True)
            grad_scores = (wide * (grad_probs - inner)).astype(BF)
            result = own_lanes(tn(grad_scores, key_rows)) * SCALE
            grads_k[part] = nn(grad_scores, by_head(queries, scaled))
            grads_v[part] = nn(probs, grad_both)
            dq_ref[here, lanes] = result.astype(BF)
        low = pl.ds(pl.multiple_of(row * length, length), block)
        high = pl.ds(pl.multiple_of(row * length + block, block), block)
        dk_ref[low, lanes] = (grads_k[0] + grads_k[1][:block]).astype(BF)
        dk_ref[high, lanes] = grads_k[1][block:].astype(BF)
        dv_ref[low, lanes] = (grads_v[0] + grads_v[1][:block]).astype(BF)
        dv_ref[high, lanes] = grads_v[1][block:].astype(BF)
        return carry

    lax.fori_loop(0, tokens // length * pairs, step, 0)
    moves[6].wait()
    publish(0, dk_ref[...], norm_ref[...])
    publish(1, dv_ref[...], norm_ref[...])
    gq_ref[...] = tn(dq_ref[...], norm_ref[...]).astype(BF)
    for kind in range(3):
        wait_kind(weight_ref, sems, kind)
    total = nn(dq_ref[...], weight_ref[0]) + nn(dk_ref[...], weight_ref[1]) + nn(dv_ref[...], weight_ref[2])
    if chained:
        moves[7].wait()
        total = total + before_ref[...]
    total_ref[...] = total
    for kind in range(3):
        for piece in range(2 * PIECES):
            pltpu.make_async_copy(
                stage_ref.at[kind, :rows], keep_ref.at[0, :rows], out_sems.at[kind, piece]
            ).wait()


def embed_back_kernel(
    where_ref, seg_ref, label_ref, grad_in, total_in, hid_in, gain_ref, patch_ref, direct_ref, win_ref,
    gwout_ref, gdown_ref, gup_ref, gpre_ref, gq_near, gq_far,
    pgrad_ref, slot_ref, keep_ref, send_ref,
    value_ref, embed_ref, acc_ref, small_ref, grad_ref, total_ref, hid_ref, sems, in_sems,
    *, length, quarter,
):
    tokens, width = hid_ref.shape
    half = tokens // 2
    moves = [
        (source.at[first : first + half], target.at[first : first + half])
        for first in (0, half)
        for source, target in ((grad_in, grad_ref), (total_in, total_ref), (hid_in, hid_ref))
    ]
    moves = start_copies(moves, in_sems)
    channels = patch_ref.shape[0]
    unit = width // 4
    rows = unit // PIECES
    sources = []
    for slot in range(4):
        source = (gq_near, gq_far)[slot // 2]
        into = (keep_ref, send_ref)[slot % 2]
        for piece in range(PIECES):
            at = (slot % 2) * unit + piece * rows
            sources.append((source.at[at : at + rows], into.at[slot // 2, piece ^ where_ref[2], :rows]))
    copies = start_copies(sources, sems.at[0])
    acc_ref[...] = jnp.zeros(acc_ref.shape, F32)

    def finish(at):
        xhat, rstd = norm_parts(hid_ref[at])
        grad = total_ref[at]
        acc_ref[1:2, :] += column_sum(grad * xhat)
        acc_ref[2:3, :] += column_sum(grad)
        value = grad_ref[at] + norm_back(grad, gain_ref[...], xhat, rstd)
        value_ref[at] = value
        embed = value.astype(BF)
        embed_ref[at] = embed
        acc_ref[0:1, :] += column_sum(embed.astype(F32))

    for side in range(2):
        for move in moves[3 * side : 3 * side + 3]:
            move.wait()
        over_rows((side + 1) * half, finish, side * half)
    acc_ref[3:5, :] = gup_ref[0:2, :]
    acc_ref[5:7, :] = gdown_ref[0:2, :]
    for slot in range(4):
        acc_ref[pl.ds(7 + (slot ^ where_ref[3]), 1), :] = gpre_ref[slot : slot + 1, :]
    small_ref[:channels] = nn(patch_ref[...].astype(BF), embed_ref[...]).astype(BF)
    small_ref[channels : 3 * channels] = gwout_ref[...].astype(BF)
    first = 3 * channels
    rows_here = tokens // length
    slots = length // quarter
    packed = [packed_flag(where_ref, seg_ref, row, length) for row in range(rows_here)]
    zero = jnp.zeros((quarter, width), F32)
    for slot in range(slots):
        value = zero
        for row in range(rows_here):
            at = row * length + slot * quarter
            here = value_ref[at : at + quarter]
            value = value + jnp.where(packed[row], 0.0, here)
            if slot == 0:
                every = here
                for later in range(1, slots):
                    every = every + value_ref[at + later * quarter : at + (later + 1) * quarter]
                value = value + jnp.where(packed[row], every, 0.0)
        small_ref[first + slot * quarter : first + (slot + 1) * quarter] = value.astype(BF)
    start = first + length
    small_ref[start : start + EXTRA] = acc_ref[...].astype(BF)
    start += EXTRA
    small_ref[start:] = jnp.zeros((small_ref.shape[0] - start, width), BF)
    moved = []
    for block in range(4):
        slot = block ^ where_ref[3]
        for piece in range(PIECES):
            at = (block * PIECES + piece) * GROUP
            moved.append((slot, piece ^ where_ref[2], small_ref.at[at : at + GROUP]))
    for index, (slot, piece, source) in enumerate(moved):

        @pl.when(slot % 2 == 0)
        def _():
            into = keep_ref.at[slot // 2, piece, rows:]
            pltpu.make_async_copy(source, into, sems.at[1, index]).start()

        @pl.when(slot % 2 == 1)
        def _():
            into = send_ref.at[slot // 2, piece, rows:]
            pltpu.make_async_copy(source, into, sems.at[1, index]).start()

    lane = lax.broadcasted_iota(jnp.int32, (1, slot_ref.shape[1] - width), 1)
    for row in range(rows_here):
        sums = []
        for slot in range(slots):
            at = row * length + slot * quarter
            sums.append(column_sum(value_ref[at : at + quarter]))
        every = sums[0]
        for slot in range(1, slots):
            every = every + sums[slot]
        for slot in range(slots):
            other = every if slot == 0 else jnp.zeros_like(every)
            index = row * slots + slot
            slot_ref[index : index + 1, :width] = jnp.where(packed[row], sums[slot], other)
            label = label_ref[row, slot]
            digits = jnp.where(lane == 0, label >> 5, jnp.where(lane == 1, label & 31, 0))
            slot_ref[index : index + 1, width:] = digits.astype(F32)
    pgrad_ref[...] = direct_ref[...] + nt(win_ref[...], embed_ref[...])
    for copy in copies:
        copy.wait()
    for index in range(4 * PIECES):
        pltpu.make_async_copy(
            small_ref.at[:GROUP], keep_ref.at[0, 0, rows:], sems.at[1, index]
        ).wait()


def add_kernel(*refs, counts):
    sources, outs = refs[: sum(counts)], refs[sum(counts) :]
    for count, out_ref in zip(counts, outs):
        total = sources[0][...].astype(F32)
        for ref in sources[1:count]:
            total = total + ref[...].astype(F32)
        out_ref[...] = total.astype(BF)
        sources = sources[count:]


def piece_list(low, high):
    found = []
    for bit, ref in ((0, low), (1, high)):
        for i in range(ref.shape[0]):
            for j in range(ref.shape[1]):
                found.append((ref, i, j, i + (bit if low.shape[0] == 1 else 0), j + (bit if low.shape[1] == 1 else 0)))
    return [(ref, i, j, 2 * x + z) for ref, i, j, x, z in found]


def place_kernel(where_ref, low_in, high_in, out, low_ref, high_ref, stage_ref, in_sems, out_sems):
    rows = low_ref.shape[2]
    start_copies([(low_in, low_ref), (high_in, high_ref)], in_sems)
    pltpu.make_async_copy(low_in, low_ref, in_sems.at[0]).wait()
    pieces = piece_list(low_ref, high_ref)
    copies = []
    for index, (ref, i, j, piece) in enumerate(pieces):
        if index == 2:
            pltpu.make_async_copy(high_in, high_ref, in_sems.at[1]).wait()
        stage_ref[index] = ref[i, j].astype(F32)
        at = pl.ds(pl.multiple_of((piece ^ where_ref[2]) * rows, rows), rows)
        copies.append(pltpu.make_async_copy(stage_ref.at[index], out.at[at], out_sems.at[index]))
        copies[-1].start()
    for copy in copies:
        copy.wait()


def place_last_kernel(
    where_ref, mix_low, mix_high, low_ref, high_ref, all_ref, cross_ref,
    gk_ref, gv_ref, go_ref, gq_ref, gin_ref, gout_ref, gpos_ref, gbin_ref, *rest,
):
    *vectors, bup_ref, bout_ref, flat_ref = rest
    rows = gq_ref.shape[0] // PIECES
    for ref, i, j, piece in piece_list(mix_low, mix_high):
        at = pl.ds(pl.multiple_of((piece ^ where_ref[2]) * rows, rows), rows)
        gk_ref[at] = ref[i, j, :rows].astype(F32)
        gv_ref[at] = ref[i, j, rows : 2 * rows].astype(F32)
        go_ref[at] = ref[i, j, 2 * rows :].astype(F32)
    for ref, i, j, piece in piece_list(low_ref, high_ref):
        at = pl.ds(pl.multiple_of((piece ^ where_ref[2]) * rows, rows), rows)
        gq_ref[at] = ref[i, j, :rows].astype(F32)
    channels = gin_ref.shape[0]
    for core, ref in enumerate((all_ref, cross_ref)):
        for far in range(2):
            for piece in range(PIECES):
                head = (2 * far + core) ^ where_ref[3]
                group = head * PIECES + (piece ^ where_ref[2])
                flat_ref[pl.ds(pl.multiple_of(group * GROUP, GROUP), GROUP)] = ref[far, piece].astype(F32)
    start = 3 * channels
    gin_ref[...] = flat_ref[:channels]
    gout_ref[...] = flat_ref[channels:start]
    length = gpos_ref.shape[0]
    gpos_ref[...] = flat_ref[start : start + length]
    start += length
    for index in range(gbin_ref.shape[0]):
        gbin_ref[index : index + 1] = flat_ref[start : start + 1, index * 128 : (index + 1) * 128]
    for index, ref in enumerate(vectors):
        ref[...] = flat_ref[start + 1 + index : start + 2 + index]
    bout_ref[...] = flat_ref[start + 6 : start + 7, : bout_ref.shape[1]]
    bup_ref[...] = flat_ref[pl.ds(start + 7 + where_ref[3], 1)]


def make_program(rows_size, heads_size):
    levels = rows_size.bit_length() - 1

    def swap_heads(array, bit):
        return lax.ppermute(array, "heads", [(i, i ^ bit) for i in range(heads_size)])

    def swap_rows(array, bit):
        return lax.ppermute(array, "rows", [(i, i ^ bit) for i in range(rows_size)])

    def add_low(arrays):
        total = arrays[0].astype(F32)
        for other in arrays[1:]:
            total = total + other.astype(F32)
        return total.astype(BF)

    def tie(*values):
        return lax.optimization_barrier(values)

    def ordered(value, token):
        return tie(value, token)[0]

    class View:
        def __init__(self, array, start=(0, 0, 0), size=None):
            self.array, self.start = array, tuple(start)
            self.size = tuple(size or array.shape[:3])

        def narrow(self, axis, index):
            start, size = list(self.start), list(self.size)
            if size[axis] > 1:
                start[axis] += index
            size[axis] = 1
            return View(self.array, start, size)

        def value(self):
            stop = [a + b for a, b in zip(self.start, self.size)] + list(self.array.shape[3:])
            return lax.slice(self.array, self.start + (0, 0), stop)

    def add_views(views):
        return add_low([view.value() for view in views])

    class Chain:
        axes = {"y": 0, "x": 1, "z": 2}

        def __init__(self, order):
            self.order = order
            self.groups = []
            self.left = list(order) + ["w"] + [a for a in reversed(order) if a != "y"]

        def view(self, array):
            return View(array.reshape((-1, 2, 2) + array.shape[-2:]))

        def parts(self):
            kind = self.left[0]
            if kind == "y":
                return [[view.narrow(0, 1) for view in self.groups[-1]]]
            if "w" in self.left[1:]:
                axis = self.axes[kind]
                return [[view.narrow(axis, 1) for view in group] for group in self.groups]
            return [self.groups[0]]

        def prepare(self):
            if "w" in self.left:
                return [add_views(part) for part in self.parts()]
            return [self.total]

        def launch(self, sends):
            self.sends = sends
            kind = self.left[0]
            if kind == "y":
                self.got = [swap_heads(send, 2) for send in sends]
            else:
                self.got = [swap_rows(send, 1 << "xzw".index(kind)) for send in sends]

        def deliver(self, got):
            kind = self.left.pop(0)
            if kind == "w":
                self.total = add_low([self.sends[0], got[0]])
                for level in range(3, levels):
                    self.total = add_low([self.total, swap_rows(self.total, 1 << level)])
            elif "w" in self.left:
                axis = self.axes[kind]
                if kind == "y":
                    self.groups = self.groups[:1]
                self.groups = [
                    [view.narrow(axis, 0) for view in group] + [View(more)]
                    for group, more in zip(self.groups, got)
                ]
            elif self.left:
                self.total = jnp.concatenate([self.sends[0], got[0]], self.axes[kind])
            else:
                self.low, self.high = self.sends[0][0], got[0][0]

    def program(
        patches, segments, labels, w_in, b_in, pos_table, cls_table, ln1_gain, ln1_bias,
        w_query, w_key, w_value, w_attn_out, ln2_gain, ln2_bias, w_up, b_up, w_down, b_down,
        w_out, b_out, latent_grad, logdet_grad,
    ):
        tokens, channels = patches.shape
        length, width = pos_table.shape
        slot_count = labels.shape[1]
        quarter = length // slot_count
        classes = cls_table.shape[0]
        part = w_query.shape[2]
        row_count = tokens // length
        head_index = lax.axis_index("heads")
        row_index = lax.axis_index("rows")
        row_bit = row_index & 1
        mask = ((row_index & 1) << 1) | ((row_index >> 1) & 1)
        where = jnp.stack([head_index * tokens, row_bit, mask, head_index]).astype(jnp.int32)
        rows = width // PIECES
        unit = part // PIECES
        heads = width // HEAD_DIM
        square = 2 * tokens * width * width

        def shape(*dims, dtype=F32):
            return jax.ShapeDtypeStruct(dims, dtype)

        def call(kernel, operands, specs, outs, out_specs, scratch=(), room=60, **options):
            return pl.pallas_call(
                functools.partial(kernel, **options) if options else kernel,
                in_specs=specs,
                out_specs=out_specs,
                out_shape=outs,
                scratch_shapes=list(scratch),
                compiler_params=pltpu.CompilerParams(vmem_limit_bytes=room << 20),
                cost_estimate=pl.CostEstimate(
                    flops=1, transcendentals=0, bytes_accessed=1
                ),
            )(*operands)

        dma = pltpu.SemaphoreType.DMA
        low = shape(tokens, width, dtype=BF)
        full = shape(tokens, width)
        half_low = shape(tokens, width // 2, dtype=BF)

        bias_rows = jnp.pad(b_up, ((0, EXTRA - 1), (0, 0)))
        pack_t = jnp.stack(
            [
                jnp.concatenate([w_query[0].T, w_key[0].T, bias_rows], 0),
                jnp.concatenate([w_value[0].T, w_attn_out[0], bias_rows], 0),
            ]
        )
        own_u, own_d = w_up[0], w_down[0]
        half_rows = width // 2
        half_t = jnp.concatenate(
            [
                jnp.where(row_bit == 0, w_query[0].T, w_value[0].T),
                jnp.where(row_bit == 0, w_key[0].T, w_attn_out[0]),
                bias_rows,
            ],
            0,
        )
        far_t = swap_heads(half_t, 2)
        near_t = swap_heads(ordered(pack_t, half_t), 1)
        half_u = lax.dynamic_slice_in_dim(own_u, row_bit * half_rows, half_rows, 0)
        half_u, half_t = tie(half_u, half_t)
        far_u = swap_heads(half_u, 2)
        half_d = lax.dynamic_slice_in_dim(own_d, row_bit * half_rows, half_rows, 0)
        half_d, half_u = tie(half_d, half_u)
        far_d = swap_heads(half_d, 2)
        cls_rows = cls_table[labels.reshape(-1)].astype(F32)
        patches_t = patches.T
        hidden0, normed1 = call(
            embed_kernel,
            (
                where, segments, ordered(patches_t, half_d), w_in, b_in[None], pos_table, cls_rows,
                ln1_gain, ln1_bias,
            ),
            [SMEM, SMEM] + [VMEM] * 7,
            (full, low),
            (VMEM, VMEM),
        )
        normed1, far_t = tie(normed1, far_t)
        far_other_t = swap_rows(far_t, 1)
        cross_t = swap_heads(far_t, 1)
        near_u = swap_heads(ordered(own_u, far_t), 1)
        near_d = swap_heads(ordered(own_d, far_t), 1)

        def attend(hidden, normed, parts):
            return call(
                attend_kernel,
                (where, segments, hidden, normed) + parts,
                [SMEM, SMEM, HBM, VMEM] + [HBM] * len(parts),
                (
                    half_low, half_low, half_low,
                    shape(row_count * heads // 2, length, length, dtype=BF), half_low, full,
                ),
                (HBM,) * 5 + (VMEM,),
                [
                    pltpu.VMEM((4, width // 2, width), BF),
                    pltpu.VMEM((row_count, 2, length, length), F32),
                    pltpu.VMEM((tokens, width), F32),
                ]
                + [pltpu.VMEM((tokens, width // 2), BF)] * 3
                + [
                    pltpu.VMEM((row_count * heads // 2, length, length), BF),
                    pltpu.VMEM((tokens, width // 2), BF),
                    dma((8,)),
                    dma((5,)),
                    dma((row_count * heads // 4,)),
                ],
                length=length,
                quarter=quarter,
                count=len(parts),
            )

        parts_near = (pack_t, near_t)
        *saved_near, mixed = attend(hidden0, normed1, parts_near)
        mixed, far_other_t, far_u = tie(mixed, far_other_t, far_u)
        cross_other_t = swap_heads(far_other_t, 1)
        far_other_u = swap_rows(far_u, 1)
        cross_u = swap_heads(far_u, 1)
        parts_far = (far_t, far_other_t, cross_t, cross_other_t)
        *saved_far, hidden1 = attend(mixed, normed1, parts_far)
        hidden1, far_other_u, far_d = tie(hidden1, far_other_u, far_d)
        cross_other_u = swap_heads(far_other_u, 1)
        far_other_d = swap_rows(far_d, 1)
        cross_d = swap_heads(far_d, 1)
        parts_u = (own_u, near_u, far_u, far_other_u, cross_u, cross_other_u)
        four = shape(heads_size, tokens, width, dtype=BF)
        normed2, activated, slope = call(
            up_kernel,
            (where, hidden1, ln2_gain, ln2_bias)
            + parts_u
            + (pack_t, near_t, far_t, cross_t),
            [SMEM] + [VMEM] * 3 + [HBM] * 10,
            (low, four, four),
            (VMEM, HBM, HBM),
            [
                pltpu.VMEM((heads_size, width, width), BF),
                pltpu.VMEM((heads_size, EXTRA, width), BF),
                pltpu.VMEM((heads_size, tokens, width), BF),
                pltpu.VMEM((heads_size, tokens, width), BF),
                dma((4,)),
                dma((4,)),
                dma((2, 4)),
            ],
        )
        normed2, far_other_d = tie(normed2, far_other_d)
        cross_other_d = swap_heads(far_other_d, 1)
        parts_d = (own_d, near_d, far_d, far_other_d, cross_d, cross_other_d)
        pieces = shape(2, PIECES, rows, width, dtype=BF)
        one = shape(PIECES, rows, width, dtype=BF)
        stage = pltpu.VMEM((2, width, width), BF)
        out_sems = dma((2, PIECES))
        latents, logdet, means, tops, direct, grad_hidden2, grad_w_out, gdown, keep_d, *sends_d = call(
            down_kernel,
            (
                where, segments, hidden1, activated, b_down, w_out.T, b_out[:, None], patches_t, latent_grad.T,
                logdet_grad[None],
            )
            + parts_d,
            [SMEM, SMEM, HBM, HBM] + [VMEM] * 6 + [HBM] * 6,
            (
                shape(channels, tokens), shape(1, tokens), shape(1, row_count), shape(1, row_count),
                shape(channels, tokens),
                full, shape(2 * channels, width), shape(8, width), pieces, one, one,
            ),
            (VMEM,) * 8 + (HBM,) * 3,
            [
                pltpu.VMEM((heads_size, width, width), BF),
                pltpu.VMEM((heads_size, tokens, width), BF),
                pltpu.VMEM((tokens, width), F32),
                pltpu.VMEM((tokens, width), BF),
                stage,
                pltpu.VMEM((tokens, width), F32),
                dma((4,)),
                dma((4,)),
                out_sems,
                dma(()),
            ],
            length=length,
            quarter=quarter,
        )
        chains = [Chain(order) for order in CHAIN_ORDERS]
        down, up, mix, last = chains

        def add_groups(*groups):
            def spec(view, start):
                size = view.size
                block = (view.array.shape[3] // 2, view.array.shape[4])

                def at(i):
                    return tuple(a // b for a, b in zip(start, size)) + (i, 0)

                return pl.BlockSpec(size + block, at)

            views = [view for group in groups for view in group]
            return pl.pallas_call(
                functools.partial(add_kernel, counts=tuple(len(group) for group in groups)),
                grid=(2,),
                in_specs=[spec(view, view.start) for view in views],
                out_specs=[spec(group[0], (0, 0, 0)) for group in groups],
                out_shape=[shape(*group[0].size, *group[0].array.shape[3:], dtype=BF) for group in groups],
                compiler_params=pltpu.CompilerParams(vmem_limit_bytes=60 << 20),
                cost_estimate=pl.CostEstimate(flops=1, transcendentals=0, bytes_accessed=1),
            )(*(view.array for view in views))

        def halves(chain, keep, gots):
            keep = chain.view(keep)
            return [[keep.narrow(0, index), chain.view(got)] for index, got in enumerate(gots)]

        grad_hidden2, *sends_d = tie(grad_hidden2, *sends_d)
        got_d = [swap_heads(send, 1) for send in sends_d]
        pre_grads, gpre = call(
            grad_pre_kernel,
            (where, grad_hidden2, slope) + parts_d,
            [SMEM, VMEM, HBM] + [HBM] * 6,
            (four, shape(8, width)),
            (HBM, VMEM),
            [
                pltpu.VMEM((heads_size, width, width), BF),
                pltpu.VMEM((heads_size, tokens, width), BF),
                pltpu.VMEM((tokens, width), BF),
                pltpu.VMEM((heads_size, tokens, width), BF),
                dma((4,)),
                dma((4,)),
                dma((4,)),
            ],
        )
        pre_grads, *got_d = tie(pre_grads, *got_d)
        down.groups = halves(down, keep_d, got_d)
        pre_grads, *sends = tie(pre_grads, *add_groups(*down.parts()))
        down.launch(sends)
        grad_hidden1, grad_mix, gup, keep_u, *sends_u = call(
            up_back_kernel,
            (where, grad_hidden2, pre_grads, normed2, hidden1, ln2_gain) + parts_u,
            [SMEM, HBM, HBM, VMEM, HBM, VMEM] + [HBM] * 6,
            (full, low, shape(8, width), pieces, one, one),
            (VMEM, VMEM, VMEM, HBM, HBM, HBM),
            [
                pltpu.VMEM((heads_size, width, width), BF),
                pltpu.VMEM((heads_size, tokens, width), BF),
                pltpu.VMEM((tokens, width), F32),
                stage,
                pltpu.VMEM((tokens, width), F32),
                pltpu.VMEM((tokens, width), F32),
                dma((4,)),
                dma((4,)),
                out_sems,
                dma((2,)),
            ],
        )
        grad_mix, *sends_u = tie(grad_mix, *sends_u)
        got_u = [swap_heads(send, 1) for send in sends_u]

        def attend_back(saved, parts, before):
            chained = () if before is None else (before,)
            mixed_pieces = shape(PIECES, 3 * unit, width, dtype=BF)
            return call(
                attend_back_kernel,
                (where, grad_mix) + tuple(saved) + (normed1,) + chained + parts,
                [SMEM] + [HBM] * (7 + len(chained) + len(parts)),
                (full, shape(width // 2, width, dtype=BF), mixed_pieces, mixed_pieces),
                (VMEM, VMEM, HBM, HBM),
                [pltpu.VMEM((4, width // 2, width), BF)]
                + [pltpu.VMEM((tokens, width // 2), BF)] * 4
                + [pltpu.VMEM((3, width // 2, width), BF), dma((8,)), dma((3, 2 * PIECES))]
                + [pltpu.VMEM((tokens, width), BF)]
                + [pltpu.VMEM((tokens, width // 2), BF)] * 3
                + [
                    pltpu.VMEM((row_count * heads // 2, length, length), BF),
                    pltpu.VMEM((tokens, width // 2), BF),
                    pltpu.VMEM((tokens, width), BF),
                    pltpu.VMEM((tokens, width), F32),
                    dma((8,)),
                ],
                length=length,
                quarter=quarter,
                count=len(parts),
                chained=before is not None,
            )

        total_far, gq_far, keep_far, send_far = attend_back(saved_far, parts_far, None)
        total_far, send_far, *got_d = tie(total_far, send_far, *down.got)
        total_far, *got_u = tie(total_far, *got_u)
        got_far = swap_heads(send_far, 1)
        down.deliver(got_d)
        up.groups = halves(up, keep_u, got_u)
        total_far, *sends = tie(total_far, *add_groups(*down.parts(), *up.parts()))
        down.launch(sends[:1])
        up.launch(sends[1:])
        total_near, gq_near, keep_near, send_near = attend_back(saved_near, parts_near, total_far)
        total_near, send_near, got_far, *got_d = tie(total_near, send_near, got_far, *down.got)
        got_near = swap_heads(send_near, 1)
        mix.groups = [[], [mix.view(keep_far), mix.view(got_far)]]
        down.deliver(got_d)
        grad_hidden1, *sends = tie(grad_hidden1, *add_groups(*down.parts(), *mix.parts()))
        down.launch(sends[:1])
        mix.launch(sends[1:])
        groups = 4 * PIECES
        last_pieces = shape(2, PIECES, unit + GROUP, width, dtype=BF)
        patches_grad, slot_rows, keep_q, send_q = call(
            embed_back_kernel,
            (
                where, segments, labels, grad_hidden1, total_near, hidden0, ln1_gain, patches_t,
                direct, w_in, grad_w_out, gdown, gup, gpre, gq_near, gq_far,
            ),
            [SMEM] * 3 + [HBM] * 3 + [VMEM] * 10,
            (shape(channels, tokens), shape(row_count * slot_count, width + 128), last_pieces, last_pieces),
            (VMEM, VMEM, HBM, HBM),
            [
                pltpu.VMEM((tokens, width), F32),
                pltpu.VMEM((tokens, width), BF),
                pltpu.VMEM((EXTRA, width), F32),
                pltpu.VMEM((groups * GROUP, width), BF),
                pltpu.VMEM((tokens, width), F32),
                pltpu.VMEM((tokens, width), F32),
                pltpu.VMEM((tokens, width), F32),
                dma((2, groups)),
                dma((6,)),
            ],
            length=length,
            quarter=quarter,
        )
        patches_grad, *got_u = tie(patches_grad, *up.got)
        patches_grad, *got_d = tie(patches_grad, *down.got)
        patches_grad, send_q = tie(patches_grad, send_q)
        last.groups = [[last.view(keep_q), last.view(swap_heads(send_q, 1))]]
        mix.groups[0] = [mix.view(keep_near), mix.view(got_near)]
        down.got, up.got = got_d, got_u
        gathered = slot_rows.astype(BF)
        gathers = [("rows", 1 << level) for level in reversed(range(levels))]
        gathers += [("heads", 2), ("heads", 1)]
        share = (len(gathers) - 1) // 4
        token = got_d[0]
        pending = {0, 1, 2}
        heads_left = [2, 1]
        got = None
        small = None
        for index in TAIL:
            if index == 4:
                more = gathers[:share] if len(gathers) > 2 + share else gathers[:1]
                for axis, bit in more:
                    gathers.pop(0)
                    if got is not None:
                        gathered = jnp.concatenate([gathered, ordered(got, token)], 0)
                    token = gathered = ordered(gathered, token)
                    got = (swap_rows if axis == "rows" else swap_heads)(gathered, bit)
                continue
            if index == 5:
                if small is None:
                    last.deliver([ordered(more, token) for more in last.got])
                    axis = Chain.axes[[a for a in last.order if a != "y"][0]] - 1
                    small = jnp.concatenate([last.low[:, :, unit:], last.high[:, :, unit:]], axis)
                    small = small.reshape(1, PIECES, GROUP, width)
                token = small = ordered(small, token)
                small_got = swap_heads(small, heads_left.pop(0))
                if heads_left:
                    small = jnp.concatenate([small, small_got], 0)
                continue
            chain = chains[index]
            if index in pending:
                chain.deliver([ordered(one, token) for one in chain.got])
            pending.add(index)
            sends = []
            for send in chain.prepare():
                token = ordered(send, token)
                sends.append(token)
            chain.launch(sends)
        gathered = jnp.concatenate([gathered, got], 0)
        for axis, bit in gathers:
            swap = swap_rows if axis == "rows" else swap_heads
            gathered = jnp.concatenate([gathered, swap(gathered, bit)], 0)
        for chain in chains[:3]:
            chain.deliver(chain.got)
        gathered = gathered.reshape(-1, width + 128)
        digits = gathered[:, width : width + 2].astype(jnp.int32)
        slot_label = digits[:, 0] * 32 + digits[:, 1]
        label_onehot = (
            lax.broadcasted_iota(jnp.int32, (classes, 1), 0) == slot_label[None, :]
        ).astype(BF)
        sum_cls = nn(label_onehot, gathered[:, :width])

        def place(chain):
            return call(
                place_kernel,
                (where, chain.low, chain.high),
                [SMEM, HBM, HBM],
                shape(width, width),
                HBM,
                [
                    pltpu.VMEM(chain.low.shape, BF),
                    pltpu.VMEM(chain.high.shape, BF),
                    pltpu.VMEM((PIECES, rows, width), F32),
                    dma((2,)),
                    dma((PIECES,)),
                ],
            )

        sum_down, sum_up = place(down), place(up)
        units = shape(part, width)
        line = shape(1, width)
        sum_k, sum_v, sum_o, sum_q, sum_w_in, sum_w_out, sum_pos, *lines = call(
            place_last_kernel,
            (where, mix.low, mix.high, last.low, last.high, small, small_got),
            [SMEM] + [VMEM] * 6,
            (units,) * 4
            + (shape(channels, width), shape(2 * channels, width), shape(length, width))
            + (shape(width // 128, 128),)
            + (line,) * 6
            + (shape(1, 2 * channels),),
            (VMEM,) * 15,
            [pltpu.VMEM((groups * GROUP, width), F32)],
        )
        sum_b_in, sum_gain1, sum_bias1, sum_gain2, sum_bias2, sum_b_down, sum_b_up, sum_b_out = lines
        return (
            latents.T,
            logdet.reshape(tokens),
            patches_grad.T,
            means.reshape(row_count),
            tops.reshape(row_count),
            sum_w_in,
            sum_b_in.reshape(width),
            sum_pos,
            sum_cls,
            sum_gain1,
            sum_bias1,
            sum_q.T[None],
            sum_k.T[None],
            sum_v.T[None],
            sum_o[None],
            sum_gain2,
            sum_bias2,
            sum_up[None],
            sum_b_up,
            sum_down[None],
            sum_b_down,
            sum_w_out.T,
            sum_b_out.reshape(2 * channels),
        )

    return program


def solution(mesh):
    tokens = P(("rows", "heads"))
    tokens2 = P(("rows", "heads"), None)
    last = P(None, None, "heads")
    middle = P(None, "heads", None)
    in_specs = (
        (tokens2, P("rows"), tokens2)
        + (P(),) * 6
        + (last, last, last, middle)
        + (P(), P(), last, P(None, "heads"), middle, P(), P(), P())
        + (tokens2, tokens)
    )
    out_specs = (
        (tokens2, tokens, tokens2, tokens, tokens)
        + (P(),) * 6
        + (last, last, last, middle)
        + (P(), P(), last, P(None, "heads"), middle, P(), P(), P())
    )
    program = make_program(mesh.shape["rows"], mesh.shape["heads"])
    return jax.shard_map(
        program, mesh=mesh, in_specs=in_specs, out_specs=out_specs, check_vma=False
    )
```

```python
import functools

import jax
import jax.numpy as jnp
from jax import lax
from jax.experimental import pallas as pl
from jax.experimental.pallas import tpu as pltpu
from jax.sharding import PartitionSpec as P

HEAD_DIM = 64
EPSILON = 1e-05
SCALE = HEAD_DIM**-0.5
BF = jnp.bfloat16
F32 = jnp.float32
PIECES = 4
EXTRA = 16
GROUP = 32
CHUNK = 64
GATHER_ROWS = 32
CHAIN_ORDERS = ("yxz", "zxy", "yxz", "zyx")
TAIL = (0, 1, 3, 1, 3, 2, 4, 1, 3, 2, 3, 4, 2, 0, 3, 4, 1, 3, 4, 2, 0, 4, 5, 1, 2, 5)

VMEM = pl.BlockSpec(memory_space=pltpu.VMEM)
SMEM = pl.BlockSpec(memory_space=pltpu.SMEM)
HBM = pl.BlockSpec(memory_space=pl.ANY)


def nn(matrix, other):
    return lax.dot_general(matrix, other, (((1,), (0,)), ((), ())), preferred_element_type=F32)


def tn(matrix, other):
    return lax.dot_general(matrix, other, (((0,), (0,)), ((), ())), preferred_element_type=F32)


def nt(matrix, other):
    return lax.dot_general(matrix, other, (((1,), (1,)), ((), ())), preferred_element_type=F32)


def norm_parts(values):
    average = jnp.mean(values, -1, keepdims=True)
    centered = values - average
    spread = jnp.mean(centered * centered, -1, keepdims=True)
    rstd = lax.rsqrt(spread + EPSILON)
    return centered * rstd, rstd


def norm_back(grad, gain, xhat, rstd):
    scaled = grad * gain
    back = scaled - jnp.mean(scaled, -1, keepdims=True)
    back = back - xhat * jnp.mean(scaled * xhat, -1, keepdims=True)
    return rstd * back


def column_sum(values):
    return jnp.sum(values, 0, keepdims=True)


def over_rows(tokens, body, first=0):
    def step(index, carry):
        body(pl.ds(pl.multiple_of(index * CHUNK, CHUNK), CHUNK))
        return carry

    lax.fori_loop(first // CHUNK, tokens // CHUNK, step, 0)


def gelu_pair(values):
    scaled = jnp.abs(values) * 0.7071067811865476
    base = 1.0 + 0.3275911 * scaled
    t = pl.reciprocal(base, approx=True)
    t = t * (2.0 - base * t)
    bell = jnp.exp(-0.5 * values * values)
    poly = 1.061405429 * t - 1.453152027
    poly = poly * t + 1.421413741
    poly = poly * t - 0.284496736
    poly = poly * t + 0.254829592
    tail = 0.5 * poly * t * bell
    below = jnp.where(values >= 0.0, 1.0 - tail, tail)
    return values * below, below + values * bell * 0.3989422804014327


def packed_flag(where_ref, seg_ref, row, length):
    start = where_ref[0] + row * length
    return seg_ref[start + length - 1] > 0


def embed_kernel(
    where_ref, seg_ref, patch_ref, w_ref, b_ref, pos_ref, cls_ref, gain_ref, bias_ref, hid_ref, norm_ref
):
    tokens, width = hid_ref.shape
    length = pos_ref.shape[0]
    slots = cls_ref.shape[0] // (tokens // length)
    quarter = length // slots
    hid_ref[...] = tn(patch_ref[...].astype(BF), w_ref[...]) + b_ref[...]
    for row in range(tokens // length):
        packed = packed_flag(where_ref, seg_ref, row, length)
        for slot in range(slots):
            at = slice(row * length + slot * quarter, row * length + (slot + 1) * quarter)
            here = pos_ref[slot * quarter : (slot + 1) * quarter].astype(F32)
            first = pos_ref[:quarter].astype(F32)
            one = cls_ref[row * slots + slot : row * slots + slot + 1]
            start = cls_ref[row * slots : row * slots + 1]
            value = hid_ref[at] + jnp.where(packed, first, here) + jnp.where(packed, one, start)
            hid_ref[at] = value
            xhat, _ = norm_parts(value)
            norm_ref[at] = (xhat * gain_ref[...] + bias_ref[...]).astype(BF)


def fetch_kind(where_ref, parts, weight_ref, sems, kind):
    unit = weight_ref.shape[1] // 2
    half, rows = kind // 2, pl.ds(unit * (kind % 2), unit)
    for slot in range(2):
        target, sem = weight_ref.at[kind, pl.ds(unit * slot, unit)], sems.at[2 * kind + slot]
        if len(parts) == 2:
            pltpu.make_async_copy(parts[slot].at[half, rows], target, sem).start()
            continue
        for other in range(2):

            @pl.when((where_ref[1] == half) == (other == 0))
            def _():
                pltpu.make_async_copy(parts[2 * slot + other].at[rows], target, sem).start()


def wait_kind(weight_ref, sems, kind):
    unit = weight_ref.shape[1] // 2
    for slot in range(2):
        target = weight_ref.at[kind, pl.ds(unit * slot, unit)]
        pltpu.make_async_copy(target, target, sems.at[2 * kind + slot]).wait()


def start_copies(copies, sems):
    made = [pltpu.make_async_copy(src, dst, sems.at[i]) for i, (src, dst) in enumerate(copies)]
    for copy in made:
        copy.start()
    return made


def fetch_full(where_ref, parts, weight_ref, sems):
    own, near, far, far_other, cross, cross_other = parts
    half = weight_ref.shape[1] // 2
    mine = pl.ds(pl.multiple_of(where_ref[1] * half, half), half)
    other = pl.ds(pl.multiple_of((1 - where_ref[1]) * half, half), half)
    copies = [
        (own, weight_ref.at[0], 0),
        (near, weight_ref.at[1], 1),
        (far, weight_ref.at[2, mine], 2),
        (far_other, weight_ref.at[2, other], 2),
        (cross, weight_ref.at[3, mine], 3),
        (cross_other, weight_ref.at[3, other], 3),
    ]
    for source, target, slot in copies:
        pltpu.make_async_copy(source, target, sems.at[slot]).start()


def wait_slot(source, into_ref, sems, slot):
    pltpu.make_async_copy(source, into_ref.at[slot], sems.at[slot]).wait()


def mask_bias(packed, quarter, length, part):
    block = length // 2
    q = (lax.broadcasted_iota(jnp.int32, (length, length), 1) & (block - 1)) + part * block
    k = lax.broadcasted_iota(jnp.int32, (length, length), 0)
    shift = quarter.bit_length() - 1
    same = (q >> shift) == (k >> shift)
    return jnp.where((k <= q) & (same | jnp.logical_not(packed)), 0.0, -1e30)


def by_head(values, lanes):
    return jnp.concatenate([values * lanes[0], values * lanes[1]], 0)


def own_lanes(values):
    block = values.shape[0] // 2
    lane = lax.broadcasted_iota(jnp.int32, (1, 128), 1)
    return jnp.where(lane < HEAD_DIM, values[:block], values[block:])


def head_lanes(value):
    lane = lax.broadcasted_iota(jnp.int32, (1, 128), 1)
    return [jnp.where(side, value, 0.0).astype(BF) for side in (lane < HEAD_DIM, lane >= HEAD_DIM)]


def attend_kernel(where_ref, seg_ref, hid_in, norm_ref, *rest, length, quarter, count):
    parts = rest[:count]
    (
        q_out, k_out, v_out, prob_out, att_out, out_ref,
        weight_ref, bias_ref, hid_ref, q_ref, k_ref, v_ref, prob_ref, att_ref, sems, io_sems, prob_sems,
    ) = rest[count:]
    tokens = hid_ref.shape[0]
    for kind in range(4):
        fetch_kind(where_ref, parts, weight_ref, sems, kind)
    moves = [
        pltpu.make_async_copy(source, target, io_sems.at[index])
        for index, (source, target) in enumerate(
            ((hid_in, hid_ref), (q_ref, q_out), (k_ref, k_out), (v_ref, v_out), (att_ref, att_out))
        )
    ]
    moves[0].start()
    for row in range(tokens // length):
        for part in range(2):
            packed = packed_flag(where_ref, seg_ref, row, length)
            bias_ref[row, part] = mask_bias(packed, quarter, length, part)
    for kind, ref in enumerate((q_ref, k_ref, v_ref)):
        wait_kind(weight_ref, sems, kind)
        ref[...] = nt(norm_ref[...], weight_ref[kind]).astype(BF)
        moves[1 + kind].start()
    pairs = q_ref.shape[1] // 128
    scaled = head_lanes(SCALE)
    block = length // 2

    def step(index, carry):
        row = index // pairs
        pair = index % pairs
        lanes = pl.ds(pl.multiple_of(pair * 128, 128), 128)
        for part in range(2):
            keys = (part + 1) * block
            here = pl.ds(pl.multiple_of(row * length + part * block, block), block)
            upto = pl.ds(pl.multiple_of(row * length, length), keys)
            queries = q_ref[here, lanes]
            key_rows = k_ref[upto, lanes]
            values = v_ref[upto, lanes]
            scores = nt(key_rows, by_head(queries, scaled)) + bias_ref[row, part, :keys]
            top = jnp.max(scores, 0, keepdims=True)
            grown = jnp.exp(scores - top)
            probs = (grown * (1.0 / jnp.sum(grown, 0, keepdims=True))).astype(BF)
            prob_ref[2 * index + part, :keys] = probs
            result = own_lanes(tn(probs, values))
            att_ref[here, lanes] = result.astype(BF)
        both = pl.ds(2 * index, 2)
        pltpu.make_async_copy(prob_ref.at[both], prob_out.at[both], prob_sems.at[index]).start()
        return carry

    lax.fori_loop(0, tokens // length * pairs, step, 0)
    moves[4].start()
    moves[0].wait()
    wait_kind(weight_ref, sems, 3)
    out_ref[...] = hid_ref[...] + nn(att_ref[...], weight_ref[3])
    for move in moves[1:]:
        move.wait()
    for index in range(tokens // length * pairs):
        both = slice(2 * index, 2 * index + 2)
        pltpu.make_async_copy(prob_ref.at[both], prob_out.at[both], prob_sems.at[index]).wait()


def up_kernel(
    where_ref, hid_ref, gain_ref, bias_ref, own, near, far, far_other, cross, cross_other,
    own_t, near_t, far_t, cross_t,
    norm_ref, act_out, slope_out, weight_ref, bup_ref, act_ref, slope_ref, sems, bias_sems, out_sems,
):
    tokens, width = hid_ref.shape
    fetch_full(where_ref, (own, near, far, far_other, cross, cross_other), weight_ref, sems)
    last = pl.ds(far_t.shape[0] - EXTRA, EXTRA)
    packs = (own_t.at[0, last], near_t.at[0, last], far_t.at[last], cross_t.at[last])
    biases = start_copies([(pack, bup_ref.at[slot]) for slot, pack in enumerate(packs)], bias_sems)

    def normalize(at):
        xhat, _ = norm_parts(hid_ref[at])
        norm_ref[at] = (xhat * gain_ref[...] + bias_ref[...]).astype(BF)

    over_rows(tokens, normalize)
    for bias in biases:
        bias.wait()
    block = 128

    def step(slot, carry):
        wait_slot(own, weight_ref, sems, slot)
        bias = bup_ref[slot, :1].astype(F32)
        for first in range(0, tokens, block):
            at = slice(first, first + block)
            pre = nn(norm_ref[at], weight_ref[slot]) + bias
            value, slope = gelu_pair(pre)
            act_ref[slot, at] = value.astype(BF)
            slope_ref[slot, at] = slope.astype(BF)
        pltpu.make_async_copy(act_ref.at[slot], act_out.at[slot], out_sems.at[0, slot]).start()
        pltpu.make_async_copy(slope_ref.at[slot], slope_out.at[slot], out_sems.at[1, slot]).start()
        return carry

    lax.fori_loop(0, 4, step, 0)
    for slot in range(4):
        pltpu.make_async_copy(act_ref.at[slot], act_out.at[slot], out_sems.at[0, slot]).wait()
        pltpu.make_async_copy(slope_ref.at[slot], slope_out.at[slot], out_sems.at[1, slot]).wait()


def send_pieces(where_ref, stage_ref, slot, keep, sends, sems, rows):
    for piece in range(PIECES):
        source = stage_ref.at[piece * rows : (piece + 1) * rows]
        target = piece ^ where_ref[2]

        @pl.when(slot % 2 == 0)
        def _():
            pltpu.make_async_copy(source, keep.at[slot // 2, target], sems.at[piece]).start()

        for index, send in enumerate(sends):

            @pl.when(slot == 2 * index + 1)
            def _():
                pltpu.make_async_copy(source, send.at[target], sems.at[piece]).start()


def wait_pieces(stage_ref, keep, sems, rows):
    for piece in range(PIECES):
        source = stage_ref.at[piece * rows : (piece + 1) * rows]
        pltpu.make_async_copy(source, keep.at[0, 0, :rows], sems.at[piece]).wait()


def down_kernel(
    where_ref, seg_ref, hid_in, act_in, bdown_ref, wout_ref, bout_ref, patch_ref, lgrad_ref, dgrad_ref,
    own, near, far, far_other, cross, cross_other,
    latent_ref, logdet_ref, mean_ref, max_ref, direct_ref, grad_ref, gwout_ref, gvec_ref, keep_ref, send_near, send_far,
    weight_ref, act_ref, total_ref, branch_ref, stage_ref, hid_ref, sems, act_sems, out_sems, hid_sem,
    *, length, quarter,
):
    tokens, width = total_ref.shape
    channels = patch_ref.shape[0]
    send_refs = (send_near, send_far)
    start_copies([(act_in.at[slot], act_ref.at[slot]) for slot in range(4)], act_sems)
    fetch_full(where_ref, (own, near, far, far_other, cross, cross_other), weight_ref, sems)
    hidden = pltpu.make_async_copy(hid_in, hid_ref, hid_sem)
    hidden.start()
    total_ref[...] = jnp.zeros(total_ref.shape, F32)

    def gather(slot, carry):
        wait_slot(act_in.at[slot], act_ref, act_sems, slot)
        wait_slot(own, weight_ref, sems, slot)
        total_ref[...] += nn(act_ref[slot], weight_ref[slot])
        return carry

    lax.fori_loop(0, 4, gather, 0)
    hidden.wait()
    top_low = (total_ref[...] + hid_ref[...] + bdown_ref[...]).astype(BF)
    head_out = nt(wout_ref[...], top_low) + bout_ref[...]
    token = lax.broadcasted_iota(jnp.int32, (1, tokens), 1)
    row_count = tokens // length
    starts = jnp.zeros((1, tokens), jnp.bool_)
    for row in range(row_count):
        packed = packed_flag(where_ref, seg_ref, row, length)
        inside = (token >= row * length) & (token < (row + 1) * length)
        fresh = (token & jnp.where(packed, quarter - 1, length - 1)) == 0
        starts = starts | (inside & fresh)
    previous = jnp.where(starts, 0.0, pltpu.roll(head_out, 1, 1))
    shifts = previous[:channels]
    logscale = previous[channels:]
    shrink = jnp.exp(-logscale)
    latents = (patch_ref[...] - shifts) * shrink
    latent_ref[...] = latents
    logdet_ref[...] = -column_sum(logscale)
    lane = lax.broadcasted_iota(jnp.int32, mean_ref.shape, 1)
    means = jnp.zeros(mean_ref.shape, F32)
    tops = means
    for row in range(row_count):
        part = logscale[:, row * length : (row + 1) * length]
        means = jnp.where(lane == row, jnp.sum(part) * (1.0 / (length * channels)), means)
        tops = jnp.where(lane == row, jnp.max(part), tops)
    mean_ref[...] = means
    max_ref[...] = tops
    lgrad = lgrad_ref[...]
    direct = lgrad * shrink
    direct_ref[...] = direct
    grad_prev = jnp.concatenate([-direct, -lgrad * latents - dgrad_ref[...]], 0)
    grad_prev = jnp.where(starts, 0.0, grad_prev)
    grad_head = pltpu.roll(grad_prev, tokens - 1, 1).astype(BF)
    gwout_ref[...] = nn(grad_head, top_low)
    grad_hidden = tn(grad_head, wout_ref[...])
    grad_ref[...] = grad_hidden
    branch_ref[...] = grad_hidden.astype(BF)
    gvec_ref[...] = jnp.zeros(gvec_ref.shape, F32)
    gvec_ref[0:1, :] = column_sum(grad_hidden)
    row_of = nt(jnp.ones((8, tokens), BF), grad_head)
    gvec_ref[1:2, : 2 * channels] = row_of[:1]
    rows = width // PIECES


    def step(slot, carry):
        @pl.when(slot >= 2)
        def _():
            wait_pieces(stage_ref.at[slot % 2], keep_ref, out_sems.at[slot % 2], rows)

        stage_ref[slot % 2] = tn(act_ref[slot], branch_ref[...]).astype(BF)
        send_pieces(where_ref, stage_ref.at[slot % 2], slot, keep_ref, send_refs, out_sems.at[slot % 2], rows)
        return carry

    lax.fori_loop(0, 4, step, 0)
    for slot in range(2):
        wait_pieces(stage_ref.at[slot], keep_ref, out_sems.at[slot], rows)


def grad_pre_kernel(
    where_ref, grad_ref, slope_in, own, near, far, far_other, cross, cross_other,
    pre_out, sum_ref, weight_ref, slope_ref, branch_ref, pre_ref, sems, slope_sems, out_sems,
):
    start_copies([(slope_in.at[slot], slope_ref.at[slot]) for slot in range(4)], slope_sems)
    fetch_full(where_ref, (own, near, far, far_other, cross, cross_other), weight_ref, sems)
    branch_ref[...] = grad_ref[...].astype(BF)

    def step(slot, carry):
        wait_slot(slope_in.at[slot], slope_ref, slope_sems, slot)
        wait_slot(own, weight_ref, sems, slot)
        grad_pre = (nt(branch_ref[...], weight_ref[slot]) * slope_ref[slot].astype(F32)).astype(BF)
        pre_ref[slot] = grad_pre
        pltpu.make_async_copy(pre_ref.at[slot], pre_out.at[slot], out_sems.at[slot]).start()
        sum_ref[pl.ds(slot, 1), :] = column_sum(grad_pre.astype(F32))
        return carry

    lax.fori_loop(0, 4, step, 0)
    for slot in range(4):
        pltpu.make_async_copy(pre_ref.at[slot], pre_out.at[slot], out_sems.at[slot]).wait()


def up_back_kernel(
    where_ref, grad_in, pre_in, norm_ref, hid_in, gain_ref, own, near, far, far_other, cross, cross_other,
    gout_ref, mix_ref, gvec_ref, keep_ref, send_near, send_far,
    weight_ref, pre_ref, total_ref, stage_ref, grad_ref, hid_ref, sems, pre_sems, out_sems, late_sems,
):
    tokens, width = grad_ref.shape
    send_refs = (send_near, send_far)
    start_copies([(pre_in.at[slot], pre_ref.at[slot]) for slot in range(4)], pre_sems)
    late = start_copies([(grad_in, grad_ref), (hid_in, hid_ref)], late_sems)
    total_ref[...] = jnp.zeros(total_ref.shape, F32)
    fetch_full(where_ref, (own, near, far, far_other, cross, cross_other), weight_ref, sems)
    gvec_ref[...] = jnp.zeros(gvec_ref.shape, F32)
    rows = width // PIECES

    def step(slot, carry):
        @pl.when(slot >= 2)
        def _():
            wait_pieces(stage_ref.at[slot % 2], keep_ref, out_sems.at[slot % 2], rows)

        wait_slot(pre_in.at[slot], pre_ref, pre_sems, slot)
        wait_slot(own, weight_ref, sems, slot)
        stage_ref[slot % 2] = tn(norm_ref[...], pre_ref[slot]).astype(BF)
        send_pieces(where_ref, stage_ref.at[slot % 2], slot, keep_ref, send_refs, out_sems.at[slot % 2], rows)
        total_ref[...] += nt(pre_ref[slot], weight_ref[slot])
        return carry

    lax.fori_loop(0, 4, step, 0)

    def finish(at):
        xhat, rstd = norm_parts(hid_ref[at])
        grad = total_ref[at]
        value = grad_ref[at] + norm_back(grad, gain_ref[...], xhat, rstd)
        gout_ref[at] = value
        mix_ref[at] = value.astype(BF)
        gvec_ref[0:1, :] += column_sum(grad * xhat)
        gvec_ref[1:2, :] += column_sum(grad)

    for copy in late:
        copy.wait()
    over_rows(tokens, finish)
    for slot in range(2):
        wait_pieces(stage_ref.at[slot], keep_ref, out_sems.at[slot], rows)


def attend_back_kernel(
    where_ref, mix_in, q_in, k_in, v_in, prob_in, att_in, norm_in, *rest, length, quarter, count, chained
):
    before_in = rest[0] if chained else None
    rest = rest[1:] if chained else rest
    parts = rest[:count]
    (
        total_ref, gq_ref, keep_ref, send_ref,
        weight_ref, gatt_ref, dq_ref, dk_ref, dv_ref, stage_ref, sems, out_sems,
        mix_ref, q_ref, k_ref, v_ref, prob_ref, att_ref, norm_ref, before_ref, in_sems,
    ) = rest[count:]
    tokens = mix_ref.shape[0]
    fetch_kind(where_ref, parts, weight_ref, sems, 3)
    moves = [
        (mix_in, mix_ref), (att_in, att_ref), (q_in, q_ref), (k_in, k_ref), (v_in, v_ref), (prob_in, prob_ref),
        (norm_in, norm_ref),
    ]
    moves = start_copies(moves + ([(before_in, before_ref)] if chained else []), in_sems)
    for kind in range(3):
        fetch_kind(where_ref, parts, weight_ref, sems, kind)
    moves[0].wait()
    wait_kind(weight_ref, sems, 3)
    gatt_ref[...] = nt(mix_ref[...], weight_ref[3]).astype(BF)
    pairs = q_ref.shape[1] // 128
    lefts = head_lanes(1.0)
    scaled = head_lanes(SCALE)
    block = length // 2
    unit = weight_ref.shape[1] // 2
    rows = unit // PIECES

    def publish(kind, left, right):
        stage_ref[kind] = tn(left, right).astype(BF)
        for slot, into in enumerate((keep_ref, send_ref)):
            for piece in range(PIECES):
                at = slot * unit + piece * rows
                pltpu.make_async_copy(
                    stage_ref.at[kind, at : at + rows],
                    into.at[piece ^ where_ref[2], kind * rows : (kind + 1) * rows],
                    out_sems.at[kind, slot * PIECES + piece],
                ).start()

    moves[1].wait()
    publish(2, att_ref[...], mix_ref[...])
    for move in moves[2:6]:
        move.wait()

    def step(index, carry):
        row = index // pairs
        pair = index % pairs
        lanes = pl.ds(pl.multiple_of(pair * 128, 128), 128)
        grads_k = [None, None]
        grads_v = [None, None]
        for part in range(2):
            keys = (part + 1) * block
            here = pl.ds(pl.multiple_of(row * length + part * block, block), block)
            upto = pl.ds(pl.multiple_of(row * length, length), keys)
            queries = q_ref[here, lanes]
            key_rows = k_ref[upto, lanes]
            values = v_ref[upto, lanes]
            grad_out = gatt_ref[here, lanes]
            probs = prob_ref[2 * index + part, :keys]
            wide = probs.astype(F32)
            grad_both = by_head(grad_out, lefts)
            grad_probs = nt(values, grad_both)
            inner = jnp.sum(wide * grad_probs, 0, keepdims=True)
            grad_scores = (wide * (grad_probs - inner)).astype(BF)
            result = own_lanes(tn(grad_scores, key_rows)) * SCALE
            grads_k[part] = nn(grad_scores, by_head(queries, scaled))
            grads_v[part] = nn(probs, grad_both)
            dq_ref[here, lanes] = result.astype(BF)
        low = pl.ds(pl.multiple_of(row * length, length), block)
        high = pl.ds(pl.multiple_of(row * length + block, block), block)
        dk_ref[low, lanes] = (grads_k[0] + grads_k[1][:block]).astype(BF)
        dk_ref[high, lanes] = grads_k[1][block:].astype(BF)
        dv_ref[low, lanes] = (grads_v[0] + grads_v[1][:block]).astype(BF)
        dv_ref[high, lanes] = grads_v[1][block:].astype(BF)
        return carry

    lax.fori_loop(0, tokens // length * pairs, step, 0)
    moves[6].wait()
    publish(0, dk_ref[...], norm_ref[...])
    publish(1, dv_ref[...], norm_ref[...])
    gq_ref[...] = tn(dq_ref[...], norm_ref[...]).astype(BF)
    for kind in range(3):
        wait_kind(weight_ref, sems, kind)
    total = nn(dq_ref[...], weight_ref[0]) + nn(dk_ref[...], weight_ref[1]) + nn(dv_ref[...], weight_ref[2])
    if chained:
        moves[7].wait()
        total = total + before_ref[...]
    total_ref[...] = total
    for kind in range(3):
        for piece in range(2 * PIECES):
            pltpu.make_async_copy(
                stage_ref.at[kind, :rows], keep_ref.at[0, :rows], out_sems.at[kind, piece]
            ).wait()


def embed_back_kernel(
    where_ref, seg_ref, label_ref, grad_in, total_in, hid_in, gain_ref, patch_ref, direct_ref, win_ref,
    gwout_ref, gdown_ref, gup_ref, gpre_ref, gq_near, gq_far,
    pgrad_ref, slot_ref, keep_ref, send_ref,
    value_ref, embed_ref, acc_ref, small_ref, rows_ref, grad_ref, total_ref, hid_ref, sems, in_sems,
    *, length, quarter,
):
    tokens, width = hid_ref.shape
    half = tokens // 2
    moves = [
        (source.at[first : first + half], target.at[first : first + half])
        for first in (0, half)
        for source, target in ((grad_in, grad_ref), (total_in, total_ref), (hid_in, hid_ref))
    ]
    moves = start_copies(moves, in_sems)
    channels = patch_ref.shape[0]
    unit = width // 4
    rows = unit // PIECES
    sources = []
    for slot in range(4):
        source = (gq_near, gq_far)[slot // 2]
        into = (keep_ref, send_ref)[slot % 2]
        for piece in range(PIECES):
            at = (slot % 2) * unit + piece * rows
            sources.append((source.at[at : at + rows], into.at[slot // 2, piece ^ where_ref[2], :rows]))
    copies = start_copies(sources, sems.at[0])
    acc_ref[...] = jnp.zeros(acc_ref.shape, F32)

    def finish(at):
        xhat, rstd = norm_parts(hid_ref[at])
        grad = total_ref[at]
        acc_ref[1:2, :] += column_sum(grad * xhat)
        acc_ref[2:3, :] += column_sum(grad)
        value = grad_ref[at] + norm_back(grad, gain_ref[...], xhat, rstd)
        value_ref[at] = value
        embed = value.astype(BF)
        embed_ref[at] = embed
        acc_ref[0:1, :] += column_sum(embed.astype(F32))

    for side in range(2):
        for move in moves[3 * side : 3 * side + 3]:
            move.wait()
        over_rows((side + 1) * half, finish, side * half)
    acc_ref[3:5, :] = gup_ref[0:2, :]
    acc_ref[5:7, :] = gdown_ref[0:2, :]
    for slot in range(4):
        acc_ref[pl.ds(7 + (slot ^ where_ref[3]), 1), :] = gpre_ref[slot : slot + 1, :]
    small_ref[:channels] = nn(patch_ref[...].astype(BF), embed_ref[...]).astype(BF)
    small_ref[channels : 3 * channels] = gwout_ref[...].astype(BF)
    first = 3 * channels
    rows_here = tokens // length
    slots = length // quarter
    packed = [packed_flag(where_ref, seg_ref, row, length) for row in range(rows_here)]
    zero = jnp.zeros((quarter, width), F32)
    for slot in range(slots):
        value = zero
        for row in range(rows_here):
            at = row * length + slot * quarter
            here = value_ref[at : at + quarter]
            value = value + jnp.where(packed[row], 0.0, here)
            if slot == 0:
                every = here
                for later in range(1, slots):
                    every = every + value_ref[at + later * quarter : at + (later + 1) * quarter]
                value = value + jnp.where(packed[row], every, 0.0)
        small_ref[first + slot * quarter : first + (slot + 1) * quarter] = value.astype(BF)
    start = first + length
    small_ref[start : start + EXTRA] = acc_ref[...].astype(BF)
    start += EXTRA
    small_ref[start:] = jnp.zeros((small_ref.shape[0] - start, width), BF)
    moved = []
    for block in range(4):
        slot = block ^ where_ref[3]
        for piece in range(PIECES):
            at = (block * PIECES + piece) * GROUP
            moved.append((slot, piece ^ where_ref[2], small_ref.at[at : at + GROUP]))
    for index, (slot, piece, source) in enumerate(moved):

        @pl.when(slot % 2 == 0)
        def _():
            into = keep_ref.at[slot // 2, piece, rows:]
            pltpu.make_async_copy(source, into, sems.at[1, index]).start()

        @pl.when(slot % 2 == 1)
        def _():
            into = send_ref.at[slot // 2, piece, rows:]
            pltpu.make_async_copy(source, into, sems.at[1, index]).start()

    lane = lax.broadcasted_iota(jnp.int32, (1, slot_ref.shape[1] - width), 1)
    for row in range(rows_here):
        sums = []
        for slot in range(slots):
            at = row * length + slot * quarter
            sums.append(column_sum(value_ref[at : at + quarter]))
        every = sums[0]
        for slot in range(1, slots):
            every = every + sums[slot]
        for slot in range(slots):
            other = every if slot == 0 else jnp.zeros_like(every)
            index = row * slots + slot
            rows_ref[index : index + 1, :width] = jnp.where(packed[row], sums[slot], other)
            label = label_ref[row, slot]
            digits = jnp.where(lane == 0, label >> 5, jnp.where(lane == 1, label & 31, 0))
            rows_ref[index : index + 1, width:] = digits.astype(F32)
    slot_ref[...] = rows_ref[...].astype(BF)
    pgrad_ref[...] = direct_ref[...] + nt(win_ref[...], embed_ref[...])
    for copy in copies:
        copy.wait()
    for index in range(4 * PIECES):
        pltpu.make_async_copy(
            small_ref.at[:GROUP], keep_ref.at[0, 0, rows:], sems.at[1, index]
        ).wait()


def add_kernel(*refs, counts):
    sources, outs = refs[: sum(counts)], refs[sum(counts) :]
    for count, out_ref in zip(counts, outs):
        total = sources[0][...].astype(F32)
        for ref in sources[1:count]:
            total = total + ref[...].astype(F32)
        out_ref[...] = total.astype(BF)
        sources = sources[count:]


def piece_list(low, high):
    found = []
    for bit, ref in ((0, low), (1, high)):
        for i in range(ref.shape[0]):
            for j in range(ref.shape[1]):
                found.append((ref, i, j, i + (bit if low.shape[0] == 1 else 0), j + (bit if low.shape[1] == 1 else 0)))
    return [(ref, i, j, 2 * x + z) for ref, i, j, x, z in found]


def place_kernel(where_ref, low_in, high_in, out, low_ref, high_ref, stage_ref, in_sems, out_sems):
    rows = low_ref.shape[2]
    start_copies([(low_in, low_ref), (high_in, high_ref)], in_sems)
    pltpu.make_async_copy(low_in, low_ref, in_sems.at[0]).wait()
    pieces = piece_list(low_ref, high_ref)
    copies = []
    for index, (ref, i, j, piece) in enumerate(pieces):
        if index == 2:
            pltpu.make_async_copy(high_in, high_ref, in_sems.at[1]).wait()
        stage_ref[index] = ref[i, j].astype(F32)
        at = pl.ds(pl.multiple_of((piece ^ where_ref[2]) * rows, rows), rows)
        copies.append(pltpu.make_async_copy(stage_ref.at[index], out.at[at], out_sems.at[index]))
        copies[-1].start()
    for copy in copies:
        copy.wait()


def place_last_kernel(
    where_ref, mix_low, mix_high, low_ref, high_ref, all_ref, cross_ref,
    gk_ref, gv_ref, go_ref, gq_ref, gin_ref, gout_ref, gpos_ref, gbin_ref, *rest,
):
    *vectors, bup_ref, bout_ref, flat_ref = rest
    rows = gq_ref.shape[0] // PIECES
    for ref, i, j, piece in piece_list(mix_low, mix_high):
        at = pl.ds(pl.multiple_of((piece ^ where_ref[2]) * rows, rows), rows)
        gk_ref[at] = ref[i, j, :rows].astype(F32)
        gv_ref[at] = ref[i, j, rows : 2 * rows].astype(F32)
        go_ref[at] = ref[i, j, 2 * rows :].astype(F32)
    for ref, i, j, piece in piece_list(low_ref, high_ref):
        at = pl.ds(pl.multiple_of((piece ^ where_ref[2]) * rows, rows), rows)
        gq_ref[at] = ref[i, j, :rows].astype(F32)
    channels = gin_ref.shape[0]
    for core, ref in enumerate((all_ref, cross_ref)):
        for far in range(2):
            for piece in range(PIECES):
                head = (2 * far + core) ^ where_ref[3]
                group = head * PIECES + (piece ^ where_ref[2])
                flat_ref[pl.ds(pl.multiple_of(group * GROUP, GROUP), GROUP)] = ref[far, piece].astype(F32)
    start = 3 * channels
    gin_ref[...] = flat_ref[:channels]
    gout_ref[...] = flat_ref[channels:start]
    length = gpos_ref.shape[0]
    gpos_ref[...] = flat_ref[start : start + length]
    start += length
    for index in range(gbin_ref.shape[0]):
        gbin_ref[index : index + 1] = flat_ref[start : start + 1, index * 128 : (index + 1) * 128]
    for index, ref in enumerate(vectors):
        ref[...] = flat_ref[start + 1 + index : start + 2 + index]
    bout_ref[...] = flat_ref[start + 6 : start + 7, : bout_ref.shape[1]]
    bup_ref[...] = flat_ref[pl.ds(start + 7 + where_ref[3], 1)]


def make_program(rows_size, heads_size):
    levels = rows_size.bit_length() - 1

    def swap_heads(array, bit):
        return lax.ppermute(array, "heads", [(i, i ^ bit) for i in range(heads_size)])

    def swap_rows(array, bit):
        return lax.ppermute(array, "rows", [(i, i ^ bit) for i in range(rows_size)])

    def add_low(arrays):
        total = arrays[0].astype(F32)
        for other in arrays[1:]:
            total = total + other.astype(F32)
        return total.astype(BF)

    def tie(*values):
        return lax.optimization_barrier(values)

    def ordered(value, token):
        return tie(value, token)[0]

    class View:
        def __init__(self, array, start=(0, 0, 0), size=None):
            self.array, self.start = array, tuple(start)
            self.size = tuple(size or array.shape[:3])

        def narrow(self, axis, index):
            start, size = list(self.start), list(self.size)
            if size[axis] > 1:
                start[axis] += index
            size[axis] = 1
            return View(self.array, start, size)

        def value(self):
            stop = [a + b for a, b in zip(self.start, self.size)] + list(self.array.shape[3:])
            return lax.slice(self.array, self.start + (0, 0), stop)

    def add_views(views):
        return add_low([view.value() for view in views])

    class Chain:
        axes = {"y": 0, "x": 1, "z": 2}

        def __init__(self, order):
            self.order = order
            self.groups = []
            self.left = list(order) + ["w"] + [a for a in reversed(order) if a != "y"]

        def view(self, array):
            return View(array.reshape((-1, 2, 2) + array.shape[-2:]))

        def parts(self):
            kind = self.left[0]
            if kind == "y":
                return [[view.narrow(0, 1) for view in self.groups[-1]]]
            if "w" in self.left[1:]:
                axis = self.axes[kind]
                return [[view.narrow(axis, 1) for view in group] for group in self.groups]
            return [self.groups[0]]

        def prepare(self):
            if "w" in self.left:
                return [add_views(part) for part in self.parts()]
            return [self.total]

        def launch(self, sends):
            self.sends = sends
            kind = self.left[0]
            if kind == "y":
                self.got = [swap_heads(send, 2) for send in sends]
            else:
                self.got = [swap_rows(send, 1 << "xzw".index(kind)) for send in sends]

        def deliver(self, got):
            kind = self.left.pop(0)
            if kind == "w":
                self.total = add_low([self.sends[0], got[0]])
                for level in range(3, levels):
                    self.total = add_low([self.total, swap_rows(self.total, 1 << level)])
            elif "w" in self.left:
                axis = self.axes[kind]
                if kind == "y":
                    self.groups = self.groups[:1]
                self.groups = [
                    [view.narrow(axis, 0) for view in group] + [View(more)]
                    for group, more in zip(self.groups, got)
                ]
            elif self.left:
                self.total = jnp.concatenate([self.sends[0], got[0]], self.axes[kind])
            else:
                self.low, self.high = self.sends[0][0], got[0][0]

    def program(
        patches, segments, labels, w_in, b_in, pos_table, cls_table, ln1_gain, ln1_bias,
        w_query, w_key, w_value, w_attn_out, ln2_gain, ln2_bias, w_up, b_up, w_down, b_down,
        w_out, b_out, latent_grad, logdet_grad,
    ):
        tokens, channels = patches.shape
        length, width = pos_table.shape
        slot_count = labels.shape[1]
        quarter = length // slot_count
        classes = cls_table.shape[0]
        part = w_query.shape[2]
        row_count = tokens // length
        head_index = lax.axis_index("heads")
        row_index = lax.axis_index("rows")
        row_bit = row_index & 1
        mask = ((row_index & 1) << 1) | ((row_index >> 1) & 1)
        where = jnp.stack([head_index * tokens, row_bit, mask, head_index]).astype(jnp.int32)
        rows = width // PIECES
        unit = part // PIECES
        heads = width // HEAD_DIM
        square = 2 * tokens * width * width

        def shape(*dims, dtype=F32):
            return jax.ShapeDtypeStruct(dims, dtype)

        def call(kernel, operands, specs, outs, out_specs, scratch=(), room=60, **options):
            return pl.pallas_call(
                functools.partial(kernel, **options) if options else kernel,
                in_specs=specs,
                out_specs=out_specs,
                out_shape=outs,
                scratch_shapes=list(scratch),
                compiler_params=pltpu.CompilerParams(vmem_limit_bytes=room << 20),
                cost_estimate=pl.CostEstimate(
                    flops=1, transcendentals=0, bytes_accessed=1
                ),
            )(*operands)

        dma = pltpu.SemaphoreType.DMA
        low = shape(tokens, width, dtype=BF)
        full = shape(tokens, width)
        half_low = shape(tokens, width // 2, dtype=BF)

        bias_rows = jnp.pad(b_up, ((0, EXTRA - 1), (0, 0)))
        pack_t = jnp.stack(
            [
                jnp.concatenate([w_query[0].T, w_key[0].T, bias_rows], 0),
                jnp.concatenate([w_value[0].T, w_attn_out[0], bias_rows], 0),
            ]
        )
        own_u, own_d = w_up[0], w_down[0]
        half_rows = width // 2
        half_t = jnp.concatenate(
            [
                jnp.where(row_bit == 0, w_query[0].T, w_value[0].T),
                jnp.where(row_bit == 0, w_key[0].T, w_attn_out[0]),
                bias_rows,
            ],
            0,
        )
        far_t = swap_heads(half_t, 2)
        near_t = swap_heads(ordered(pack_t, half_t), 1)
        half_u = lax.dynamic_slice_in_dim(own_u, row_bit * half_rows, half_rows, 0)
        half_u, half_t = tie(half_u, half_t)
        far_u = swap_heads(half_u, 2)
        half_d = lax.dynamic_slice_in_dim(own_d, row_bit * half_rows, half_rows, 0)
        half_d, half_u = tie(half_d, half_u)
        far_d = swap_heads(half_d, 2)
        cls_rows = cls_table[labels.reshape(-1)].astype(F32)
        patches_t = patches.T
        hidden0, normed1 = call(
            embed_kernel,
            (
                where, segments, ordered(patches_t, half_d), w_in, b_in[None], pos_table, cls_rows,
                ln1_gain, ln1_bias,
            ),
            [SMEM, SMEM] + [VMEM] * 7,
            (full, low),
            (VMEM, VMEM),
        )
        normed1, far_t = tie(normed1, far_t)
        far_other_t = swap_rows(far_t, 1)
        cross_t = swap_heads(far_t, 1)
        near_u = swap_heads(ordered(own_u, far_t), 1)
        near_d = swap_heads(ordered(own_d, far_t), 1)

        def attend(hidden, normed, parts):
            return call(
                attend_kernel,
                (where, segments, hidden, normed) + parts,
                [SMEM, SMEM, HBM, VMEM] + [HBM] * len(parts),
                (
                    half_low, half_low, half_low,
                    shape(row_count * heads // 2, length, length, dtype=BF), half_low, full,
                ),
                (HBM,) * 5 + (VMEM,),
                [
                    pltpu.VMEM((4, width // 2, width), BF),
                    pltpu.VMEM((row_count, 2, length, length), F32),
                    pltpu.VMEM((tokens, width), F32),
                ]
                + [pltpu.VMEM((tokens, width // 2), BF)] * 3
                + [
                    pltpu.VMEM((row_count * heads // 2, length, length), BF),
                    pltpu.VMEM((tokens, width // 2), BF),
                    dma((8,)),
                    dma((5,)),
                    dma((row_count * heads // 4,)),
                ],
                length=length,
                quarter=quarter,
                count=len(parts),
            )

        parts_near = (pack_t, near_t)
        *saved_near, mixed = attend(hidden0, normed1, parts_near)
        mixed, far_other_t, far_u = tie(mixed, far_other_t, far_u)
        cross_other_t = swap_heads(far_other_t, 1)
        far_other_u = swap_rows(far_u, 1)
        cross_u = swap_heads(far_u, 1)
        parts_far = (far_t, far_other_t, cross_t, cross_other_t)
        *saved_far, hidden1 = attend(mixed, normed1, parts_far)
        hidden1, far_other_u, far_d = tie(hidden1, far_other_u, far_d)
        cross_other_u = swap_heads(far_other_u, 1)
        far_other_d = swap_rows(far_d, 1)
        cross_d = swap_heads(far_d, 1)
        parts_u = (own_u, near_u, far_u, far_other_u, cross_u, cross_other_u)
        four = shape(heads_size, tokens, width, dtype=BF)
        normed2, activated, slope = call(
            up_kernel,
            (where, hidden1, ln2_gain, ln2_bias)
            + parts_u
            + (pack_t, near_t, far_t, cross_t),
            [SMEM] + [VMEM] * 3 + [HBM] * 10,
            (low, four, four),
            (VMEM, HBM, HBM),
            [
                pltpu.VMEM((heads_size, width, width), BF),
                pltpu.VMEM((heads_size, EXTRA, width), BF),
                pltpu.VMEM((heads_size, tokens, width), BF),
                pltpu.VMEM((heads_size, tokens, width), BF),
                dma((4,)),
                dma((4,)),
                dma((2, 4)),
            ],
        )
        normed2, far_other_d = tie(normed2, far_other_d)
        cross_other_d = swap_heads(far_other_d, 1)
        parts_d = (own_d, near_d, far_d, far_other_d, cross_d, cross_other_d)
        pieces = shape(2, PIECES, rows, width, dtype=BF)
        one = shape(PIECES, rows, width, dtype=BF)
        stage = pltpu.VMEM((2, width, width), BF)
        out_sems = dma((2, PIECES))
        latents, logdet, means, tops, direct, grad_hidden2, grad_w_out, gdown, keep_d, *sends_d = call(
            down_kernel,
            (
                where, segments, hidden1, activated, b_down, w_out.T, b_out[:, None], patches_t, latent_grad.T,
                logdet_grad[None],
            )
            + parts_d,
            [SMEM, SMEM, HBM, HBM] + [VMEM] * 6 + [HBM] * 6,
            (
                shape(channels, tokens), shape(1, tokens), shape(1, row_count), shape(1, row_count),
                shape(channels, tokens),
                full, shape(2 * channels, width), shape(8, width), pieces, one, one,
            ),
            (VMEM,) * 8 + (HBM,) * 3,
            [
                pltpu.VMEM((heads_size, width, width), BF),
                pltpu.VMEM((heads_size, tokens, width), BF),
                pltpu.VMEM((tokens, width), F32),
                pltpu.VMEM((tokens, width), BF),
                stage,
                pltpu.VMEM((tokens, width), F32),
                dma((4,)),
                dma((4,)),
                out_sems,
                dma(()),
            ],
            length=length,
            quarter=quarter,
        )
        chains = [Chain(order) for order in CHAIN_ORDERS]
        down, up, mix, last = chains

        def add_groups(*groups):
            def spec(view, start):
                size = view.size
                block = (view.array.shape[3] // 2, view.array.shape[4])

                def at(i):
                    return tuple(a // b for a, b in zip(start, size)) + (i, 0)

                return pl.BlockSpec(size + block, at)

            views = [view for group in groups for view in group]
            return pl.pallas_call(
                functools.partial(add_kernel, counts=tuple(len(group) for group in groups)),
                grid=(2,),
                in_specs=[spec(view, view.start) for view in views],
                out_specs=[spec(group[0], (0, 0, 0)) for group in groups],
                out_shape=[shape(*group[0].size, *group[0].array.shape[3:], dtype=BF) for group in groups],
                compiler_params=pltpu.CompilerParams(vmem_limit_bytes=60 << 20),
                cost_estimate=pl.CostEstimate(flops=1, transcendentals=0, bytes_accessed=1),
            )(*(view.array for view in views))

        def halves(chain, keep, gots):
            keep = chain.view(keep)
            return [[keep.narrow(0, index), chain.view(got)] for index, got in enumerate(gots)]

        grad_hidden2, *sends_d = tie(grad_hidden2, *sends_d)
        got_d = [swap_heads(send, 1) for send in sends_d]
        pre_grads, gpre = call(
            grad_pre_kernel,
            (where, grad_hidden2, slope) + parts_d,
            [SMEM, VMEM, HBM] + [HBM] * 6,
            (four, shape(8, width)),
            (HBM, VMEM),
            [
                pltpu.VMEM((heads_size, width, width), BF),
                pltpu.VMEM((heads_size, tokens, width), BF),
                pltpu.VMEM((tokens, width), BF),
                pltpu.VMEM((heads_size, tokens, width), BF),
                dma((4,)),
                dma((4,)),
                dma((4,)),
            ],
        )
        pre_grads, *got_d = tie(pre_grads, *got_d)
        down.groups = halves(down, keep_d, got_d)
        pre_grads, *sends = tie(pre_grads, *add_groups(*down.parts()))
        down.launch(sends)
        grad_hidden1, grad_mix, gup, keep_u, *sends_u = call(
            up_back_kernel,
            (where, grad_hidden2, pre_grads, normed2, hidden1, ln2_gain) + parts_u,
            [SMEM, HBM, HBM, VMEM, HBM, VMEM] + [HBM] * 6,
            (full, low, shape(8, width), pieces, one, one),
            (VMEM, VMEM, VMEM, HBM, HBM, HBM),
            [
                pltpu.VMEM((heads_size, width, width), BF),
                pltpu.VMEM((heads_size, tokens, width), BF),
                pltpu.VMEM((tokens, width), F32),
                stage,
                pltpu.VMEM((tokens, width), F32),
                pltpu.VMEM((tokens, width), F32),
                dma((4,)),
                dma((4,)),
                out_sems,
                dma((2,)),
            ],
        )
        grad_mix, *sends_u = tie(grad_mix, *sends_u)
        got_u = [swap_heads(send, 1) for send in sends_u]

        def attend_back(saved, parts, before):
            chained = () if before is None else (before,)
            mixed_pieces = shape(PIECES, 3 * unit, width, dtype=BF)
            return call(
                attend_back_kernel,
                (where, grad_mix) + tuple(saved) + (normed1,) + chained + parts,
                [SMEM] + [HBM] * (7 + len(chained) + len(parts)),
                (full, shape(width // 2, width, dtype=BF), mixed_pieces, mixed_pieces),
                (VMEM, VMEM, HBM, HBM),
                [pltpu.VMEM((4, width // 2, width), BF)]
                + [pltpu.VMEM((tokens, width // 2), BF)] * 4
                + [pltpu.VMEM((3, width // 2, width), BF), dma((8,)), dma((3, 2 * PIECES))]
                + [pltpu.VMEM((tokens, width), BF)]
                + [pltpu.VMEM((tokens, width // 2), BF)] * 3
                + [
                    pltpu.VMEM((row_count * heads // 2, length, length), BF),
                    pltpu.VMEM((tokens, width // 2), BF),
                    pltpu.VMEM((tokens, width), BF),
                    pltpu.VMEM((tokens, width), F32),
                    dma((8,)),
                ],
                length=length,
                quarter=quarter,
                count=len(parts),
                chained=before is not None,
            )

        total_far, gq_far, keep_far, send_far = attend_back(saved_far, parts_far, None)
        total_far, send_far, *got_d = tie(total_far, send_far, *down.got)
        total_far, *got_u = tie(total_far, *got_u)
        got_far = swap_heads(send_far, 1)
        down.deliver(got_d)
        up.groups = halves(up, keep_u, got_u)
        total_far, *sends = tie(total_far, *add_groups(*down.parts(), *up.parts()))
        down.launch(sends[:1])
        up.launch(sends[1:])
        total_near, gq_near, keep_near, send_near = attend_back(saved_near, parts_near, total_far)
        total_near, send_near, got_far, *got_d = tie(total_near, send_near, got_far, *down.got)
        got_near = swap_heads(send_near, 1)
        mix.groups = [[], [mix.view(keep_far), mix.view(got_far)]]
        down.deliver(got_d)
        grad_hidden1, *sends = tie(grad_hidden1, *add_groups(*down.parts(), *mix.parts()))
        down.launch(sends[:1])
        mix.launch(sends[1:])
        groups = 4 * PIECES
        last_pieces = shape(2, PIECES, unit + GROUP, width, dtype=BF)
        patches_grad, slot_rows, keep_q, send_q = call(
            embed_back_kernel,
            (
                where, segments, labels, grad_hidden1, total_near, hidden0, ln1_gain, patches_t,
                direct, w_in, grad_w_out, gdown, gup, gpre, gq_near, gq_far,
            ),
            [SMEM] * 3 + [HBM] * 3 + [VMEM] * 10,
            (shape(channels, tokens), shape(row_count * slot_count, width + 128, dtype=BF), last_pieces, last_pieces),
            (VMEM, VMEM, HBM, HBM),
            [
                pltpu.VMEM((tokens, width), F32),
                pltpu.VMEM((tokens, width), BF),
                pltpu.VMEM((EXTRA, width), F32),
                pltpu.VMEM((groups * GROUP, width), BF),
                pltpu.VMEM((row_count * slot_count, width + 128), F32),
                pltpu.VMEM((tokens, width), F32),
                pltpu.VMEM((tokens, width), F32),
                pltpu.VMEM((tokens, width), F32),
                dma((2, groups)),
                dma((6,)),
            ],
            length=length,
            quarter=quarter,
        )
        patches_grad, *got_u = tie(patches_grad, *up.got)
        patches_grad, *got_d = tie(patches_grad, *down.got)
        patches_grad, send_q = tie(patches_grad, send_q)
        last.groups = [[last.view(keep_q), last.view(swap_heads(send_q, 1))]]
        mix.groups[0] = [mix.view(keep_near), mix.view(got_near)]
        down.got, up.got = got_d, got_u
        gathered = slot_rows
        gathers = [("rows", 1 << level) for level in reversed(range(levels))]
        gathers += [("heads", 2), ("heads", 1)]
        share = (len(gathers) - 1) // 4
        token = got_d[0]
        pending = {0, 1, 2}
        heads_left = [2, 1]
        got = None
        small = None
        for index in TAIL:
            if index == 4:
                more = gathers[:share] if len(gathers) > 2 + share else gathers[:1]
                for axis, bit in more:
                    gathers.pop(0)
                    if got is not None:
                        gathered = jnp.concatenate([gathered, ordered(got, token)], 0)
                    token = gathered = ordered(gathered, token)
                    got = (swap_rows if axis == "rows" else swap_heads)(gathered, bit)
                continue
            if index == 5:
                if small is None:
                    last.deliver([ordered(more, token) for more in last.got])
                    axis = Chain.axes[[a for a in last.order if a != "y"][0]] - 1
                    small = jnp.concatenate([last.low[:, :, unit:], last.high[:, :, unit:]], axis)
                    small = small.reshape(1, PIECES, GROUP, width)
                token = small = ordered(small, token)
                small_got = swap_heads(small, heads_left.pop(0))
                if heads_left:
                    small = jnp.concatenate([small, small_got], 0)
                continue
            chain = chains[index]
            if index in pending:
                chain.deliver([ordered(one, token) for one in chain.got])
            pending.add(index)
            sends = []
            for send in chain.prepare():
                token = ordered(send, token)
                sends.append(token)
            chain.launch(sends)
        gathered = jnp.concatenate([gathered, got], 0)
        for axis, bit in gathers:
            swap = swap_rows if axis == "rows" else swap_heads
            gathered = jnp.concatenate([gathered, swap(gathered, bit)], 0)
        for chain in chains[:3]:
            chain.deliver(chain.got)
        gathered = gathered.reshape(-1, width + 128)
        digits = gathered[:, width : width + 2].astype(jnp.int32)
        slot_label = digits[:, 0] * 32 + digits[:, 1]
        label_onehot = (
            lax.broadcasted_iota(jnp.int32, (classes, 1), 0) == slot_label[None, :]
        ).astype(BF)
        sum_cls = nn(label_onehot, gathered[:, :width])

        def place(chain):
            return call(
                place_kernel,
                (where, chain.low, chain.high),
                [SMEM, HBM, HBM],
                shape(width, width),
                HBM,
                [
                    pltpu.VMEM(chain.low.shape, BF),
                    pltpu.VMEM(chain.high.shape, BF),
                    pltpu.VMEM((PIECES, rows, width), F32),
                    dma((2,)),
                    dma((PIECES,)),
                ],
            )

        sum_down, sum_up = place(down), place(up)
        units = shape(part, width)
        line = shape(1, width)
        sum_k, sum_v, sum_o, sum_q, sum_w_in, sum_w_out, sum_pos, *lines = call(
            place_last_kernel,
            (where, mix.low, mix.high, last.low, last.high, small, small_got),
            [SMEM] + [VMEM] * 6,
            (units,) * 4
            + (shape(channels, width), shape(2 * channels, width), shape(length, width))
            + (shape(width // 128, 128),)
            + (line,) * 6
            + (shape(1, 2 * channels),),
            (VMEM,) * 15,
            [pltpu.VMEM((groups * GROUP, width), F32)],
        )
        sum_b_in, sum_gain1, sum_bias1, sum_gain2, sum_bias2, sum_b_down, sum_b_up, sum_b_out = lines
        return (
            latents.T,
            logdet.reshape(tokens),
            patches_grad.T,
            means.reshape(row_count),
            tops.reshape(row_count),
            sum_w_in,
            sum_b_in.reshape(width),
            sum_pos,
            sum_cls,
            sum_gain1,
            sum_bias1,
            sum_q.T[None],
            sum_k.T[None],
            sum_v.T[None],
            sum_o[None],
            sum_gain2,
            sum_bias2,
            sum_up[None],
            sum_b_up,
            sum_down[None],
            sum_b_down,
            sum_w_out.T,
            sum_b_out.reshape(2 * channels),
        )

    return program


def solution(mesh):
    tokens = P(("rows", "heads"))
    tokens2 = P(("rows", "heads"), None)
    last = P(None, None, "heads")
    middle = P(None, "heads", None)
    in_specs = (
        (tokens2, P("rows"), tokens2)
        + (P(),) * 6
        + (last, last, last, middle)
        + (P(), P(), last, P(None, "heads"), middle, P(), P(), P())
        + (tokens2, tokens)
    )
    out_specs = (
        (tokens2, tokens, tokens2, tokens, tokens)
        + (P(),) * 6
        + (last, last, last, middle)
        + (P(), P(), last, P(None, "heads"), middle, P(), P(), P())
    )
    program = make_program(mesh.shape["rows"], mesh.shape["heads"])
    return jax.shard_map(
        program, mesh=mesh, in_specs=in_specs, out_specs=out_specs, check_vma=False
    )
```
